32 devices in a mesh: grp: 2 (over x), seq: 16 (over z, y, core).
Axes of the slice: x: 2, y: 2, z: 4, core: 2. Of those that a mesh axis runs over, the one named last changes fastest.
Arguments:
- activations: bfloat16 [16384, 1536], P(('grp', 'seq')), parts along dimension 0, may hold values from -60 to 60, as said below
- dilated_tap_weight: bfloat16 [3, 1536, 768], replicated, may hold values from -0.09375 to 0.09375
- conv_mix: bfloat16 [768, 1536], replicated, may hold values from -0.21875 to 0.21875
- w_query: bfloat16 [1536, 128], replicated, may hold values from -0.15625 to 0.15625
- w_keyval: bfloat16 [1536, 256], replicated, may hold values from -0.15625 to 0.15625
- contact_tiles: bfloat16 [16, 128, 128], replicated, may hold values from -8 to 250, as said below
- tile_codes: int32 [128, 65], P(('grp', 'seq')), parts along dimension 0, may hold values from 0 to 15
- bin_valid: int32 [16384], P('grp'), parts along dimension 0, may hold values 0 or 1
Outputs:
- attended: bfloat16 [16384, 128], P(('grp', 'seq')), parts along dimension 0
The draws below stay inside these ranges and needn't reach their ends.
There are 2 independent parts, one for each index of `grp`. The reference program is written for one: setup_inputs(seed, part) draws one part's arguments, and reference() takes and returns one part's arrays. A program takes and returns all parts, laid end to end along the dimension named above; an argument that names none is the same for every part. Nothing has to cross between parts.
Inputs may be any that keep to these rules, and one draw needn't show every extreme that they name: `activations`: finite values. `contact_tiles`: finite values.
All inputs are finite; a program needn't handle non-finite values.
Results may differ from the reference program's by a relative error of at most 0.005.
Values may be sent and summed in bfloat16 or wider, within the bound.
No kernel may reach another device: no remote copies, remote signals or barrier semaphores. Data moves between devices by JAX's collectives and lax.ppermute only.
A program may use at most 64 MiB of HBM per device.

```python
import math
import jax
import jax.numpy as jnp
from jax import lax

C = 1536
HID = 768
HEADS = 1
HDIM = 128
CONV_DILATION = 8
HALF = 4096
TILE = 128
NCODE = 16
WINDOW_BINS = 8192
NOFF = 65
QTILES = 64


def draw_activations(key, part):
    key_rows = jax.random.fold_in(key, 11)
    key_cols = jax.random.fold_in(key, 12)
    key_base = jax.random.fold_in(key, 13)
    row_scale = jnp.exp(jax.random.uniform(key_rows, (WINDOW_BINS, 1), jnp.float32, math.log(0.3), math.log(3.0)))
    col_scale = jnp.exp(jax.random.uniform(key_cols, (1, C), jnp.float32, math.log(0.3), math.log(3.0)))
    base_draw = jnp.clip(jax.random.normal(key_base, (WINDOW_BINS, C), jnp.float32), -5.0, 5.0)
    return (row_scale * col_scale * base_draw).astype(jnp.bfloat16)


def draw_contact_tiles(key, part):
    key_base = jax.random.fold_in(key, 21)
    result = 2.0 * jnp.clip(jax.random.normal(key_base, (NCODE, TILE, TILE), jnp.float32), -4.0, 4.0)
    return result.astype(jnp.bfloat16)


def touch_ends(entries, rng, low, high):
    place = [jax.random.randint(jax.random.fold_in(rng, axis), (), 0, length) for axis, length in enumerate(entries.shape)]
    longest = entries.shape.index(max(entries.shape))
    neighbour = place[:longest] + [(place[longest] + 1) % entries.shape[longest]] + place[longest + 1:]
    return entries.at[tuple(place)].set(low).at[tuple(neighbour)].set(high)


def normal_values(stream_key, shape, spread, reach, kind=jnp.bfloat16):
    return jnp.clip(spread * jax.random.normal(stream_key, shape, jnp.float32), -reach, reach).astype(kind)


def setup_inputs(seed: int = 0, part: int = 0) -> dict:
    arg_keys = jax.random.split(jax.random.key(seed), 9)
    part_keys = jax.random.split(jax.random.fold_in(arg_keys[8], part), 9)
    activations = draw_activations(jax.random.fold_in(jax.random.fold_in(arg_keys[8], part), 71), part)
    dilated_tap_weight = normal_values(arg_keys[1], (3, C, HID), (3 * C) ** -0.5, 0.09375)
    conv_mix = normal_values(arg_keys[2], (HID, C), HID ** -0.5, 0.21875)
    w_query = normal_values(arg_keys[3], (C, HEADS * HDIM), C ** -0.5, 0.15625)
    w_keyval = normal_values(arg_keys[4], (C, 2 * HEADS * HDIM), C ** -0.5, 0.15625)
    contact_tiles = draw_contact_tiles(jax.random.fold_in(arg_keys[8], 71), part)
    tile_codes = touch_ends(jax.random.randint(part_keys[6], (QTILES, NOFF), 0, NCODE), jax.random.fold_in(part_keys[6], 1), 0, NCODE - 1).astype(jnp.int32)
    bin_valid = touch_ends((jax.random.randint(part_keys[7], (WINDOW_BINS,), 0, 8) < 7).astype(jnp.int32), jax.random.fold_in(part_keys[7], 1), 0, 1)
    return dict(activations=activations, dilated_tap_weight=dilated_tap_weight, conv_mix=conv_mix, w_query=w_query, w_keyval=w_keyval, contact_tiles=contact_tiles, tile_codes=tile_codes, bin_valid=bin_valid)


masked_score = -1e+30
norm_eps = 1e-06

def reference(activations, dilated_tap_weight, conv_mix, w_query, w_keyval, contact_tiles, tile_codes, bin_valid):
    raised_features = jax.nn.gelu(activations.astype(jnp.float32), approximate=False).astype(jnp.bfloat16)
    border_padded = jnp.pad(raised_features, ((CONV_DILATION, CONV_DILATION), (0, 0)))
    conv_sum = jnp.zeros((WINDOW_BINS, HID), jnp.float32)
    for tap_position in range(3):
        offset_features = border_padded[tap_position * CONV_DILATION:tap_position * CONV_DILATION + WINDOW_BINS]
        conv_sum = conv_sum + jnp.dot(offset_features, dilated_tap_weight[tap_position], preferred_element_type=jnp.float32)
    squeezed = jax.nn.gelu(conv_sum, approximate=False).astype(jnp.bfloat16)
    mixed_rows = activations.astype(jnp.float32) + jnp.dot(squeezed, conv_mix, preferred_element_type=jnp.float32)
    normed = (mixed_rows * lax.rsqrt(lax.optimization_barrier(jnp.mean(mixed_rows * mixed_rows, axis=-1, keepdims=True)) + norm_eps)).astype(jnp.bfloat16)
    queries = lax.optimization_barrier(jnp.dot(normed, w_query, preferred_element_type=jnp.float32).astype(jnp.bfloat16))
    keyval = lax.optimization_barrier(jnp.dot(normed, w_keyval, preferred_element_type=jnp.float32).astype(jnp.bfloat16))
    width_heads = HEADS * HDIM
    block_rows = math.gcd(WINDOW_BINS, 512)
    window = block_rows + 2 * HALF
    kv_padded = jnp.pad(keyval, ((HALF, HALF), (0, 0)))
    valid_padded = jnp.pad(bin_valid, (HALF, HALF))
    scale = 1.0 / math.sqrt(HDIM)

    def one_block(block_start):
        query_heads = lax.dynamic_slice(queries, (block_start, jnp.int32(0)), (block_rows, width_heads)).reshape(block_rows, HEADS, HDIM).astype(jnp.float32)
        kv_block = lax.dynamic_slice(kv_padded, (block_start, jnp.int32(0)), (window, 2 * width_heads))
        valid_keys = lax.dynamic_slice_in_dim(valid_padded, block_start, window)
        query_pos = block_start + jnp.arange(block_rows, dtype=jnp.int32)
        key_pos = block_start - HALF + jnp.arange(window, dtype=jnp.int32)
        key_heads = kv_block[:, :width_heads].reshape(window, HEADS, HDIM).astype(jnp.float32)
        value_heads = kv_block[:, width_heads:].reshape(window, HEADS, HDIM).astype(jnp.float32)
        raw_scores = jnp.einsum('qhd,khd->qhk', query_heads, key_heads) * scale
        query_tiles = query_pos // TILE
        key_tiles = jnp.floor_divide(key_pos, TILE)
        offset = jnp.clip(key_tiles[None, :] - query_tiles[:, None] + HALF // TILE, 0, NOFF - 1).astype(jnp.int32)
        picked = tile_codes[query_tiles[:, None], offset]
        bias_block = contact_tiles[picked, (query_pos % TILE)[:, None], jnp.remainder(key_pos, TILE)[None, :]].astype(jnp.float32)
        inside = (key_pos >= 0) & (key_pos < WINDOW_BINS)
        in_band = jnp.abs(key_pos[None, :] - query_pos[:, None]) <= HALF
        kept_pairs = inside[None, :] & in_band & ((valid_keys[None, :] == 1) | (key_pos[None, :] == query_pos[:, None]))
        scores = jnp.where(kept_pairs[:, None, :], raw_scores + bias_block[:, None, :], masked_score)
        row_peak = lax.optimization_barrier(jnp.max(scores, axis=-1, keepdims=True))
        probs = jnp.exp(scores - row_peak)
        row_total = lax.optimization_barrier(jnp.sum(probs, axis=-1))
        rounded = lax.optimization_barrier(probs.astype(jnp.bfloat16)).astype(jnp.float32)
        weighted = jnp.einsum('qhk,khd->qhd', rounded, value_heads)
        return (weighted / row_total[..., None]).reshape(block_rows, width_heads).astype(jnp.bfloat16)
    starts = (jnp.arange(WINDOW_BINS // block_rows, dtype=jnp.int32) * block_rows).astype(jnp.int32)
    blocks = lax.map(one_block, starts)
    return blocks.reshape(WINDOW_BINS, width_heads)
```

```python
import functools
import math

import jax
import jax.numpy as jnp
from jax import lax
from jax.experimental import pallas as pl
from jax.experimental.pallas import tpu as pltpu
from jax.sharding import PartitionSpec as P

HDIM = 128
CONV_DILATION = 8
HALF = 4096


masked_score = -1e30
norm_eps = 1e-06


def padded(x, sides, width):
    for axis, dim in sides:
        size, length = (lax.axis_size(axis), x.shape[dim])
        up = [(i, (i + 1) % size) for i in range(size - 1)]
        down = [(j, i) for i, j in up]
        last = lax.slice_in_dim(x, length - width, length, axis=dim)
        initial = lax.slice_in_dim(x, 0, width, axis=dim)
        before = lax.ppermute(last, axis, up)
        after = lax.ppermute(initial, axis, down)
        x = jnp.concatenate([before, x, after], axis=dim)
    return x


LOG2E = 1.4426950408889634


def attend_kernel(
    reach,
    codes_ref,
    place_ref,
    q_ref,
    kv_ref,
    tiles_ref,
    valid_ref,
    out_ref,
    kv_buf,
    bias_buf,
    scores,
    peak,
    total,
    acc,
    sems,
):
    rows, head_dim = q_ref.shape
    code_count, tile, _ = tiles_ref.shape
    tiles_per_block = rows // tile
    position = place_ref[0]
    first = place_ref[1]
    count = place_ref[2]
    factor = LOG2E / math.sqrt(head_dim)

    def fetch(i):
        return pltpu.make_async_copy(
            kv_ref.at[pl.ds((first + i) * rows, rows), :], kv_buf.at[i], sems.at[i]
        )

    @pl.loop(0, count)
    def _(i):
        fetch(i).start()

    bias_buf[...] = tiles_ref[...].astype(jnp.float32) * LOG2E
    peak[...] = jnp.full_like(peak, masked_score)

    @pl.loop(0, count)
    def _(i):
        fetch(i).wait()
        block = first + i
        keys = kv_buf[i, :, :head_dim]
        raw = lax.dot_general(
            q_ref[...], keys, (((1,), (1,)), ((), ())), preferred_element_type=jnp.float32
        )
        invalid = jnp.where(valid_ref[block] == 1, 0.0, masked_score)
        shift = block - position

        def tile_scores(qt, kt):
            offset = jnp.clip(shift * tiles_per_block + kt - qt + HALF // tile, 0, 2 * (HALF // tile))
            part = raw[qt * tile : (qt + 1) * tile, kt * tile : (kt + 1) * tile]
            return part * factor + bias_buf[codes_ref[qt, offset]]

        def keep(qt, columns):
            peak_now = peak[qt * tile : (qt + 1) * tile, :]
            for kt, column in enumerate(columns):
                scores[i, qt * tile : (qt + 1) * tile, kt * tile : (kt + 1) * tile] = column
                peak_now = jnp.maximum(peak_now, column)
            peak[qt * tile : (qt + 1) * tile, :] = peak_now

        plain = (shift != 0) & (jnp.abs(shift) < reach)

        @pl.when(plain)
        def _():
            for qt in range(tiles_per_block):
                keep(
                    qt,
                    [
                        tile_scores(qt, kt) + invalid[:, kt * tile : (kt + 1) * tile]
                        for kt in range(tiles_per_block)
                    ],
                )

        @pl.when(jnp.logical_not(plain))
        def _():
            lag = lax.broadcasted_iota(jnp.int32, (tile, tile), 1) - lax.broadcasted_iota(
                jnp.int32, (tile, tile), 0
            )
            for qt in range(tiles_per_block):
                columns = []
                for kt in range(tiles_per_block):
                    apart = lag + (shift * rows + (kt - qt) * tile)
                    dropped = jnp.where(
                        apart == 0, 0.0, invalid[:, kt * tile : (kt + 1) * tile]
                    )
                    dropped = jnp.where(jnp.abs(apart) <= HALF, dropped, masked_score)
                    columns.append(tile_scores(qt, kt) + dropped)
                keep(qt, columns)

    peak[...] = jnp.broadcast_to(jnp.max(peak[...], axis=1, keepdims=True), peak.shape)
    total[...] = jnp.zeros_like(total)
    acc[...] = jnp.zeros_like(acc)

    @pl.loop(0, count)
    def _(i):
        parts = []
        sums = total[...]
        for kt in range(tiles_per_block):
            probs = jnp.exp2(scores[i, :, kt * tile : (kt + 1) * tile] - peak[...])
            sums = sums + probs
            parts.append(probs.astype(jnp.bfloat16))
        total[...] = sums
        acc[...] += jnp.dot(
            jnp.concatenate(parts, axis=1),
            kv_buf[i, :, head_dim:],
            preferred_element_type=jnp.float32,
        )

    out_ref[...] = (acc[...] / jnp.sum(total[...], axis=1, keepdims=True)).astype(out_ref.dtype)


def attend(queries, everything, contact_tiles, tile_codes, bin_valid, position, seq_size):
    rows, head_dim = queries.shape
    reach = HALF // rows
    tile = contact_tiles.shape[1]
    slots = min(seq_size, 2 * reach + 1)
    first = jnp.maximum(position - reach, 0)
    last = jnp.minimum(position + reach, seq_size - 1)
    place = jnp.stack([position, first, last - first + 1]).astype(jnp.int32)
    valid_rows = bin_valid.reshape(seq_size, 1, rows)
    vmem = pl.BlockSpec(memory_space=pltpu.VMEM)
    smem = pl.BlockSpec(memory_space=pltpu.SMEM)
    return pl.pallas_call(
        functools.partial(attend_kernel, reach),
        out_shape=jax.ShapeDtypeStruct((rows, head_dim), jnp.bfloat16),
        in_specs=[smem, smem, vmem, pl.BlockSpec(memory_space=pl.ANY), vmem, vmem],
        out_specs=vmem,
        scratch_shapes=[
            pltpu.VMEM((slots, rows, 2 * head_dim), jnp.bfloat16),
            pltpu.VMEM(contact_tiles.shape, jnp.float32),
            pltpu.VMEM((slots, rows, rows), jnp.float32),
            pltpu.VMEM((rows, tile), jnp.float32),
            pltpu.VMEM((rows, tile), jnp.float32),
            pltpu.VMEM((rows, head_dim), jnp.float32),
            pltpu.SemaphoreType.DMA((slots,)),
        ],
        compiler_params=pltpu.CompilerParams(vmem_limit_bytes=60 << 20),
        name="attend",
    )(tile_codes, place, queries, everything, contact_tiles, valid_rows)


def per_device(
    activations,
    dilated_tap_weight,
    conv_mix,
    w_query,
    w_keyval,
    contact_tiles,
    tile_codes,
    bin_valid,
):
    genomic_bin_rows = activations.shape[0]
    seq_size = lax.axis_size("seq")
    position = lax.axis_index("seq")
    border_padded = padded(activations, (("seq", 0),), CONV_DILATION)
    raised_features = jax.nn.gelu(border_padded.astype(jnp.float32), approximate=False).astype(
        jnp.bfloat16
    )
    tap_low = jnp.dot(raised_features, dilated_tap_weight[0], preferred_element_type=jnp.float32)
    tap_mid = jnp.dot(raised_features, dilated_tap_weight[1], preferred_element_type=jnp.float32)
    tap_high = jnp.dot(raised_features, dilated_tap_weight[2], preferred_element_type=jnp.float32)
    conv_sum = (
        tap_low[0:genomic_bin_rows] + tap_mid[CONV_DILATION : CONV_DILATION + genomic_bin_rows]
    )
    conv_sum = conv_sum + tap_high[2 * CONV_DILATION : 2 * CONV_DILATION + genomic_bin_rows]
    squeezed = jax.nn.gelu(conv_sum, approximate=False).astype(jnp.bfloat16)
    mixed_rows = activations.astype(jnp.float32) + jnp.dot(
        squeezed, conv_mix, preferred_element_type=jnp.float32
    )
    normed = (
        mixed_rows * lax.rsqrt(jnp.mean(mixed_rows * mixed_rows, axis=-1, keepdims=True) + norm_eps)
    ).astype(jnp.bfloat16)
    queries = jnp.dot(normed, w_query, preferred_element_type=jnp.float32).astype(jnp.bfloat16)
    keyval = jnp.dot(normed, w_keyval, preferred_element_type=jnp.float32).astype(jnp.bfloat16)
    everything = lax.all_gather(keyval, "seq", axis=0, tiled=True)
    return attend(queries, everything, contact_tiles, tile_codes, bin_valid, position, seq_size)


def solution(mesh):
    in_specs = (P(("grp", "seq"), None), P(), P(), P(), P(), P(), P(("grp", "seq"), None), P("grp"))
    out_specs = P(("grp", "seq"), None)
    return jax.shard_map(
        per_device, mesh=mesh, in_specs=in_specs, out_specs=out_specs, check_vma=False
    )
```

```python
import functools
import math

import jax
import jax.numpy as jnp
from jax import lax
from jax.experimental import pallas as pl
from jax.experimental.pallas import tpu as pltpu
from jax.sharding import PartitionSpec as P

HDIM = 128
CONV_DILATION = 8
HALF = 4096


masked_score = -1e30
norm_eps = 1e-06


def halo_rows(activations):
    size = lax.axis_size("seq")
    odd = lax.axis_index("seq") % 2 == 1
    rows = activations.shape[0]
    initial = lax.slice_in_dim(activations, 0, CONV_DILATION, axis=0)
    last = lax.slice_in_dim(activations, rows - CONV_DILATION, rows, axis=0)
    inner = [(i, i ^ 1) for i in range(size)]
    outer = [(i, i + 1) for i in range(1, size - 1, 2)] + [(i + 1, i) for i in range(1, size - 1, 2)]
    from_outer = lax.ppermute(jnp.where(odd, last, initial), "seq", outer)
    from_inner = lax.ppermute(jnp.where(odd, initial, last), "seq", inner)
    before = jnp.where(odd, from_inner, from_outer)
    after = jnp.where(odd, from_outer, from_inner)
    return jnp.concatenate([before, after], axis=0)


def gelu(v):
    return 0.5 * v * (1.0 + lax.erf(v * math.sqrt(0.5)))


def front_kernel(
    x_hbm,
    halo_ref,
    taps_hbm,
    mix_hbm,
    wq_hbm,
    wkv_hbm,
    q_ref,
    kv_ref,
    x_ref,
    taps,
    mix,
    wq,
    wkv,
    outer,
    inner,
    squeezed,
    mixed,
    sems,
):
    rows, channels = x_ref.shape
    hidden = squeezed.shape[1]
    copies = [
        pltpu.make_async_copy(x_hbm, x_ref, sems.at[0]),
        pltpu.make_async_copy(taps_hbm, taps, sems.at[1]),
        pltpu.make_async_copy(mix_hbm, mix, sems.at[2]),
        pltpu.make_async_copy(wq_hbm, wq, sems.at[3]),
        pltpu.make_async_copy(wkv_hbm, wkv, sems.at[4]),
    ]
    for copy in copies:
        copy.start()
    edge = gelu(halo_ref[...].astype(jnp.float32))
    step = 32
    d = CONV_DILATION
    copies[0].wait()

    def lift(i, tail):
        r = pl.multiple_of(i * step, step)
        g = gelu(x_ref[pl.ds(r, step), :].astype(jnp.float32))
        inner[pl.ds(r, step), :] = g.astype(jnp.bfloat16)
        outer[pl.ds(r, step), :] = jnp.concatenate([tail, g[: step - d]], axis=0).astype(
            jnp.bfloat16
        )
        return g[step - d :]

    tail = lax.fori_loop(0, rows // step, lift, edge[:d])
    outer[rows : rows + 2 * d, :] = jnp.concatenate([tail, edge[d:]], axis=0).astype(jnp.bfloat16)

    copies[1].wait()
    wide = 256
    for n in range(hidden // wide):
        cols = slice(n * wide, (n + 1) * wide)
        conv = jnp.dot(outer[0:rows, :], taps[0, :, cols], preferred_element_type=jnp.float32)
        conv += jnp.dot(inner[...], taps[1, :, cols], preferred_element_type=jnp.float32)
        conv += jnp.dot(
            outer[2 * d : rows + 2 * d, :], taps[2, :, cols], preferred_element_type=jnp.float32
        )
        squeezed[:, cols] = gelu(conv).astype(jnp.bfloat16)

    copies[2].wait()
    square = jnp.zeros((rows, 128), jnp.float32)
    for n in range(channels // wide):
        cols = slice(n * wide, (n + 1) * wide)
        part = x_ref[:, cols].astype(jnp.float32) + jnp.dot(
            squeezed[...], mix[:, cols], preferred_element_type=jnp.float32
        )
        mixed[:, cols] = part
        for k in range(wide // 128):
            piece = part[:, k * 128 : (k + 1) * 128]
            square += piece * piece
    gain = lax.rsqrt(jnp.sum(square, axis=1, keepdims=True) / channels + norm_eps)
    copies[3].wait()
    copies[4].wait()
    normed = (mixed[...] * gain).astype(jnp.bfloat16)
    q_ref[...] = jnp.dot(normed, wq[...], preferred_element_type=jnp.float32).astype(jnp.bfloat16)
    kv_ref[...] = jnp.dot(normed, wkv[...], preferred_element_type=jnp.float32).astype(jnp.bfloat16)


def front(activations, halo, dilated_tap_weight, conv_mix, w_query, w_keyval):
    rows, channels = activations.shape
    hidden = conv_mix.shape[0]
    anywhere = pl.BlockSpec(memory_space=pl.ANY)
    vmem = pl.BlockSpec(memory_space=pltpu.VMEM)
    bf16 = jnp.bfloat16
    return pl.pallas_call(
        front_kernel,
        out_shape=[
            jax.ShapeDtypeStruct((rows, w_query.shape[1]), bf16),
            jax.ShapeDtypeStruct((rows, w_keyval.shape[1]), bf16),
        ],
        in_specs=[anywhere, vmem, anywhere, anywhere, anywhere, anywhere],
        out_specs=[vmem, vmem],
        scratch_shapes=[
            pltpu.VMEM(activations.shape, bf16),
            pltpu.VMEM(dilated_tap_weight.shape, bf16),
            pltpu.VMEM(conv_mix.shape, bf16),
            pltpu.VMEM(w_query.shape, bf16),
            pltpu.VMEM(w_keyval.shape, bf16),
            pltpu.VMEM((rows + 2 * CONV_DILATION, channels), bf16),
            pltpu.VMEM((rows, channels), bf16),
            pltpu.VMEM((rows, hidden), bf16),
            pltpu.VMEM((rows, channels), jnp.float32),
            pltpu.SemaphoreType.DMA((5,)),
        ],
        compiler_params=pltpu.CompilerParams(vmem_limit_bytes=60 << 20),
        name="front",
    )(activations, halo, dilated_tap_weight, conv_mix, w_query, w_keyval)


LOG2E = 1.4426950408889634


def attend_kernel(
    reach,
    codes_ref,
    place_ref,
    q_ref,
    kv_ref,
    tiles_ref,
    valid_ref,
    out_ref,
    kv_buf,
    bias_buf,
    scores,
    peak,
    total,
    acc,
    sems,
):
    rows, head_dim = q_ref.shape
    code_count, tile, _ = tiles_ref.shape
    tiles_per_block = rows // tile
    position = place_ref[0]
    first = place_ref[1]
    count = place_ref[2]
    factor = LOG2E / math.sqrt(head_dim)

    def fetch(i):
        return pltpu.make_async_copy(
            kv_ref.at[pl.ds((first + i) * rows, rows), :], kv_buf.at[i], sems.at[i]
        )

    @pl.loop(0, count)
    def _(i):
        fetch(i).start()

    bias_buf[...] = tiles_ref[...].astype(jnp.float32) * LOG2E
    peak[...] = jnp.full_like(peak, masked_score)

    @pl.loop(0, count)
    def _(i):
        fetch(i).wait()
        block = first + i
        keys = kv_buf[i, :, :head_dim]
        raw = lax.dot_general(
            q_ref[...], keys, (((1,), (1,)), ((), ())), preferred_element_type=jnp.float32
        )
        invalid = jnp.where(valid_ref[block] == 1, 0.0, masked_score)
        shift = block - position

        def tile_scores(qt, kt):
            offset = jnp.clip(shift * tiles_per_block + kt - qt + HALF // tile, 0, 2 * (HALF // tile))
            part = raw[qt * tile : (qt + 1) * tile, kt * tile : (kt + 1) * tile]
            return part * factor + bias_buf[codes_ref[qt, offset]]

        def keep(qt, columns):
            peak_now = peak[qt * tile : (qt + 1) * tile, :]
            for kt, column in enumerate(columns):
                scores[i, qt * tile : (qt + 1) * tile, kt * tile : (kt + 1) * tile] = column
                peak_now = jnp.maximum(peak_now, column)
            peak[qt * tile : (qt + 1) * tile, :] = peak_now

        plain = (shift != 0) & (jnp.abs(shift) < reach)

        @pl.when(plain)
        def _():
            for qt in range(tiles_per_block):
                keep(
                    qt,
                    [
                        tile_scores(qt, kt) + invalid[:, kt * tile : (kt + 1) * tile]
                        for kt in range(tiles_per_block)
                    ],
                )

        @pl.when(jnp.logical_not(plain))
        def _():
            lag = lax.broadcasted_iota(jnp.int32, (tile, tile), 1) - lax.broadcasted_iota(
                jnp.int32, (tile, tile), 0
            )
            for qt in range(tiles_per_block):
                columns = []
                for kt in range(tiles_per_block):
                    apart = lag + (shift * rows + (kt - qt) * tile)
                    dropped = jnp.where(
                        apart == 0, 0.0, invalid[:, kt * tile : (kt + 1) * tile]
                    )
                    dropped = jnp.where(jnp.abs(apart) <= HALF, dropped, masked_score)
                    columns.append(tile_scores(qt, kt) + dropped)
                keep(qt, columns)

    peak[...] = jnp.broadcast_to(jnp.max(peak[...], axis=1, keepdims=True), peak.shape)
    total[...] = jnp.zeros_like(total)
    acc[...] = jnp.zeros_like(acc)

    @pl.loop(0, count)
    def _(i):
        parts = []
        sums = total[...]
        for kt in range(tiles_per_block):
            probs = jnp.exp2(scores[i, :, kt * tile : (kt + 1) * tile] - peak[...])
            sums = sums + probs
            parts.append(probs.astype(jnp.bfloat16))
        total[...] = sums
        acc[...] += jnp.dot(
            jnp.concatenate(parts, axis=1),
            kv_buf[i, :, head_dim:],
            preferred_element_type=jnp.float32,
        )

    out_ref[...] = (acc[...] / jnp.sum(total[...], axis=1, keepdims=True)).astype(out_ref.dtype)


def attend(queries, everything, contact_tiles, tile_codes, bin_valid, position, seq_size):
    rows, head_dim = queries.shape
    reach = HALF // rows
    tile = contact_tiles.shape[1]
    slots = min(seq_size, 2 * reach + 1)
    first = jnp.maximum(position - reach, 0)
    last = jnp.minimum(position + reach, seq_size - 1)
    place = jnp.stack([position, first, last - first + 1]).astype(jnp.int32)
    valid_rows = bin_valid.reshape(seq_size, 1, rows)
    vmem = pl.BlockSpec(memory_space=pltpu.VMEM)
    smem = pl.BlockSpec(memory_space=pltpu.SMEM)
    return pl.pallas_call(
        functools.partial(attend_kernel, reach),
        out_shape=jax.ShapeDtypeStruct((rows, head_dim), jnp.bfloat16),
        in_specs=[smem, smem, vmem, pl.BlockSpec(memory_space=pl.ANY), vmem, vmem],
        out_specs=vmem,
        scratch_shapes=[
            pltpu.VMEM((slots, rows, 2 * head_dim), jnp.bfloat16),
            pltpu.VMEM(contact_tiles.shape, jnp.float32),
            pltpu.VMEM((slots, rows, rows), jnp.float32),
            pltpu.VMEM((rows, tile), jnp.float32),
            pltpu.VMEM((rows, tile), jnp.float32),
            pltpu.VMEM((rows, head_dim), jnp.float32),
            pltpu.SemaphoreType.DMA((slots,)),
        ],
        compiler_params=pltpu.CompilerParams(vmem_limit_bytes=60 << 20),
        name="attend",
    )(tile_codes, place, queries, everything, contact_tiles, valid_rows)


def per_device(
    activations,
    dilated_tap_weight,
    conv_mix,
    w_query,
    w_keyval,
    contact_tiles,
    tile_codes,
    bin_valid,
):
    seq_size = lax.axis_size("seq")
    position = lax.axis_index("seq")
    queries, keyval = front(
        activations, halo_rows(activations), dilated_tap_weight, conv_mix, w_query, w_keyval
    )
    everything = lax.all_gather(keyval, "seq", axis=0, tiled=True)
    return attend(queries, everything, contact_tiles, tile_codes, bin_valid, position, seq_size)


def solution(mesh):
    in_specs = (P(("grp", "seq"), None), P(), P(), P(), P(), P(), P(("grp", "seq"), None), P("grp"))
    out_specs = P(("grp", "seq"), None)
    return jax.shard_map(
        per_device, mesh=mesh, in_specs=in_specs, out_specs=out_specs, check_vma=False
    )
```

```python
import functools
import math

import jax
import jax.numpy as jnp
from jax import lax
from jax.experimental import pallas as pl
from jax.experimental.pallas import tpu as pltpu
from jax.sharding import PartitionSpec as P

HDIM = 128
CONV_DILATION = 8
HALF = 4096


masked_score = -1e30
norm_eps = 1e-06


def halo_rows(activations):
    size = lax.axis_size("seq")
    odd = lax.axis_index("seq") % 2 == 1
    rows = activations.shape[0]
    initial = lax.slice_in_dim(activations, 0, CONV_DILATION, axis=0)
    last = lax.slice_in_dim(activations, rows - CONV_DILATION, rows, axis=0)
    inner = [(i, i ^ 1) for i in range(size)]
    outer = [(i, i + 1) for i in range(1, size - 1, 2)] + [(i + 1, i) for i in range(1, size - 1, 2)]
    from_outer = lax.ppermute(jnp.where(odd, last, initial), "seq", outer)
    from_inner = lax.ppermute(jnp.where(odd, initial, last), "seq", inner)
    before = jnp.where(odd, from_inner, from_outer)
    after = jnp.where(odd, from_outer, from_inner)
    return jnp.concatenate([before, after], axis=0)


def gelu(v):
    return 0.5 * v * (1.0 + lax.erf(v * math.sqrt(0.5)))


def front_kernel(
    x_hbm,
    halo_ref,
    codes_ref,
    taps_hbm,
    mix_hbm,
    wq_hbm,
    wkv_hbm,
    q_ref,
    kv_ref,
    x_ref,
    taps,
    mix,
    wq,
    wkv,
    outer,
    inner,
    squeezed,
    mixed,
    sems,
):
    rows, channels = x_ref.shape
    hidden = squeezed.shape[1]
    copies = [
        pltpu.make_async_copy(x_hbm, x_ref, sems.at[0]),
        pltpu.make_async_copy(taps_hbm, taps, sems.at[1]),
        pltpu.make_async_copy(mix_hbm, mix, sems.at[2]),
        pltpu.make_async_copy(wq_hbm, wq, sems.at[3]),
        pltpu.make_async_copy(wkv_hbm, wkv, sems.at[4]),
    ]
    for copy in copies:
        copy.start()
    edge = gelu(halo_ref[...].astype(jnp.float32))
    step = 32
    d = CONV_DILATION
    copies[0].wait()

    def lift(i, tail):
        r = pl.multiple_of(i * step, step)
        g = gelu(x_ref[pl.ds(r, step), :].astype(jnp.float32))
        inner[pl.ds(r, step), :] = g.astype(jnp.bfloat16)
        outer[pl.ds(r, step), :] = jnp.concatenate([tail, g[: step - d]], axis=0).astype(
            jnp.bfloat16
        )
        return g[step - d :]

    tail = lax.fori_loop(0, rows // step, lift, edge[:d])
    outer[rows : rows + 2 * d, :] = jnp.concatenate([tail, edge[d:]], axis=0).astype(jnp.bfloat16)

    copies[1].wait()
    wide = 256
    for n in range(hidden // wide):
        cols = slice(n * wide, (n + 1) * wide)
        conv = jnp.dot(outer[0:rows, :], taps[0, :, cols], preferred_element_type=jnp.float32)
        conv += jnp.dot(inner[...], taps[1, :, cols], preferred_element_type=jnp.float32)
        conv += jnp.dot(
            outer[2 * d : rows + 2 * d, :], taps[2, :, cols], preferred_element_type=jnp.float32
        )
        squeezed[:, cols] = gelu(conv).astype(jnp.bfloat16)

    copies[2].wait()
    square = jnp.zeros((rows, 128), jnp.float32)
    for n in range(channels // wide):
        cols = slice(n * wide, (n + 1) * wide)
        part = x_ref[:, cols].astype(jnp.float32) + jnp.dot(
            squeezed[...], mix[:, cols], preferred_element_type=jnp.float32
        )
        mixed[:, cols] = part
        for k in range(wide // 128):
            piece = part[:, k * 128 : (k + 1) * 128]
            square += piece * piece
    gain = lax.rsqrt(jnp.sum(square, axis=1, keepdims=True) / channels + norm_eps)
    copies[3].wait()
    copies[4].wait()
    normed = (mixed[...] * gain).astype(jnp.bfloat16)
    q_ref[0:rows, :] = jnp.dot(normed, wq[...], preferred_element_type=jnp.float32).astype(
        jnp.bfloat16
    )
    q_ref[rows:, :] = codes_ref[...].astype(jnp.float32).astype(jnp.bfloat16)
    kv_ref[...] = jnp.dot(normed, wkv[...], preferred_element_type=jnp.float32).astype(jnp.bfloat16)


CODE_ROWS = 16


def front(activations, halo, tile_codes, dilated_tap_weight, conv_mix, w_query, w_keyval):
    rows, channels = activations.shape
    hidden = conv_mix.shape[0]
    codes = jnp.pad(
        tile_codes,
        ((0, CODE_ROWS - tile_codes.shape[0]), (0, w_query.shape[1] - tile_codes.shape[1])),
    )
    anywhere = pl.BlockSpec(memory_space=pl.ANY)
    vmem = pl.BlockSpec(memory_space=pltpu.VMEM)
    bf16 = jnp.bfloat16
    return pl.pallas_call(
        front_kernel,
        out_shape=[
            jax.ShapeDtypeStruct((rows + CODE_ROWS, w_query.shape[1]), bf16),
            jax.ShapeDtypeStruct((rows, w_keyval.shape[1]), bf16),
        ],
        in_specs=[anywhere, vmem, vmem, anywhere, anywhere, anywhere, anywhere],
        out_specs=[vmem, vmem],
        scratch_shapes=[
            pltpu.VMEM(activations.shape, bf16),
            pltpu.VMEM(dilated_tap_weight.shape, bf16),
            pltpu.VMEM(conv_mix.shape, bf16),
            pltpu.VMEM(w_query.shape, bf16),
            pltpu.VMEM(w_keyval.shape, bf16),
            pltpu.VMEM((rows + 2 * CONV_DILATION, channels), bf16),
            pltpu.VMEM((rows, channels), bf16),
            pltpu.VMEM((rows, hidden), bf16),
            pltpu.VMEM((rows, channels), jnp.float32),
            pltpu.SemaphoreType.DMA((5,)),
        ],
        compiler_params=pltpu.CompilerParams(vmem_limit_bytes=60 << 20),
        name="front",
    )(activations, halo, codes, dilated_tap_weight, conv_mix, w_query, w_keyval)


LOG2E = 1.4426950408889634


def attend_kernel(
    reach,
    codes_ref,
    place_ref,
    q_ref,
    kv_ref,
    tiles_ref,
    valid_ref,
    out_ref,
    kv_buf,
    bias_buf,
    scores,
    peak,
    total,
    acc,
    sems,
):
    rows, head_dim = q_ref.shape
    code_count, tile, _ = tiles_ref.shape
    tiles_per_block = rows // tile
    position = place_ref[0]
    first = place_ref[1]
    count = place_ref[2]
    factor = LOG2E / math.sqrt(head_dim)

    def fetch(i):
        return pltpu.make_async_copy(
            kv_ref.at[pl.ds((first + i) * rows, rows), :], kv_buf.at[i], sems.at[i]
        )

    @pl.loop(0, count)
    def _(i):
        fetch(i).start()

    bias_buf[...] = tiles_ref[...].astype(jnp.float32) * LOG2E
    peak[...] = jnp.full_like(peak, masked_score)

    @pl.loop(0, count)
    def _(i):
        fetch(i).wait()
        block = first + i
        keys = kv_buf[i, :, :head_dim]
        raw = lax.dot_general(
            q_ref[...], keys, (((1,), (1,)), ((), ())), preferred_element_type=jnp.float32
        )
        invalid = jnp.where(valid_ref[block] == 1, 0.0, masked_score)
        shift = block - position

        def tile_scores(qt, kt):
            offset = jnp.clip(shift * tiles_per_block + kt - qt + HALF // tile, 0, 2 * (HALF // tile))
            part = raw[qt * tile : (qt + 1) * tile, kt * tile : (kt + 1) * tile]
            return part * factor + bias_buf[codes_ref[qt, offset]]

        def keep(qt, columns):
            peak_now = peak[qt * tile : (qt + 1) * tile, :]
            for kt, column in enumerate(columns):
                scores[i, qt * tile : (qt + 1) * tile, kt * tile : (kt + 1) * tile] = column
                peak_now = jnp.maximum(peak_now, column)
            peak[qt * tile : (qt + 1) * tile, :] = peak_now

        plain = (shift != 0) & (jnp.abs(shift) < reach)

        @pl.when(plain)
        def _():
            for qt in range(tiles_per_block):
                keep(
                    qt,
                    [
                        tile_scores(qt, kt) + invalid[:, kt * tile : (kt + 1) * tile]
                        for kt in range(tiles_per_block)
                    ],
                )

        @pl.when(jnp.logical_not(plain))
        def _():
            lag = lax.broadcasted_iota(jnp.int32, (tile, tile), 1) - lax.broadcasted_iota(
                jnp.int32, (tile, tile), 0
            )
            for qt in range(tiles_per_block):
                columns = []
                for kt in range(tiles_per_block):
                    apart = lag + (shift * rows + (kt - qt) * tile)
                    dropped = jnp.where(
                        apart == 0, 0.0, invalid[:, kt * tile : (kt + 1) * tile]
                    )
                    dropped = jnp.where(jnp.abs(apart) <= HALF, dropped, masked_score)
                    columns.append(tile_scores(qt, kt) + dropped)
                keep(qt, columns)

    peak[...] = jnp.broadcast_to(jnp.max(peak[...], axis=1, keepdims=True), peak.shape)
    total[...] = jnp.zeros_like(total)
    acc[...] = jnp.zeros_like(acc)

    @pl.loop(0, count)
    def _(i):
        parts = []
        sums = total[...]
        for kt in range(tiles_per_block):
            probs = jnp.exp2(scores[i, :, kt * tile : (kt + 1) * tile] - peak[...])
            sums = sums + probs
            parts.append(probs.astype(jnp.bfloat16))
        total[...] = sums
        acc[...] += jnp.dot(
            jnp.concatenate(parts, axis=1),
            kv_buf[i, :, head_dim:],
            preferred_element_type=jnp.float32,
        )

    out_ref[...] = (acc[...] / jnp.sum(total[...], axis=1, keepdims=True)).astype(out_ref.dtype)


def score_block(
    reach, shift, raw, invalid, table, code_at, tile, tiles_per_block, keep
):
    factor = LOG2E / math.sqrt(HDIM)
    rows = tile * tiles_per_block

    def tile_scores(qt, kt):
        offset = jnp.clip(shift * tiles_per_block + kt - qt + HALF // tile, 0, 2 * (HALF // tile))
        part = raw[qt * tile : (qt + 1) * tile, kt * tile : (kt + 1) * tile]
        return part * factor + table[code_at(qt, offset)]

    plain = (shift != 0) & (jnp.abs(shift) < reach)

    @pl.when(plain)
    def _():
        for qt in range(tiles_per_block):
            keep(
                qt,
                [
                    tile_scores(qt, kt) + invalid[:, kt * tile : (kt + 1) * tile]
                    for kt in range(tiles_per_block)
                ],
            )

    @pl.when(jnp.logical_not(plain))
    def _():
        lag = lax.broadcasted_iota(jnp.int32, (tile, tile), 1) - lax.broadcasted_iota(
            jnp.int32, (tile, tile), 0
        )
        for qt in range(tiles_per_block):
            columns = []
            for kt in range(tiles_per_block):
                apart = lag + (shift * rows + (kt - qt) * tile)
                dropped = jnp.where(apart == 0, 0.0, invalid[:, kt * tile : (kt + 1) * tile])
                dropped = jnp.where(jnp.abs(apart) <= HALF, dropped, masked_score)
                columns.append(tile_scores(qt, kt) + dropped)
            keep(qt, columns)


def absorb_kernel(reach, flips, blocks, begin, pack, codes_ref, *refs):
    sets, n = len(flips), len(blocks)
    q_refs, refs = refs[:sets], refs[sets:]
    kv_refs, refs = refs[:n], refs[n:]
    tiles_ref, valid_ref = refs[:2]
    refs = refs[2:]
    if not begin:
        state_refs, refs = refs[: 3 * sets], refs[3 * sets :]
    outs = 1 if pack else 3 * sets
    out_refs, refs = refs[:outs], refs[outs:]
    kv_buf, table, scores, peak, total, acc, sems = refs
    rows, head_dim = acc.shape
    tile = tiles_ref.shape[1]
    tiles_per_block = rows // tile
    position = lax.axis_index("seq")
    copies = [
        pltpu.make_async_copy(kv_refs[j], kv_buf.at[j], sems.at[j]) for j in range(n)
    ]
    for copy in copies:
        copy.start()
    table[...] = tiles_ref[...].astype(jnp.float32) * LOG2E
    for copy in copies:
        copy.wait()

    def pick(values, j):
        chosen = jnp.int32(values[0])
        for k in range(1, n):
            chosen = jnp.where(j == k, values[k], chosen)
        return chosen

    for s, flip in enumerate(flips):
        owner = position ^ flip
        q_ref = q_refs[s]
        half = 0 if flip == 0 else tiles_per_block
        if begin:
            peak[...] = jnp.full_like(peak, masked_score)
        else:
            peak[...] = state_refs[3 * s][...]

        def shift_of(j):
            return (position ^ pick(blocks, j)) - owner

        @pl.loop(0, n)
        def _(j):
            shift = shift_of(j)

            @pl.when(jnp.abs(shift) <= reach)
            def _():
                raw = lax.dot_general(
                    q_ref[0:rows, :],
                    kv_buf[j, :, :head_dim],
                    (((1,), (1,)), ((), ())),
                    preferred_element_type=jnp.float32,
                )
                invalid = jnp.where(valid_ref[owner + shift] == 1, 0.0, masked_score)

                def keep(qt, columns):
                    span = slice(qt * tile, (qt + 1) * tile)
                    peak_now = peak[span, :]
                    for kt, column in enumerate(columns):
                        scores[j, span, kt * tile : (kt + 1) * tile] = column
                        peak_now = jnp.maximum(peak_now, column)
                    peak[span, :] = peak_now

                score_block(
                    reach,
                    shift,
                    raw,
                    invalid,
                    table,
                    lambda qt, offset: codes_ref[half + qt, offset],
                    tile,
                    tiles_per_block,
                    keep,
                )

        peak[...] = jnp.broadcast_to(jnp.max(peak[...], axis=1, keepdims=True), peak.shape)
        if begin:
            total[...] = jnp.zeros_like(total)
            acc[...] = jnp.zeros_like(acc)
        else:
            rescale = jnp.exp2(state_refs[3 * s][...] - peak[...])
            total[...] = state_refs[3 * s + 1][...] * rescale
            acc[...] = state_refs[3 * s + 2][...] * rescale

        @pl.loop(0, n)
        def _(j):
            @pl.when(jnp.abs(shift_of(j)) <= reach)
            def _():
                parts = []
                sums = total[...]
                for kt in range(tiles_per_block):
                    probs = jnp.exp2(scores[j, :, kt * tile : (kt + 1) * tile] - peak[...])
                    sums = sums + probs
                    parts.append(probs.astype(jnp.bfloat16))
                total[...] = sums
                acc[...] += jnp.dot(
                    jnp.concatenate(parts, axis=1),
                    kv_buf[j, :, head_dim:],
                    preferred_element_type=jnp.float32,
                )

        if pack:
            out_refs[0][0:rows, :] = acc[...]
            sums = jnp.broadcast_to(jnp.sum(total[...], axis=1, keepdims=True), total.shape)
            eye = on_diagonal(tile)
            lines = []
            for column in (peak[...], sums):
                for qt in range(tiles_per_block):
                    part = column[qt * tile : (qt + 1) * tile, :]
                    lines.append(jnp.sum(jnp.where(eye, part, 0.0), axis=0, keepdims=True))
            out_refs[0][rows:, :] = jnp.concatenate(lines, axis=0)
        else:
            out_refs[3 * s][...] = peak[...]
            out_refs[3 * s + 1][...] = total[...]
            out_refs[3 * s + 2][...] = acc[...]


def on_diagonal(tile):
    return lax.broadcasted_iota(jnp.int32, (tile, tile), 0) == lax.broadcasted_iota(
        jnp.int32, (tile, tile), 1
    )


def absorb(name, reach, codes, queries, keyvals, contact_tiles, valid_rows, flips, blocks, state, pack):
    rows = keyvals[0].shape[0]
    head_dim = queries[0].shape[1]
    tile = contact_tiles.shape[1]
    n = len(blocks)
    vmem = pl.BlockSpec(memory_space=pltpu.VMEM)
    smem = pl.BlockSpec(memory_space=pltpu.SMEM)
    anywhere = pl.BlockSpec(memory_space=pl.ANY)
    column = jax.ShapeDtypeStruct((rows, tile), jnp.float32)
    if pack:
        out_shape = [jax.ShapeDtypeStruct((rows + 2 * (rows // tile), head_dim), jnp.float32)]
    else:
        out_shape = [column, column, column] * len(flips)
    units = len(flips) * n
    return pl.pallas_call(
        functools.partial(absorb_kernel, reach, flips, blocks, not state, pack),
        out_shape=out_shape,
        in_specs=[smem]
        + [vmem] * len(flips)
        + [anywhere] * n
        + [vmem, vmem]
        + [vmem] * len(state),
        out_specs=[vmem] * len(out_shape),
        scratch_shapes=[
            pltpu.VMEM((n, rows, 2 * head_dim), jnp.bfloat16),
            pltpu.VMEM(contact_tiles.shape, jnp.float32),
            pltpu.VMEM((n, rows, rows), jnp.float32),
            pltpu.VMEM((rows, tile), jnp.float32),
            pltpu.VMEM((rows, tile), jnp.float32),
            pltpu.VMEM((rows, head_dim), jnp.float32),
            pltpu.SemaphoreType.DMA((n,)),
        ],
        compiler_params=pltpu.CompilerParams(vmem_limit_bytes=40 << 20),
        cost_estimate=pl.CostEstimate(
            flops=units * 4 * rows * rows * head_dim,
            bytes_accessed=units * 4 * rows * rows,
            transcendentals=units * rows * rows,
        ),
        name=name,
    )(codes, *queries, *keyvals, contact_tiles, valid_rows, *state)


def merge_kernel(peak_ref, total_ref, acc_ref, pack_ref, out_ref):
    rows, head_dim = acc_ref.shape
    tile = peak_ref.shape[1]
    eye = on_diagonal(tile)
    count = rows // tile
    for qt in range(count):
        span = slice(qt * tile, (qt + 1) * tile)

        def column(line):
            row = pack_ref[rows + line : rows + line + 1, :]
            return jnp.sum(jnp.where(eye, row, 0.0), axis=1, keepdims=True)

        peak_a = peak_ref[span, :]
        peak_b = column(qt)
        total_a = jnp.sum(total_ref[span, :], axis=1, keepdims=True)
        total_b = column(count + qt)
        top = jnp.maximum(peak_a, peak_b)
        scale_a = jnp.exp2(peak_a - top)
        scale_b = jnp.exp2(peak_b - top)
        whole = total_a * scale_a + total_b * scale_b
        out_ref[span, :] = (
            (acc_ref[span, :] * scale_a + pack_ref[span, :] * scale_b) / whole
        ).astype(out_ref.dtype)


def attend_split(queries, keyval, contact_tiles, tile_codes, bin_valid, seq_size):
    rows = keyval.shape[0]
    reach = HALF // rows
    z = seq_size // 4
    half = z // 2
    valid_rows = bin_valid.reshape(seq_size, 1, rows)

    def trade(x, flip, some=None):
        pairs = [(i, i ^ flip) for i in range(seq_size) if some is None or some(i // z)]
        return lax.ppermute(x, "seq", pairs)

    twin = trade(keyval, 1)
    peer_queries = trade(queries, half)
    near = trade(keyval, z)
    middle = trade(keyval, 3 * z, lambda level: level in (1, 2))
    far = trade(keyval, 2 * z)
    peer_codes = peer_queries[rows : rows + tile_codes.shape[0], : tile_codes.shape[1]]
    codes = jnp.concatenate([tile_codes, peer_codes.astype(jnp.int32)], axis=0)
    common = (contact_tiles, valid_rows)
    both = [queries, peer_queries]
    state = absorb(
        "own", reach, codes, both, [keyval, twin], *common, (0, half), (0, 1), [], False
    )
    near, middle, state = lax.optimization_barrier((near, middle, state))
    near_twin, middle_twin = trade(near, 1), trade(middle, 1)
    state = absorb(
        "near",
        reach,
        codes,
        both,
        [near, near_twin, middle, middle_twin],
        *common,
        (0, half),
        (z, z + 1, 3 * z, 3 * z + 1),
        state,
        False,
    )
    far, state = lax.optimization_barrier((far, state))
    last = [far, trade(far, 1)]
    steps = (2 * z, 2 * z + 1)
    (pack,) = absorb(
        "far_peer", reach, codes, [peer_queries], last, *common, (half,), steps, state[3:], True
    )
    other = trade(pack, half)
    peak, total, acc = absorb(
        "far_own", reach, codes, [queries], last, *common, (0,), steps, state[:3], False
    )
    vmem = pl.BlockSpec(memory_space=pltpu.VMEM)
    return pl.pallas_call(
        merge_kernel,
        out_shape=jax.ShapeDtypeStruct((rows, queries.shape[1]), jnp.bfloat16),
        in_specs=[vmem] * 4,
        out_specs=vmem,
        compiler_params=pltpu.CompilerParams(vmem_limit_bytes=8 << 20),
        name="merge",
    )(peak, total, acc, other)


def attend(queries, everything, contact_tiles, tile_codes, bin_valid, position, seq_size):
    rows, head_dim = queries.shape
    reach = HALF // rows
    tile = contact_tiles.shape[1]
    slots = min(seq_size, 2 * reach + 1)
    first = jnp.maximum(position - reach, 0)
    last = jnp.minimum(position + reach, seq_size - 1)
    place = jnp.stack([position, first, last - first + 1]).astype(jnp.int32)
    valid_rows = bin_valid.reshape(seq_size, 1, rows)
    vmem = pl.BlockSpec(memory_space=pltpu.VMEM)
    smem = pl.BlockSpec(memory_space=pltpu.SMEM)
    return pl.pallas_call(
        functools.partial(attend_kernel, reach),
        out_shape=jax.ShapeDtypeStruct((rows, head_dim), jnp.bfloat16),
        in_specs=[smem, smem, vmem, pl.BlockSpec(memory_space=pl.ANY), vmem, vmem],
        out_specs=vmem,
        scratch_shapes=[
            pltpu.VMEM((slots, rows, 2 * head_dim), jnp.bfloat16),
            pltpu.VMEM(contact_tiles.shape, jnp.float32),
            pltpu.VMEM((slots, rows, rows), jnp.float32),
            pltpu.VMEM((rows, tile), jnp.float32),
            pltpu.VMEM((rows, tile), jnp.float32),
            pltpu.VMEM((rows, head_dim), jnp.float32),
            pltpu.SemaphoreType.DMA((slots,)),
        ],
        compiler_params=pltpu.CompilerParams(vmem_limit_bytes=60 << 20),
        name="attend",
    )(tile_codes, place, queries, everything, contact_tiles, valid_rows)


def per_device(
    activations,
    dilated_tap_weight,
    conv_mix,
    w_query,
    w_keyval,
    contact_tiles,
    tile_codes,
    bin_valid,
):
    seq_size = lax.axis_size("seq")
    position = lax.axis_index("seq")
    queries, keyval = front(
        activations,
        halo_rows(activations),
        tile_codes,
        dilated_tap_weight,
        conv_mix,
        w_query,
        w_keyval,
    )
    if seq_size == 16 and seq_size * activations.shape[0] == 2 * HALF:
        return attend_split(queries, keyval, contact_tiles, tile_codes, bin_valid, seq_size)
    queries = queries[: activations.shape[0]]
    everything = lax.all_gather(keyval, "seq", axis=0, tiled=True)
    return attend(queries, everything, contact_tiles, tile_codes, bin_valid, position, seq_size)


def solution(mesh):
    in_specs = (P(("grp", "seq"), None), P(), P(), P(), P(), P(), P(("grp", "seq"), None), P("grp"))
    out_specs = P(("grp", "seq"), None)
    return jax.shard_map(
        per_device, mesh=mesh, in_specs=in_specs, out_specs=out_specs, check_vma=False
    )
```

```python
import functools
import math

import jax
import jax.numpy as jnp
from jax import lax
from jax.experimental import pallas as pl
from jax.experimental.pallas import tpu as pltpu
from jax.sharding import PartitionSpec as P


HDIM = 128
CONV_DILATION = 8
HALF = 4096


masked_score = -1e30
norm_eps = 1e-06
LOG2E = 1.4426950408889634


def halo_rows(activations):
    size = lax.axis_size("seq")
    odd = lax.axis_index("seq") % 2 == 1
    rows = activations.shape[0]
    initial = lax.slice_in_dim(activations, 0, CONV_DILATION, axis=0)
    last = lax.slice_in_dim(activations, rows - CONV_DILATION, rows, axis=0)
    inner = [(i, i ^ 1) for i in range(size)]
    outer = [(i, i + 1) for i in range(1, size - 1, 2)] + [(i + 1, i) for i in range(1, size - 1, 2)]
    from_inner = lax.ppermute(jnp.where(odd, initial, last), "seq", inner)
    from_outer = lax.ppermute(jnp.where(odd, last, initial), "seq", outer)
    return from_inner, from_outer


def gelu(v):
    return 0.5 * v * (1.0 + lax.erf(v * math.sqrt(0.5)))


def lift_kernel(x_hbm, taps_hbm, mix_hbm, wq_hbm, wkv_hbm, tiles_hbm, *refs):
    x_ref, taps, mix, wq, wkv, inner, outer, table, tiles, sems = refs
    copies = [
        pltpu.make_async_copy(source, target, sems.at[i])
        for i, (source, target) in enumerate(
            [
                (x_hbm, x_ref),
                (tiles_hbm, tiles),
                (taps_hbm, taps),
                (mix_hbm, mix),
                (wq_hbm, wq),
                (wkv_hbm, wkv),
            ]
        )
    ]
    for copy in copies:
        copy.start()
    rows, channels = x_ref.shape
    step = 32
    d = CONV_DILATION
    copies[0].wait()

    def lift(i, tail):
        r = pl.multiple_of(i * step, step)
        g = gelu(x_ref[pl.ds(r, step), :].astype(jnp.float32))
        inner[pl.ds(r, step), :] = g.astype(jnp.bfloat16)
        outer[pl.ds(r, step), :] = jnp.concatenate([tail, g[: step - d]], axis=0).astype(
            jnp.bfloat16
        )
        return g[step - d :]

    edge = jnp.zeros((d, channels), jnp.float32)
    tail = lax.fori_loop(0, rows // step, lift, edge)
    outer[rows : rows + 2 * d, :] = jnp.concatenate([tail, edge], axis=0).astype(jnp.bfloat16)
    copies[1].wait()
    table[...] = tiles[...].astype(jnp.float32) * LOG2E
    for copy in copies[2:]:
        copy.wait()


def lift(activations, dilated_tap_weight, conv_mix, w_query, w_keyval, contact_tiles):
    rows, channels = activations.shape
    moved = [
        pltpu.with_memory_space_constraint(a, pltpu.HBM)
        for a in (activations, dilated_tap_weight, conv_mix, w_query, w_keyval)
    ]
    contact_tiles = pltpu.with_memory_space_constraint(contact_tiles, pltpu.HBM)
    vmem = pl.BlockSpec(memory_space=pltpu.VMEM)
    return pl.pallas_call(
        lift_kernel,
        out_shape=[jax.ShapeDtypeStruct(a.shape, a.dtype) for a in moved]
        + [
            jax.ShapeDtypeStruct((rows, channels), jnp.bfloat16),
            jax.ShapeDtypeStruct((rows + 2 * CONV_DILATION, channels), jnp.bfloat16),
            jax.ShapeDtypeStruct(contact_tiles.shape, jnp.float32),
        ],
        in_specs=[pl.BlockSpec(memory_space=pltpu.HBM)] * 6,
        out_specs=[vmem] * 8,
        scratch_shapes=[
            pltpu.VMEM(contact_tiles.shape, contact_tiles.dtype),
            pltpu.SemaphoreType.DMA((6,)),
        ],
        compiler_params=pltpu.CompilerParams(vmem_limit_bytes=24 << 20),
        name="lift",
    )(*moved, contact_tiles)


def front_kernel(
    x_ref,
    taps,
    mix,
    wq,
    wkv,
    inner,
    outer_ref,
    twin_ref,
    outside_ref,
    codes_ref,
    q_ref,
    kv_ref,
    outer,
    squeezed,
    mixed,
):
    rows, channels = x_ref.shape
    hidden = squeezed.shape[1]
    d = CONV_DILATION
    odd = lax.axis_index("seq") % 2 == 1
    beside = gelu(twin_ref[...].astype(jnp.float32))
    beyond = gelu(outside_ref[...].astype(jnp.float32))
    before = jnp.where(odd, beside, beyond)
    after = jnp.where(odd, beyond, beside)
    outer[...] = outer_ref[...]
    initial = outer_ref[0 : 2 * d, :].astype(jnp.float32)[d:]
    last = outer_ref[rows : rows + 2 * d, :].astype(jnp.float32)[:d]
    outer[0 : 2 * d, :] = jnp.concatenate([before, initial], axis=0).astype(jnp.bfloat16)
    outer[rows : rows + 2 * d, :] = jnp.concatenate([last, after], axis=0).astype(jnp.bfloat16)

    wide = 256
    for n in range(hidden // wide):
        cols = slice(n * wide, (n + 1) * wide)
        conv = jnp.dot(outer[0:rows, :], taps[0, :, cols], preferred_element_type=jnp.float32)
        conv += jnp.dot(inner[...], taps[1, :, cols], preferred_element_type=jnp.float32)
        conv += jnp.dot(
            outer[2 * d : rows + 2 * d, :], taps[2, :, cols], preferred_element_type=jnp.float32
        )
        squeezed[:, cols] = gelu(conv).astype(jnp.bfloat16)

    square = jnp.zeros((rows, 128), jnp.float32)
    for n in range(channels // wide):
        cols = slice(n * wide, (n + 1) * wide)
        part = x_ref[:, cols].astype(jnp.float32) + jnp.dot(
            squeezed[...], mix[:, cols], preferred_element_type=jnp.float32
        )
        mixed[:, cols] = part
        for k in range(wide // 128):
            piece = part[:, k * 128 : (k + 1) * 128]
            square += piece * piece
    gain = lax.rsqrt(jnp.sum(square, axis=1, keepdims=True) / channels + norm_eps)
    normed = (mixed[...] * gain).astype(jnp.bfloat16)
    q_ref[0:rows, :] = jnp.dot(normed, wq[...], preferred_element_type=jnp.float32).astype(
        jnp.bfloat16
    )
    q_ref[rows:, :] = jnp.zeros((q_ref.shape[0] - rows, q_ref.shape[1]), jnp.bfloat16)
    q_ref[rows : rows + codes_ref.shape[0], 0 : codes_ref.shape[1]] = (
        codes_ref[...].astype(jnp.float32).astype(jnp.bfloat16)
    )
    kv_ref[...] = jnp.dot(normed, wkv[...], preferred_element_type=jnp.float32).astype(jnp.bfloat16)


CODE_ROWS = 16


def front(lifted, halo, tile_codes):
    activations, _, conv_mix, w_query, w_keyval, _, outer = lifted
    rows, channels = activations.shape
    vmem = pl.BlockSpec(memory_space=pltpu.VMEM)
    bf16 = jnp.bfloat16
    return pl.pallas_call(
        front_kernel,
        out_shape=[
            jax.ShapeDtypeStruct((rows + CODE_ROWS, w_query.shape[1]), bf16),
            jax.ShapeDtypeStruct((rows, w_keyval.shape[1]), bf16),
        ],
        in_specs=[vmem] * 10,
        out_specs=[vmem, vmem],
        scratch_shapes=[
            pltpu.VMEM(outer.shape, bf16),
            pltpu.VMEM((rows, conv_mix.shape[0]), bf16),
            pltpu.VMEM((rows, channels), jnp.float32),
        ],
        compiler_params=pltpu.CompilerParams(vmem_limit_bytes=24 << 20),
        name="front",
    )(*lifted, *halo, tile_codes)


def attend_kernel(
    reach,
    codes_ref,
    place_ref,
    q_ref,
    kv_ref,
    tiles_ref,
    valid_ref,
    out_ref,
    kv_buf,
    bias_buf,
    scores,
    peak,
    total,
    acc,
    sems,
):
    rows, head_dim = q_ref.shape
    _, tile, _ = tiles_ref.shape
    tiles_per_block = rows // tile
    position = place_ref[0]
    first = place_ref[1]
    count = place_ref[2]
    factor = LOG2E / math.sqrt(head_dim)

    def fetch(i):
        return pltpu.make_async_copy(
            kv_ref.at[pl.ds((first + i) * rows, rows), :], kv_buf.at[i], sems.at[i]
        )

    @pl.loop(0, count)
    def _(i):
        fetch(i).start()

    bias_buf[...] = tiles_ref[...].astype(jnp.float32) * LOG2E
    peak[...] = jnp.full_like(peak, masked_score)

    @pl.loop(0, count)
    def _(i):
        fetch(i).wait()
        block = first + i
        keys = kv_buf[i, :, :head_dim]
        raw = lax.dot_general(
            q_ref[...], keys, (((1,), (1,)), ((), ())), preferred_element_type=jnp.float32
        )
        invalid = jnp.where(valid_ref[block] == 1, 0.0, masked_score)
        shift = block - position

        def tile_scores(qt, kt):
            offset = jnp.clip(shift * tiles_per_block + kt - qt + HALF // tile, 0, 2 * (HALF // tile))
            part = raw[qt * tile : (qt + 1) * tile, kt * tile : (kt + 1) * tile]
            return part * factor + bias_buf[codes_ref[qt, offset]]

        def keep(qt, columns):
            peak_now = peak[qt * tile : (qt + 1) * tile, :]
            for kt, column in enumerate(columns):
                scores[i, qt * tile : (qt + 1) * tile, kt * tile : (kt + 1) * tile] = column
                peak_now = jnp.maximum(peak_now, column)
            peak[qt * tile : (qt + 1) * tile, :] = peak_now

        plain = (shift != 0) & (jnp.abs(shift) < reach)

        @pl.when(plain)
        def _():
            for qt in range(tiles_per_block):
                keep(
                    qt,
                    [
                        tile_scores(qt, kt) + invalid[:, kt * tile : (kt + 1) * tile]
                        for kt in range(tiles_per_block)
                    ],
                )

        @pl.when(jnp.logical_not(plain))
        def _():
            lag = lax.broadcasted_iota(jnp.int32, (tile, tile), 1) - lax.broadcasted_iota(
                jnp.int32, (tile, tile), 0
            )
            for qt in range(tiles_per_block):
                columns = []
                for kt in range(tiles_per_block):
                    apart = lag + (shift * rows + (kt - qt) * tile)
                    dropped = jnp.where(
                        apart == 0, 0.0, invalid[:, kt * tile : (kt + 1) * tile]
                    )
                    dropped = jnp.where(jnp.abs(apart) <= HALF, dropped, masked_score)
                    columns.append(tile_scores(qt, kt) + dropped)
                keep(qt, columns)

    peak[...] = jnp.broadcast_to(jnp.max(peak[...], axis=1, keepdims=True), peak.shape)
    total[...] = jnp.zeros_like(total)
    acc[...] = jnp.zeros_like(acc)

    @pl.loop(0, count)
    def _(i):
        parts = []
        sums = total[...]
        for kt in range(tiles_per_block):
            probs = jnp.exp2(scores[i, :, kt * tile : (kt + 1) * tile] - peak[...])
            sums = sums + probs
            parts.append(probs.astype(jnp.bfloat16))
        total[...] = sums
        acc[...] += jnp.dot(
            jnp.concatenate(parts, axis=1),
            kv_buf[i, :, head_dim:],
            preferred_element_type=jnp.float32,
        )

    out_ref[...] = (acc[...] / jnp.sum(total[...], axis=1, keepdims=True)).astype(out_ref.dtype)


def block_scores(shift, edge, raw, invalid, table, codes_ref, half, qt, tile):
    factor = LOG2E / math.sqrt(HDIM)
    count = raw.shape[1] // tile
    columns = []
    if edge:
        lag = lax.broadcasted_iota(jnp.int32, (tile, tile), 1) - lax.broadcasted_iota(
            jnp.int32, (tile, tile), 0
        )
    for kt in range(count):
        span = slice(kt * tile, (kt + 1) * tile)
        offset = jnp.clip(shift * count + kt - qt + HALF // tile, 0, 2 * (HALF // tile))
        dropped = invalid[:, span]
        if edge:
            apart = lag + (shift * (tile * count) + (kt - qt) * tile)
            dropped = jnp.where(apart == 0, 0.0, dropped)
            dropped = jnp.where(jnp.abs(apart) <= HALF, dropped, masked_score)
        part = raw[qt * tile : (qt + 1) * tile, span]
        columns.append((part * factor + table[codes_ref[half + qt, offset]]) + dropped)
    return columns


def absorb_kernel(reach, flips, blocks, begin, pack, codes_ref, *refs):
    sets, n = len(flips), len(blocks)
    q_refs, refs = refs[:sets], refs[sets:]
    kv_refs, refs = refs[:n], refs[n:]
    table, valid_ref = refs[:2]
    refs = refs[2:]
    if not begin:
        state_refs, refs = refs[: 3 * sets], refs[3 * sets :]
    outs = 1 if pack else 3 * sets
    out_refs, refs = refs[:outs], refs[outs:]
    scores, peak, total, acc = refs
    rows, head_dim = acc.shape
    tile = table.shape[1]
    tiles_per_block = rows // tile
    position = lax.axis_index("seq")

    for s, flip in enumerate(flips):
        owner = position ^ flip
        q_ref = q_refs[s]
        half = 0 if flip == 0 else tiles_per_block
        if begin:
            peak[...] = jnp.full_like(peak, masked_score)
        else:
            peak[...] = state_refs[3 * s][...]

        def each(step):
            for j, block in enumerate(blocks):
                shift = (position ^ block) - owner
                run = functools.partial(step, j, shift, (block ^ flip) in (0, reach))
                if block ^ flip < reach:
                    run()
                else:
                    pl.when(jnp.abs(shift) <= reach)(run)

        def score(j, shift, edge):
            raw = lax.dot_general(
                q_ref[0:rows, :],
                kv_refs[j][:, :head_dim],
                (((1,), (1,)), ((), ())),
                preferred_element_type=jnp.float32,
            )
            invalid = jnp.where(valid_ref[owner + shift] == 1, 0.0, masked_score)
            for qt in range(tiles_per_block):
                span = slice(qt * tile, (qt + 1) * tile)
                peak_now = peak[span, :]
                columns = block_scores(
                    shift, edge, raw, invalid, table, codes_ref, half, qt, tile
                )
                for kt, column in enumerate(columns):
                    scores[j, span, kt * tile : (kt + 1) * tile] = column
                    peak_now = jnp.maximum(peak_now, column)
                peak[span, :] = peak_now

        def weigh(j, shift, edge):
            parts = []
            sums = total[...]
            for kt in range(tiles_per_block):
                probs = jnp.exp2(scores[j, :, kt * tile : (kt + 1) * tile] - peak[...])
                sums = sums + probs
                parts.append(probs.astype(jnp.bfloat16))
            total[...] = sums
            acc[...] += jnp.dot(
                jnp.concatenate(parts, axis=1),
                kv_refs[j][:, head_dim:],
                preferred_element_type=jnp.float32,
            )

        each(score)
        peak[...] = jnp.broadcast_to(jnp.max(peak[...], axis=1, keepdims=True), peak.shape)
        if begin:
            total[...] = jnp.zeros_like(total)
            acc[...] = jnp.zeros_like(acc)
        else:
            rescale = jnp.exp2(state_refs[3 * s][...] - peak[...])
            total[...] = state_refs[3 * s + 1][...] * rescale
            acc[...] = state_refs[3 * s + 2][...] * rescale
        each(weigh)

        if pack:
            out_refs[0][0:rows, :] = acc[...]
            sums = jnp.broadcast_to(jnp.sum(total[...], axis=1, keepdims=True), total.shape)
            eye = on_diagonal(tile)
            lines = []
            for column in (peak[...], sums):
                for qt in range(tiles_per_block):
                    part = column[qt * tile : (qt + 1) * tile, :]
                    lines.append(jnp.sum(jnp.where(eye, part, 0.0), axis=0, keepdims=True))
            out_refs[0][rows:, :] = jnp.concatenate(lines, axis=0)
        else:
            out_refs[3 * s][...] = peak[...]
            out_refs[3 * s + 1][...] = total[...]
            out_refs[3 * s + 2][...] = acc[...]


def on_diagonal(tile):
    return lax.broadcasted_iota(jnp.int32, (tile, tile), 0) == lax.broadcasted_iota(
        jnp.int32, (tile, tile), 1
    )


def absorb(reach, codes, queries, keyvals, table, valid_rows, flips, blocks, state, pack):
    rows = keyvals[0].shape[0]
    head_dim = queries[0].shape[1]
    tile = table.shape[1]
    n = len(blocks)
    vmem = pl.BlockSpec(memory_space=pltpu.VMEM)
    smem = pl.BlockSpec(memory_space=pltpu.SMEM)
    column = jax.ShapeDtypeStruct((rows, tile), jnp.float32)
    if pack:
        out_shape = [jax.ShapeDtypeStruct((rows + 2 * (rows // tile), head_dim), jnp.float32)]
    else:
        out_shape = [column, column, column] * len(flips)
    units = len(flips) * n
    return pl.pallas_call(
        functools.partial(absorb_kernel, reach, flips, blocks, not state, pack),
        out_shape=out_shape,
        in_specs=[smem] + [vmem] * (len(flips) + n + 2 + len(state)),
        out_specs=[vmem] * len(out_shape),
        scratch_shapes=[
            pltpu.VMEM((n, rows, rows), jnp.float32),
            pltpu.VMEM((rows, tile), jnp.float32),
            pltpu.VMEM((rows, tile), jnp.float32),
            pltpu.VMEM((rows, head_dim), jnp.float32),
        ],
        compiler_params=pltpu.CompilerParams(vmem_limit_bytes=24 << 20),
        cost_estimate=pl.CostEstimate(
            flops=units * 4 * rows * rows * head_dim,
            bytes_accessed=units * 4 * rows * rows,
            transcendentals=units * rows * rows,
        ),
    )(codes, *queries, *keyvals, table, valid_rows, *state)


def merge_kernel(peak_ref, total_ref, acc_ref, pack_ref, out_ref):
    rows, _ = acc_ref.shape
    tile = peak_ref.shape[1]
    eye = on_diagonal(tile)
    count = rows // tile
    for qt in range(count):
        span = slice(qt * tile, (qt + 1) * tile)

        def column(line):
            row = pack_ref[rows + line : rows + line + 1, :]
            return jnp.sum(jnp.where(eye, row, 0.0), axis=1, keepdims=True)

        peak_a = peak_ref[span, :]
        peak_b = column(qt)
        total_a = jnp.sum(total_ref[span, :], axis=1, keepdims=True)
        total_b = column(count + qt)
        top = jnp.maximum(peak_a, peak_b)
        scale_a = jnp.exp2(peak_a - top)
        scale_b = jnp.exp2(peak_b - top)
        whole = total_a * scale_a + total_b * scale_b
        out_ref[span, :] = (
            (acc_ref[span, :] * scale_a + pack_ref[span, :] * scale_b) / whole
        ).astype(out_ref.dtype)


def attend_split(queries, keyval, table, tile_codes, bin_valid, seq_size):
    rows = keyval.shape[0]
    reach = HALF // rows
    z = seq_size // 4
    half = z // 2
    valid_rows = bin_valid.reshape(seq_size, 1, rows)

    def trade(x, flip, some=None):
        pairs = [(i, i ^ flip) for i in range(seq_size) if some is None or some(i // z)]
        return lax.ppermute(x, "seq", pairs)

    peer_queries = trade(queries, half)
    far = trade(keyval, 2 * z)
    middle = trade(keyval, 3 * z, lambda level: level in (1, 2))
    near = trade(keyval, z)
    twin = trade(keyval, 1)
    peer_codes = peer_queries[rows : rows + tile_codes.shape[0], : tile_codes.shape[1]]
    codes = jnp.concatenate([tile_codes, peer_codes.astype(jnp.int32)], axis=0)
    common = (table, valid_rows)
    state = absorb(
        reach, codes, [queries, peer_queries], [keyval, twin], *common, (0, half), (0, 1), [], False
    )
    near, state = lax.optimization_barrier((near, state))
    near_twin = trade(near, 1)
    state = absorb(
        reach,
        codes,
        [queries, peer_queries],
        [near, near_twin],
        *common,
        (0, half),
        (z, z + 1),
        state,
        False,
    )
    middle, far, state = lax.optimization_barrier((middle, far, state))
    middle_twin = trade(middle, 1)
    far_twin = trade(far, 1)
    away = [middle, middle_twin, far, far_twin]
    leaps = (3 * z, 3 * z + 1, 2 * z, 2 * z + 1)
    (pack,) = absorb(reach, codes, [peer_queries], away, *common, (half,), leaps, state[3:], True)
    other = trade(pack, half)
    peak, total, acc = absorb(reach, codes, [queries], away, *common, (0,), leaps, state[:3], False)
    vmem = pl.BlockSpec(memory_space=pltpu.VMEM)
    return pl.pallas_call(
        merge_kernel,
        out_shape=jax.ShapeDtypeStruct((rows, queries.shape[1]), jnp.bfloat16),
        in_specs=[vmem] * 4,
        out_specs=vmem,
        compiler_params=pltpu.CompilerParams(vmem_limit_bytes=8 << 20),
        name="merge",
    )(peak, total, acc, other)


def attend(queries, everything, contact_tiles, tile_codes, bin_valid, position, seq_size):
    rows, head_dim = queries.shape
    reach = HALF // rows
    tile = contact_tiles.shape[1]
    slots = min(seq_size, 2 * reach + 1)
    first = jnp.maximum(position - reach, 0)
    last = jnp.minimum(position + reach, seq_size - 1)
    place = jnp.stack([position, first, last - first + 1]).astype(jnp.int32)
    valid_rows = bin_valid.reshape(seq_size, 1, rows)
    vmem = pl.BlockSpec(memory_space=pltpu.VMEM)
    smem = pl.BlockSpec(memory_space=pltpu.SMEM)
    return pl.pallas_call(
        functools.partial(attend_kernel, reach),
        out_shape=jax.ShapeDtypeStruct((rows, head_dim), jnp.bfloat16),
        in_specs=[smem, smem, vmem, pl.BlockSpec(memory_space=pl.ANY), vmem, vmem],
        out_specs=vmem,
        scratch_shapes=[
            pltpu.VMEM((slots, rows, 2 * head_dim), jnp.bfloat16),
            pltpu.VMEM(contact_tiles.shape, jnp.float32),
            pltpu.VMEM((slots, rows, rows), jnp.float32),
            pltpu.VMEM((rows, tile), jnp.float32),
            pltpu.VMEM((rows, tile), jnp.float32),
            pltpu.VMEM((rows, head_dim), jnp.float32),
            pltpu.SemaphoreType.DMA((slots,)),
        ],
        compiler_params=pltpu.CompilerParams(vmem_limit_bytes=60 << 20),
        name="attend",
    )(tile_codes, place, queries, everything, contact_tiles, valid_rows)


def per_device(
    activations,
    dilated_tap_weight,
    conv_mix,
    w_query,
    w_keyval,
    contact_tiles,
    tile_codes,
    bin_valid,
):
    seq_size = lax.axis_size("seq")
    position = lax.axis_index("seq")
    halo = halo_rows(activations)
    *lifted, table = lift(
        activations, dilated_tap_weight, conv_mix, w_query, w_keyval, contact_tiles
    )
    queries, keyval = front(lifted, halo, tile_codes)
    if seq_size == 16 and seq_size * activations.shape[0] == 2 * HALF:
        return attend_split(queries, keyval, table, tile_codes, bin_valid, seq_size)
    queries = queries[: activations.shape[0]]
    everything = lax.all_gather(keyval, "seq", axis=0, tiled=True)
    return attend(queries, everything, contact_tiles, tile_codes, bin_valid, position, seq_size)


def solution(mesh):
    in_specs = (P(("grp", "seq"), None), P(), P(), P(), P(), P(), P(("grp", "seq"), None), P("grp"))
    out_specs = P(("grp", "seq"), None)
    return jax.shard_map(
        per_device, mesh=mesh, in_specs=in_specs, out_specs=out_specs, check_vma=False
    )
```

```python
import functools
import math

import jax
import jax.numpy as jnp
from jax import lax
from jax.experimental import pallas as pl
from jax.experimental.pallas import tpu as pltpu
from jax.sharding import PartitionSpec as P


HDIM = 128
CONV_DILATION = 8
HALF = 4096


masked_score = -1e30
norm_eps = 1e-06
LOG2E = 1.4426950408889634


def halo_rows(activations):
    size = lax.axis_size("seq")
    odd = lax.axis_index("seq") % 2 == 1
    rows = activations.shape[0]
    initial = lax.slice_in_dim(activations, 0, CONV_DILATION, axis=0)
    last = lax.slice_in_dim(activations, rows - CONV_DILATION, rows, axis=0)
    inner = [(i, i ^ 1) for i in range(size)]
    outer = [(i, i + 1) for i in range(1, size - 1, 2)] + [(i + 1, i) for i in range(1, size - 1, 2)]
    from_inner = lax.ppermute(jnp.where(odd, initial, last), "seq", inner)
    from_outer = lax.ppermute(jnp.where(odd, last, initial), "seq", outer)
    return from_inner, from_outer


def gelu(v):
    return 0.5 * v * (1.0 + lax.erf(v * math.sqrt(0.5)))


def lift_kernel(x_hbm, taps_hbm, mix_hbm, wq_hbm, wkv_hbm, tiles_hbm, *refs):
    x_ref, taps, mix, wq, wkv, inner, outer, table, tiles, sems = refs
    copies = [
        pltpu.make_async_copy(source, target, sems.at[i])
        for i, (source, target) in enumerate(
            [
                (x_hbm, x_ref),
                (tiles_hbm, tiles),
                (taps_hbm, taps),
                (mix_hbm, mix),
                (wq_hbm, wq),
                (wkv_hbm, wkv),
            ]
        )
    ]
    for copy in copies:
        copy.start()
    rows, channels = x_ref.shape
    step = 32
    d = CONV_DILATION
    copies[0].wait()

    def lift(i, tail):
        r = pl.multiple_of(i * step, step)
        g = gelu(x_ref[pl.ds(r, step), :].astype(jnp.float32))
        inner[pl.ds(r, step), :] = g.astype(jnp.bfloat16)
        outer[pl.ds(r, step), :] = jnp.concatenate([tail, g[: step - d]], axis=0).astype(
            jnp.bfloat16
        )
        return g[step - d :]

    edge = jnp.zeros((d, channels), jnp.float32)
    tail = lax.fori_loop(0, rows // step, lift, edge)
    outer[rows : rows + 2 * d, :] = jnp.concatenate([tail, edge], axis=0).astype(jnp.bfloat16)
    copies[1].wait()
    table[...] = tiles[...].astype(jnp.float32) * LOG2E
    for copy in copies[2:]:
        copy.wait()


def lift(activations, dilated_tap_weight, conv_mix, w_query, w_keyval, contact_tiles):
    rows, channels = activations.shape
    moved = [
        pltpu.with_memory_space_constraint(a, pltpu.HBM)
        for a in (activations, dilated_tap_weight, conv_mix, w_query, w_keyval)
    ]
    contact_tiles = pltpu.with_memory_space_constraint(contact_tiles, pltpu.HBM)
    vmem = pl.BlockSpec(memory_space=pltpu.VMEM)
    return pl.pallas_call(
        lift_kernel,
        out_shape=[jax.ShapeDtypeStruct(a.shape, a.dtype) for a in moved]
        + [
            jax.ShapeDtypeStruct((rows, channels), jnp.bfloat16),
            jax.ShapeDtypeStruct((rows + 2 * CONV_DILATION, channels), jnp.bfloat16),
            jax.ShapeDtypeStruct(contact_tiles.shape, jnp.float32),
        ],
        in_specs=[pl.BlockSpec(memory_space=pltpu.HBM)] * 6,
        out_specs=[vmem] * 8,
        scratch_shapes=[
            pltpu.VMEM(contact_tiles.shape, contact_tiles.dtype),
            pltpu.SemaphoreType.DMA((6,)),
        ],
        compiler_params=pltpu.CompilerParams(vmem_limit_bytes=24 << 20),
        name="lift",
    )(*moved, contact_tiles)


def front_kernel(
    x_ref,
    taps,
    mix,
    wq,
    wkv,
    inner,
    outer_ref,
    twin_ref,
    outside_ref,
    codes_ref,
    q_ref,
    kv_ref,
    outer,
    squeezed,
    mixed,
):
    rows, channels = x_ref.shape
    hidden = squeezed.shape[1]
    d = CONV_DILATION
    odd = lax.axis_index("seq") % 2 == 1
    beside = gelu(twin_ref[...].astype(jnp.float32))
    beyond = gelu(outside_ref[...].astype(jnp.float32))
    before = jnp.where(odd, beside, beyond)
    after = jnp.where(odd, beyond, beside)
    outer[...] = outer_ref[...]
    initial = outer_ref[0 : 2 * d, :].astype(jnp.float32)[d:]
    last = outer_ref[rows : rows + 2 * d, :].astype(jnp.float32)[:d]
    outer[0 : 2 * d, :] = jnp.concatenate([before, initial], axis=0).astype(jnp.bfloat16)
    outer[rows : rows + 2 * d, :] = jnp.concatenate([last, after], axis=0).astype(jnp.bfloat16)

    wide = 256
    for n in range(hidden // wide):
        cols = slice(n * wide, (n + 1) * wide)
        conv = jnp.dot(outer[0:rows, :], taps[0, :, cols], preferred_element_type=jnp.float32)
        conv += jnp.dot(inner[...], taps[1, :, cols], preferred_element_type=jnp.float32)
        conv += jnp.dot(
            outer[2 * d : rows + 2 * d, :], taps[2, :, cols], preferred_element_type=jnp.float32
        )
        squeezed[:, cols] = gelu(conv).astype(jnp.bfloat16)

    square = jnp.zeros((rows, 128), jnp.float32)
    for n in range(channels // wide):
        cols = slice(n * wide, (n + 1) * wide)
        part = x_ref[:, cols].astype(jnp.float32) + jnp.dot(
            squeezed[...], mix[:, cols], preferred_element_type=jnp.float32
        )
        mixed[:, cols] = part
        for k in range(wide // 128):
            piece = part[:, k * 128 : (k + 1) * 128]
            square += piece * piece
    gain = lax.rsqrt(jnp.sum(square, axis=1, keepdims=True) / channels + norm_eps)
    normed = (mixed[...] * gain).astype(jnp.bfloat16)
    q_ref[0:rows, :] = jnp.dot(normed, wq[...], preferred_element_type=jnp.float32).astype(
        jnp.bfloat16
    )
    q_ref[rows:, :] = jnp.zeros((q_ref.shape[0] - rows, q_ref.shape[1]), jnp.bfloat16)
    q_ref[rows : rows + codes_ref.shape[0], 0 : codes_ref.shape[1]] = (
        codes_ref[...].astype(jnp.float32).astype(jnp.bfloat16)
    )
    kv_ref[...] = jnp.dot(normed, wkv[...], preferred_element_type=jnp.float32).astype(jnp.bfloat16)


CODE_ROWS = 16


def front(lifted, halo, tile_codes):
    activations, _, conv_mix, w_query, w_keyval, _, outer = lifted
    rows, channels = activations.shape
    vmem = pl.BlockSpec(memory_space=pltpu.VMEM)
    bf16 = jnp.bfloat16
    return pl.pallas_call(
        front_kernel,
        out_shape=[
            jax.ShapeDtypeStruct((rows + CODE_ROWS, w_query.shape[1]), bf16),
            jax.ShapeDtypeStruct((rows, w_keyval.shape[1]), bf16),
        ],
        in_specs=[vmem] * 10,
        out_specs=[vmem, vmem],
        scratch_shapes=[
            pltpu.VMEM(outer.shape, bf16),
            pltpu.VMEM((rows, conv_mix.shape[0]), bf16),
            pltpu.VMEM((rows, channels), jnp.float32),
        ],
        compiler_params=pltpu.CompilerParams(vmem_limit_bytes=24 << 20),
        name="front",
    )(*lifted, *halo, tile_codes)


def attend_kernel(
    reach,
    codes_ref,
    place_ref,
    q_ref,
    kv_ref,
    tiles_ref,
    valid_ref,
    out_ref,
    kv_buf,
    bias_buf,
    scores,
    peak,
    total,
    acc,
    sems,
):
    rows, head_dim = q_ref.shape
    _, tile, _ = tiles_ref.shape
    tiles_per_block = rows // tile
    position = place_ref[0]
    first = place_ref[1]
    count = place_ref[2]
    factor = LOG2E / math.sqrt(head_dim)

    def fetch(i):
        return pltpu.make_async_copy(
            kv_ref.at[pl.ds((first + i) * rows, rows), :], kv_buf.at[i], sems.at[i]
        )

    @pl.loop(0, count)
    def _(i):
        fetch(i).start()

    bias_buf[...] = tiles_ref[...].astype(jnp.float32) * LOG2E
    peak[...] = jnp.full_like(peak, masked_score)

    @pl.loop(0, count)
    def _(i):
        fetch(i).wait()
        block = first + i
        keys = kv_buf[i, :, :head_dim]
        raw = lax.dot_general(
            q_ref[...], keys, (((1,), (1,)), ((), ())), preferred_element_type=jnp.float32
        )
        invalid = jnp.where(valid_ref[block] == 1, 0.0, masked_score)
        shift = block - position

        def tile_scores(qt, kt):
            offset = jnp.clip(shift * tiles_per_block + kt - qt + HALF // tile, 0, 2 * (HALF // tile))
            part = raw[qt * tile : (qt + 1) * tile, kt * tile : (kt + 1) * tile]
            return part * factor + bias_buf[codes_ref[qt, offset]]

        def keep(qt, columns):
            peak_now = peak[qt * tile : (qt + 1) * tile, :]
            for kt, column in enumerate(columns):
                scores[i, qt * tile : (qt + 1) * tile, kt * tile : (kt + 1) * tile] = column
                peak_now = jnp.maximum(peak_now, column)
            peak[qt * tile : (qt + 1) * tile, :] = peak_now

        plain = (shift != 0) & (jnp.abs(shift) < reach)

        @pl.when(plain)
        def _():
            for qt in range(tiles_per_block):
                keep(
                    qt,
                    [
                        tile_scores(qt, kt) + invalid[:, kt * tile : (kt + 1) * tile]
                        for kt in range(tiles_per_block)
                    ],
                )

        @pl.when(jnp.logical_not(plain))
        def _():
            lag = lax.broadcasted_iota(jnp.int32, (tile, tile), 1) - lax.broadcasted_iota(
                jnp.int32, (tile, tile), 0
            )
            for qt in range(tiles_per_block):
                columns = []
                for kt in range(tiles_per_block):
                    apart = lag + (shift * rows + (kt - qt) * tile)
                    dropped = jnp.where(
                        apart == 0, 0.0, invalid[:, kt * tile : (kt + 1) * tile]
                    )
                    dropped = jnp.where(jnp.abs(apart) <= HALF, dropped, masked_score)
                    columns.append(tile_scores(qt, kt) + dropped)
                keep(qt, columns)

    peak[...] = jnp.broadcast_to(jnp.max(peak[...], axis=1, keepdims=True), peak.shape)
    total[...] = jnp.zeros_like(total)
    acc[...] = jnp.zeros_like(acc)

    @pl.loop(0, count)
    def _(i):
        parts = []
        sums = total[...]
        for kt in range(tiles_per_block):
            probs = jnp.exp2(scores[i, :, kt * tile : (kt + 1) * tile] - peak[...])
            sums = sums + probs
            parts.append(probs.astype(jnp.bfloat16))
        total[...] = sums
        acc[...] += jnp.dot(
            jnp.concatenate(parts, axis=1),
            kv_buf[i, :, head_dim:],
            preferred_element_type=jnp.float32,
        )

    out_ref[...] = (acc[...] / jnp.sum(total[...], axis=1, keepdims=True)).astype(out_ref.dtype)


def block_scores(shift, edge, raw, invalid, table, codes_ref, half, qt, tile):
    factor = LOG2E / math.sqrt(HDIM)
    count = raw.shape[1] // tile
    columns = []
    if edge:
        lag = lax.broadcasted_iota(jnp.int32, (tile, tile), 1) - lax.broadcasted_iota(
            jnp.int32, (tile, tile), 0
        )
    for kt in range(count):
        span = slice(kt * tile, (kt + 1) * tile)
        offset = jnp.clip(shift * count + kt - qt + HALF // tile, 0, 2 * (HALF // tile))
        dropped = invalid[:, span]
        if edge:
            apart = lag + (shift * (tile * count) + (kt - qt) * tile)
            dropped = jnp.where(apart == 0, 0.0, dropped)
            dropped = jnp.where(jnp.abs(apart) <= HALF, dropped, masked_score)
        part = raw[qt * tile : (qt + 1) * tile, span]
        columns.append((part * factor + table[codes_ref[half + qt, offset]]) + dropped)
    return columns


def absorb_kernel(reach, flips, blocks, begin, pack, codes_ref, *refs):
    sets, n = len(flips), len(blocks)
    q_refs, refs = refs[:sets], refs[sets:]
    kv_refs, refs = refs[:n], refs[n:]
    table, valid_ref = refs[:2]
    refs = refs[2:]
    if not begin:
        state_refs, refs = refs[: 3 * sets], refs[3 * sets :]
    outs = 1 if pack else 3 * sets
    out_refs, refs = refs[:outs], refs[outs:]
    scores, peak, total, acc = refs
    rows, head_dim = acc.shape
    tile = table.shape[1]
    tiles_per_block = rows // tile
    position = lax.axis_index("seq")

    for s, flip in enumerate(flips):
        owner = position ^ flip
        q_ref = q_refs[s]
        half = 0 if flip == 0 else tiles_per_block
        if begin:
            peak[...] = jnp.full_like(peak, masked_score)
        else:
            peak[...] = state_refs[3 * s][...]

        def each(step):
            for j, block in enumerate(blocks):
                shift = (position ^ block) - owner
                run = functools.partial(step, j, shift, (block ^ flip) in (0, reach))
                if block ^ flip < reach:
                    run()
                else:
                    pl.when(jnp.abs(shift) <= reach)(run)

        def score(j, shift, edge):
            raw = lax.dot_general(
                q_ref[0:rows, :],
                kv_refs[j][:, :head_dim],
                (((1,), (1,)), ((), ())),
                preferred_element_type=jnp.float32,
            )
            invalid = jnp.where(valid_ref[owner + shift] == 1, 0.0, masked_score)
            for qt in range(tiles_per_block):
                span = slice(qt * tile, (qt + 1) * tile)
                peak_now = peak[span, :]
                columns = block_scores(
                    shift, edge, raw, invalid, table, codes_ref, half, qt, tile
                )
                for kt, column in enumerate(columns):
                    scores[j, span, kt * tile : (kt + 1) * tile] = column
                    peak_now = jnp.maximum(peak_now, column)
                peak[span, :] = peak_now

        def weigh(j, shift, edge):
            parts = []
            sums = total[...]
            for kt in range(tiles_per_block):
                probs = jnp.exp2(scores[j, :, kt * tile : (kt + 1) * tile] - peak[...])
                sums = sums + probs
                parts.append(probs.astype(jnp.bfloat16))
            total[...] = sums
            acc[...] += jnp.dot(
                jnp.concatenate(parts, axis=1),
                kv_refs[j][:, head_dim:],
                preferred_element_type=jnp.float32,
            )

        each(score)
        peak[...] = jnp.broadcast_to(jnp.max(peak[...], axis=1, keepdims=True), peak.shape)
        if begin:
            total[...] = jnp.zeros_like(total)
            acc[...] = jnp.zeros_like(acc)
        else:
            rescale = jnp.exp2(state_refs[3 * s][...] - peak[...])
            total[...] = state_refs[3 * s + 1][...] * rescale
            acc[...] = state_refs[3 * s + 2][...] * rescale
        each(weigh)

        if pack:
            out_refs[0][0:rows, :] = acc[...].astype(jnp.bfloat16)
            sums = jnp.broadcast_to(jnp.sum(total[...], axis=1, keepdims=True), total.shape)
            eye = on_diagonal(tile)
            lines = []
            for column in (peak[...], sums):
                for qt in range(tiles_per_block):
                    part = column[qt * tile : (qt + 1) * tile, :]
                    lines.append(jnp.sum(jnp.where(eye, part, 0.0), axis=0, keepdims=True))
            exact = jnp.concatenate(lines, axis=0)
            pieces = []
            for _ in range(3):
                piece = exact.astype(jnp.bfloat16).astype(jnp.float32)
                exact = exact - piece
                pieces.append(piece)
            pieces.append(jnp.zeros_like(exact))
            out_refs[0][rows:, :] = jnp.concatenate(pieces, axis=0).astype(jnp.bfloat16)
        else:
            out_refs[3 * s][...] = peak[...]
            out_refs[3 * s + 1][...] = total[...]
            out_refs[3 * s + 2][...] = acc[...]


def on_diagonal(tile):
    return lax.broadcasted_iota(jnp.int32, (tile, tile), 0) == lax.broadcasted_iota(
        jnp.int32, (tile, tile), 1
    )


def absorb(reach, codes, queries, keyvals, table, valid_rows, flips, blocks, state, pack):
    rows = keyvals[0].shape[0]
    head_dim = queries[0].shape[1]
    tile = table.shape[1]
    n = len(blocks)
    vmem = pl.BlockSpec(memory_space=pltpu.VMEM)
    smem = pl.BlockSpec(memory_space=pltpu.SMEM)
    column = jax.ShapeDtypeStruct((rows, tile), jnp.float32)
    if pack:
        out_shape = [jax.ShapeDtypeStruct((rows + 8 * (rows // tile), head_dim), jnp.bfloat16)]
    else:
        out_shape = [column, column, column] * len(flips)
    units = len(flips) * n
    return pl.pallas_call(
        functools.partial(absorb_kernel, reach, flips, blocks, not state, pack),
        out_shape=out_shape,
        in_specs=[smem] + [vmem] * (len(flips) + n + 2 + len(state)),
        out_specs=[vmem] * len(out_shape),
        scratch_shapes=[
            pltpu.VMEM((n, rows, rows), jnp.float32),
            pltpu.VMEM((rows, tile), jnp.float32),
            pltpu.VMEM((rows, tile), jnp.float32),
            pltpu.VMEM((rows, head_dim), jnp.float32),
        ],
        compiler_params=pltpu.CompilerParams(vmem_limit_bytes=24 << 20),
        cost_estimate=pl.CostEstimate(
            flops=units * 4 * rows * rows * head_dim,
            bytes_accessed=units * 4 * rows * rows,
            transcendentals=units * rows * rows,
        ),
    )(codes, *queries, *keyvals, table, valid_rows, *state)


def merge_kernel(peak_ref, total_ref, acc_ref, pack_ref, out_ref):
    rows, _ = acc_ref.shape
    tile = peak_ref.shape[1]
    eye = on_diagonal(tile)
    count = rows // tile
    pieces = pack_ref[rows:, :].astype(jnp.float32)
    lines = 2 * count
    exact = pieces[:lines] + pieces[lines : 2 * lines] + pieces[2 * lines : 3 * lines]
    for qt in range(count):
        span = slice(qt * tile, (qt + 1) * tile)

        def column(line):
            row = exact[line : line + 1, :]
            return jnp.sum(jnp.where(eye, row, 0.0), axis=1, keepdims=True)

        peak_a = peak_ref[span, :]
        peak_b = column(qt)
        total_a = jnp.sum(total_ref[span, :], axis=1, keepdims=True)
        total_b = column(count + qt)
        top = jnp.maximum(peak_a, peak_b)
        scale_a = jnp.exp2(peak_a - top)
        scale_b = jnp.exp2(peak_b - top)
        whole = total_a * scale_a + total_b * scale_b
        out_ref[span, :] = (
            (acc_ref[span, :] * scale_a + pack_ref[span, :].astype(jnp.float32) * scale_b) / whole
        ).astype(out_ref.dtype)


def attend_split(queries, keyval, table, tile_codes, bin_valid, seq_size):
    rows = keyval.shape[0]
    reach = HALF // rows
    z = seq_size // 4
    half = z // 2
    valid_rows = bin_valid.reshape(seq_size, 1, rows)

    def trade(x, flip, some=None):
        pairs = [(i, i ^ flip) for i in range(seq_size) if some is None or some(i // z)]
        return lax.ppermute(x, "seq", pairs)

    peer_queries = trade(queries, half)
    far = trade(keyval, 2 * z)
    middle = trade(keyval, 3 * z, lambda level: level in (1, 2))
    near = trade(keyval, z)
    twin = trade(keyval, 1)
    peer_codes = peer_queries[rows : rows + tile_codes.shape[0], : tile_codes.shape[1]]
    codes = jnp.concatenate([tile_codes, peer_codes.astype(jnp.int32)], axis=0)
    common = (table, valid_rows)
    state = absorb(
        reach, codes, [queries, peer_queries], [keyval, twin], *common, (0, half), (0, 1), [], False
    )
    near, middle, state = lax.optimization_barrier((near, middle, state))
    near_twin = trade(near, 1)
    middle_twin = trade(middle, 1)
    state = absorb(
        reach,
        codes,
        [queries, peer_queries],
        [near, near_twin, middle, middle_twin],
        *common,
        (0, half),
        (z, z + 1, 3 * z, 3 * z + 1),
        state,
        False,
    )
    far, state = lax.optimization_barrier((far, state))
    far_twin = trade(far, 1)
    away = [far, far_twin]
    leaps = (2 * z, 2 * z + 1)
    (pack,) = absorb(reach, codes, [peer_queries], away, *common, (half,), leaps, state[3:], True)
    other = trade(pack, half)
    peak, total, acc = absorb(reach, codes, [queries], away, *common, (0,), leaps, state[:3], False)
    vmem = pl.BlockSpec(memory_space=pltpu.VMEM)
    return pl.pallas_call(
        merge_kernel,
        out_shape=jax.ShapeDtypeStruct((rows, queries.shape[1]), jnp.bfloat16),
        in_specs=[vmem] * 4,
        out_specs=vmem,
        compiler_params=pltpu.CompilerParams(vmem_limit_bytes=8 << 20),
        name="merge",
    )(peak, total, acc, other)


def attend(queries, everything, contact_tiles, tile_codes, bin_valid, position, seq_size):
    rows, head_dim = queries.shape
    reach = HALF // rows
    tile = contact_tiles.shape[1]
    slots = min(seq_size, 2 * reach + 1)
    first = jnp.maximum(position - reach, 0)
    last = jnp.minimum(position + reach, seq_size - 1)
    place = jnp.stack([position, first, last - first + 1]).astype(jnp.int32)
    valid_rows = bin_valid.reshape(seq_size, 1, rows)
    vmem = pl.BlockSpec(memory_space=pltpu.VMEM)
    smem = pl.BlockSpec(memory_space=pltpu.SMEM)
    return pl.pallas_call(
        functools.partial(attend_kernel, reach),
        out_shape=jax.ShapeDtypeStruct((rows, head_dim), jnp.bfloat16),
        in_specs=[smem, smem, vmem, pl.BlockSpec(memory_space=pl.ANY), vmem, vmem],
        out_specs=vmem,
        scratch_shapes=[
            pltpu.VMEM((slots, rows, 2 * head_dim), jnp.bfloat16),
            pltpu.VMEM(contact_tiles.shape, jnp.float32),
            pltpu.VMEM((slots, rows, rows), jnp.float32),
            pltpu.VMEM((rows, tile), jnp.float32),
            pltpu.VMEM((rows, tile), jnp.float32),
            pltpu.VMEM((rows, head_dim), jnp.float32),
            pltpu.SemaphoreType.DMA((slots,)),
        ],
        compiler_params=pltpu.CompilerParams(vmem_limit_bytes=60 << 20),
        name="attend",
    )(tile_codes, place, queries, everything, contact_tiles, valid_rows)


def per_device(
    activations,
    dilated_tap_weight,
    conv_mix,
    w_query,
    w_keyval,
    contact_tiles,
    tile_codes,
    bin_valid,
):
    seq_size = lax.axis_size("seq")
    position = lax.axis_index("seq")
    halo = halo_rows(activations)
    *lifted, table = lift(
        activations, dilated_tap_weight, conv_mix, w_query, w_keyval, contact_tiles
    )
    queries, keyval = front(lifted, halo, tile_codes)
    if seq_size == 16 and seq_size * activations.shape[0] == 2 * HALF:
        return attend_split(queries, keyval, table, tile_codes, bin_valid, seq_size)
    queries = queries[: activations.shape[0]]
    everything = lax.all_gather(keyval, "seq", axis=0, tiled=True)
    return attend(queries, everything, contact_tiles, tile_codes, bin_valid, position, seq_size)


def solution(mesh):
    in_specs = (P(("grp", "seq"), None), P(), P(), P(), P(), P(), P(("grp", "seq"), None), P("grp"))
    out_specs = P(("grp", "seq"), None)
    return jax.shard_map(
        per_device, mesh=mesh, in_specs=in_specs, out_specs=out_specs, check_vma=False
    )
```

```python
import functools
import math

import jax
import jax.numpy as jnp
from jax import lax
from jax.experimental import pallas as pl
from jax.experimental.pallas import tpu as pltpu
from jax.sharding import PartitionSpec as P


HDIM = 128
CONV_DILATION = 8
HALF = 4096


masked_score = -1e30
norm_eps = 1e-06
LOG2E = 1.4426950408889634


def halo_rows(activations):
    size = lax.axis_size("seq")
    odd = lax.axis_index("seq") % 2 == 1
    rows = activations.shape[0]
    initial = lax.slice_in_dim(activations, 0, CONV_DILATION, axis=0)
    last = lax.slice_in_dim(activations, rows - CONV_DILATION, rows, axis=0)
    inner = [(i, i ^ 1) for i in range(size)]
    outer = [(i, i + 1) for i in range(1, size - 1, 2)] + [(i + 1, i) for i in range(1, size - 1, 2)]
    from_inner = lax.ppermute(jnp.where(odd, initial, last), "seq", inner)
    from_outer = lax.ppermute(jnp.where(odd, last, initial), "seq", outer)
    return from_inner, from_outer


def gelu(v):
    return 0.5 * v * (1.0 + lax.erf(v * math.sqrt(0.5)))


def lift_kernel(x_hbm, taps_hbm, mix_hbm, wq_hbm, wkv_hbm, tiles_hbm, *refs):
    x_ref, taps, mix, wq, wkv, inner, outer, table, tiles, sems = refs
    copies = [
        pltpu.make_async_copy(source, target, sems.at[i])
        for i, (source, target) in enumerate(
            [
                (x_hbm, x_ref),
                (tiles_hbm, tiles),
                (taps_hbm, taps),
                (mix_hbm, mix),
                (wq_hbm, wq),
                (wkv_hbm, wkv),
            ]
        )
    ]
    for copy in copies:
        copy.start()
    rows, channels = x_ref.shape
    step = 32
    d = CONV_DILATION
    copies[0].wait()

    def lift(i, tail):
        r = pl.multiple_of(i * step, step)
        g = gelu(x_ref[pl.ds(r, step), :].astype(jnp.float32))
        inner[pl.ds(r, step), :] = g.astype(jnp.bfloat16)
        outer[pl.ds(r, step), :] = jnp.concatenate([tail, g[: step - d]], axis=0).astype(
            jnp.bfloat16
        )
        return g[step - d :]

    edge = jnp.zeros((d, channels), jnp.float32)
    tail = lax.fori_loop(0, rows // step, lift, edge)
    outer[rows : rows + 2 * d, :] = jnp.concatenate([tail, edge], axis=0).astype(jnp.bfloat16)
    copies[1].wait()
    table[...] = tiles[...].astype(jnp.float32) * LOG2E
    for copy in copies[2:]:
        copy.wait()


def lift(activations, dilated_tap_weight, conv_mix, w_query, w_keyval, contact_tiles):
    rows, channels = activations.shape
    moved = [
        pltpu.with_memory_space_constraint(a, pltpu.HBM)
        for a in (activations, dilated_tap_weight, conv_mix, w_query, w_keyval)
    ]
    contact_tiles = pltpu.with_memory_space_constraint(contact_tiles, pltpu.HBM)
    vmem = pl.BlockSpec(memory_space=pltpu.VMEM)
    return pl.pallas_call(
        lift_kernel,
        out_shape=[jax.ShapeDtypeStruct(a.shape, a.dtype) for a in moved]
        + [
            jax.ShapeDtypeStruct((rows, channels), jnp.bfloat16),
            jax.ShapeDtypeStruct((rows + 2 * CONV_DILATION, channels), jnp.bfloat16),
            jax.ShapeDtypeStruct(contact_tiles.shape, jnp.float32),
        ],
        in_specs=[pl.BlockSpec(memory_space=pltpu.HBM)] * 6,
        out_specs=[vmem] * 8,
        scratch_shapes=[
            pltpu.VMEM(contact_tiles.shape, contact_tiles.dtype),
            pltpu.SemaphoreType.DMA((6,)),
        ],
        compiler_params=pltpu.CompilerParams(vmem_limit_bytes=24 << 20),
        name="lift",
    )(*moved, contact_tiles)


def front_kernel(
    x_ref,
    taps,
    mix,
    wq,
    wkv,
    inner,
    outer_ref,
    twin_ref,
    outside_ref,
    codes_ref,
    q_ref,
    kv_ref,
    outer,
    squeezed,
    mixed,
):
    rows, channels = x_ref.shape
    hidden = squeezed.shape[1]
    d = CONV_DILATION
    odd = lax.axis_index("seq") % 2 == 1
    beside = gelu(twin_ref[...].astype(jnp.float32))
    beyond = gelu(outside_ref[...].astype(jnp.float32))
    before = jnp.where(odd, beside, beyond)
    after = jnp.where(odd, beyond, beside)
    outer[...] = outer_ref[...]
    initial = outer_ref[0 : 2 * d, :].astype(jnp.float32)[d:]
    last = outer_ref[rows : rows + 2 * d, :].astype(jnp.float32)[:d]
    outer[0 : 2 * d, :] = jnp.concatenate([before, initial], axis=0).astype(jnp.bfloat16)
    outer[rows : rows + 2 * d, :] = jnp.concatenate([last, after], axis=0).astype(jnp.bfloat16)

    wide = 256
    taps_rows, mix_rows, out_rows = rows // 2, rows // 1, rows // 1
    for n in range(hidden // wide):
        cols = slice(n * wide, (n + 1) * wide)
        for r in range(0, rows, taps_rows):
            conv = jnp.dot(
                outer[r : r + taps_rows, :], taps[0, :, cols], preferred_element_type=jnp.float32
            )
            conv += jnp.dot(
                inner[r : r + taps_rows, :], taps[1, :, cols], preferred_element_type=jnp.float32
            )
            conv += jnp.dot(
                outer[r + 2 * d : r + 2 * d + taps_rows, :],
                taps[2, :, cols],
                preferred_element_type=jnp.float32,
            )
            squeezed[r : r + taps_rows, cols] = gelu(conv).astype(jnp.bfloat16)

    squares = [jnp.zeros((mix_rows, 128), jnp.float32) for _ in range(rows // mix_rows)]
    for n in range(channels // wide):
        cols = slice(n * wide, (n + 1) * wide)
        for i in range(rows // mix_rows):
            span = slice(i * mix_rows, (i + 1) * mix_rows)
            part = x_ref[span, cols].astype(jnp.float32) + jnp.dot(
                squeezed[span, :], mix[:, cols], preferred_element_type=jnp.float32
            )
            mixed[span, cols] = part
            for k in range(wide // 128):
                piece = part[:, k * 128 : (k + 1) * 128]
                squares[i] += piece * piece
    gain = lax.rsqrt(
        jnp.sum(jnp.concatenate(squares, axis=0), axis=1, keepdims=True) / channels + norm_eps
    )
    for r in range(0, rows, out_rows):
        span = slice(r, r + out_rows)
        normed = (mixed[span, :] * gain[span]).astype(jnp.bfloat16)
        q_ref[span, :] = jnp.dot(normed, wq[...], preferred_element_type=jnp.float32).astype(
            jnp.bfloat16
        )
        kv_ref[span, :] = jnp.dot(normed, wkv[...], preferred_element_type=jnp.float32).astype(
            jnp.bfloat16
        )
    q_ref[rows:, :] = jnp.zeros((q_ref.shape[0] - rows, q_ref.shape[1]), jnp.bfloat16)
    q_ref[rows : rows + codes_ref.shape[0], 0 : codes_ref.shape[1]] = (
        codes_ref[...].astype(jnp.float32).astype(jnp.bfloat16)
    )


CODE_ROWS = 16


def front(lifted, halo, tile_codes):
    activations, _, conv_mix, w_query, w_keyval, _, outer = lifted
    rows, channels = activations.shape
    vmem = pl.BlockSpec(memory_space=pltpu.VMEM)
    bf16 = jnp.bfloat16
    return pl.pallas_call(
        front_kernel,
        out_shape=[
            jax.ShapeDtypeStruct((rows + CODE_ROWS, w_query.shape[1]), bf16),
            jax.ShapeDtypeStruct((rows, w_keyval.shape[1]), bf16),
        ],
        in_specs=[vmem] * 10,
        out_specs=[vmem, vmem],
        scratch_shapes=[
            pltpu.VMEM(outer.shape, bf16),
            pltpu.VMEM((rows, conv_mix.shape[0]), bf16),
            pltpu.VMEM((rows, channels), jnp.float32),
        ],
        compiler_params=pltpu.CompilerParams(vmem_limit_bytes=24 << 20),
        name="front",
    )(*lifted, *halo, tile_codes)


def attend_kernel(
    reach,
    codes_ref,
    place_ref,
    q_ref,
    kv_ref,
    tiles_ref,
    valid_ref,
    out_ref,
    kv_buf,
    bias_buf,
    scores,
    peak,
    total,
    acc,
    sems,
):
    rows, head_dim = q_ref.shape
    _, tile, _ = tiles_ref.shape
    tiles_per_block = rows // tile
    position = place_ref[0]
    first = place_ref[1]
    count = place_ref[2]
    factor = LOG2E / math.sqrt(head_dim)

    def fetch(i):
        return pltpu.make_async_copy(
            kv_ref.at[pl.ds((first + i) * rows, rows), :], kv_buf.at[i], sems.at[i]
        )

    @pl.loop(0, count)
    def _(i):
        fetch(i).start()

    bias_buf[...] = tiles_ref[...].astype(jnp.float32) * LOG2E
    peak[...] = jnp.full_like(peak, masked_score)

    @pl.loop(0, count)
    def _(i):
        fetch(i).wait()
        block = first + i
        keys = kv_buf[i, :, :head_dim]
        raw = lax.dot_general(
            q_ref[...], keys, (((1,), (1,)), ((), ())), preferred_element_type=jnp.float32
        )
        invalid = jnp.where(valid_ref[block] == 1, 0.0, masked_score)
        shift = block - position

        def tile_scores(qt, kt):
            offset = jnp.clip(shift * tiles_per_block + kt - qt + HALF // tile, 0, 2 * (HALF // tile))
            part = raw[qt * tile : (qt + 1) * tile, kt * tile : (kt + 1) * tile]
            return part * factor + bias_buf[codes_ref[qt, offset]]

        def keep(qt, columns):
            peak_now = peak[qt * tile : (qt + 1) * tile, :]
            for kt, column in enumerate(columns):
                scores[i, qt * tile : (qt + 1) * tile, kt * tile : (kt + 1) * tile] = column
                peak_now = jnp.maximum(peak_now, column)
            peak[qt * tile : (qt + 1) * tile, :] = peak_now

        plain = (shift != 0) & (jnp.abs(shift) < reach)

        @pl.when(plain)
        def _():
            for qt in range(tiles_per_block):
                keep(
                    qt,
                    [
                        tile_scores(qt, kt) + invalid[:, kt * tile : (kt + 1) * tile]
                        for kt in range(tiles_per_block)
                    ],
                )

        @pl.when(jnp.logical_not(plain))
        def _():
            lag = lax.broadcasted_iota(jnp.int32, (tile, tile), 1) - lax.broadcasted_iota(
                jnp.int32, (tile, tile), 0
            )
            for qt in range(tiles_per_block):
                columns = []
                for kt in range(tiles_per_block):
                    apart = lag + (shift * rows + (kt - qt) * tile)
                    dropped = jnp.where(
                        apart == 0, 0.0, invalid[:, kt * tile : (kt + 1) * tile]
                    )
                    dropped = jnp.where(jnp.abs(apart) <= HALF, dropped, masked_score)
                    columns.append(tile_scores(qt, kt) + dropped)
                keep(qt, columns)

    peak[...] = jnp.broadcast_to(jnp.max(peak[...], axis=1, keepdims=True), peak.shape)
    total[...] = jnp.zeros_like(total)
    acc[...] = jnp.zeros_like(acc)

    @pl.loop(0, count)
    def _(i):
        parts = []
        sums = total[...]
        for kt in range(tiles_per_block):
            probs = jnp.exp2(scores[i, :, kt * tile : (kt + 1) * tile] - peak[...])
            sums = sums + probs
            parts.append(probs.astype(jnp.bfloat16))
        total[...] = sums
        acc[...] += jnp.dot(
            jnp.concatenate(parts, axis=1),
            kv_buf[i, :, head_dim:],
            preferred_element_type=jnp.float32,
        )

    out_ref[...] = (acc[...] / jnp.sum(total[...], axis=1, keepdims=True)).astype(out_ref.dtype)


def block_scores(shift, edge, raw, invalid, table, codes_ref, half, qt, tile):
    factor = LOG2E / math.sqrt(HDIM)
    count = raw.shape[1] // tile
    columns = []
    if edge:
        lag = lax.broadcasted_iota(jnp.int32, (tile, tile), 1) - lax.broadcasted_iota(
            jnp.int32, (tile, tile), 0
        )
    for kt in range(count):
        span = slice(kt * tile, (kt + 1) * tile)
        offset = jnp.clip(shift * count + kt - qt + HALF // tile, 0, 2 * (HALF // tile))
        dropped = invalid[:, span]
        if edge:
            apart = lag + (shift * (tile * count) + (kt - qt) * tile)
            dropped = jnp.where(apart == 0, 0.0, dropped)
            dropped = jnp.where(jnp.abs(apart) <= HALF, dropped, masked_score)
        part = raw[qt * tile : (qt + 1) * tile, span]
        columns.append((part * factor + table[codes_ref[half + qt, offset]]) + dropped)
    return columns


def absorb_kernel(reach, flips, blocks, begin, pack, codes_ref, *refs):
    sets, n = len(flips), len(blocks)
    q_refs, refs = refs[:sets], refs[sets:]
    kv_refs, refs = refs[:n], refs[n:]
    table, valid_ref = refs[:2]
    refs = refs[2:]
    if not begin:
        state_refs, refs = refs[: 3 * sets], refs[3 * sets :]
    outs = 1 if pack else 3 * sets
    out_refs, refs = refs[:outs], refs[outs:]
    scores, peak, total, acc = refs
    rows, head_dim = acc.shape
    tile = table.shape[1]
    tiles_per_block = rows // tile
    position = lax.axis_index("seq")

    for s, flip in enumerate(flips):
        owner = position ^ flip
        q_ref = q_refs[s]
        half = 0 if flip == 0 else tiles_per_block
        if begin:
            peak[...] = jnp.full_like(peak, masked_score)
        else:
            peak[...] = state_refs[3 * s][...]

        def each(step):
            for j, block in enumerate(blocks):
                shift = (position ^ block) - owner
                run = functools.partial(step, j, shift, (block ^ flip) in (0, reach))
                if block ^ flip < reach:
                    run()
                else:
                    pl.when(jnp.abs(shift) <= reach)(run)

        def score(j, shift, edge):
            raw = lax.dot_general(
                q_ref[0:rows, :],
                kv_refs[j][:, :head_dim],
                (((1,), (1,)), ((), ())),
                preferred_element_type=jnp.float32,
            )
            invalid = jnp.where(valid_ref[owner + shift] == 1, 0.0, masked_score)
            for qt in range(tiles_per_block):
                span = slice(qt * tile, (qt + 1) * tile)
                peak_now = peak[span, :]
                columns = block_scores(
                    shift, edge, raw, invalid, table, codes_ref, half, qt, tile
                )
                for kt, column in enumerate(columns):
                    scores[j, span, kt * tile : (kt + 1) * tile] = column
                    peak_now = jnp.maximum(peak_now, column)
                peak[span, :] = peak_now

        def weigh(j, shift, edge):
            parts = []
            sums = total[...]
            for kt in range(tiles_per_block):
                probs = jnp.exp2(scores[j, :, kt * tile : (kt + 1) * tile] - peak[...])
                sums = sums + probs
                parts.append(probs.astype(jnp.bfloat16))
            total[...] = sums
            acc[...] += jnp.dot(
                jnp.concatenate(parts, axis=1),
                kv_refs[j][:, head_dim:],
                preferred_element_type=jnp.float32,
            )

        each(score)
        peak[...] = jnp.broadcast_to(jnp.max(peak[...], axis=1, keepdims=True), peak.shape)
        if begin:
            total[...] = jnp.zeros_like(total)
            acc[...] = jnp.zeros_like(acc)
        else:
            rescale = jnp.exp2(state_refs[3 * s][...] - peak[...])
            total[...] = state_refs[3 * s + 1][...] * rescale
            acc[...] = state_refs[3 * s + 2][...] * rescale
        each(weigh)

        if pack:
            out_refs[0][0:rows, :] = acc[...].astype(jnp.bfloat16)
            sums = jnp.broadcast_to(jnp.sum(total[...], axis=1, keepdims=True), total.shape)
            eye = on_diagonal(tile)
            lines = []
            for column in (peak[...], sums):
                for qt in range(tiles_per_block):
                    part = column[qt * tile : (qt + 1) * tile, :]
                    lines.append(jnp.sum(jnp.where(eye, part, 0.0), axis=0, keepdims=True))
            exact = jnp.concatenate(lines, axis=0)
            pieces = []
            for _ in range(3):
                piece = exact.astype(jnp.bfloat16).astype(jnp.float32)
                exact = exact - piece
                pieces.append(piece)
            pieces.append(jnp.zeros_like(exact))
            out_refs[0][rows:, :] = jnp.concatenate(pieces, axis=0).astype(jnp.bfloat16)
        else:
            out_refs[3 * s][...] = peak[...]
            out_refs[3 * s + 1][...] = total[...]
            out_refs[3 * s + 2][...] = acc[...]


def on_diagonal(tile):
    return lax.broadcasted_iota(jnp.int32, (tile, tile), 0) == lax.broadcasted_iota(
        jnp.int32, (tile, tile), 1
    )


def absorb(reach, codes, queries, keyvals, table, valid_rows, flips, blocks, state, pack):
    rows = keyvals[0].shape[0]
    head_dim = queries[0].shape[1]
    tile = table.shape[1]
    n = len(blocks)
    vmem = pl.BlockSpec(memory_space=pltpu.VMEM)
    smem = pl.BlockSpec(memory_space=pltpu.SMEM)
    column = jax.ShapeDtypeStruct((rows, tile), jnp.float32)
    if pack:
        out_shape = [jax.ShapeDtypeStruct((rows + 8 * (rows // tile), head_dim), jnp.bfloat16)]
    else:
        out_shape = [column, column, column] * len(flips)
    units = len(flips) * n
    return pl.pallas_call(
        functools.partial(absorb_kernel, reach, flips, blocks, not state, pack),
        out_shape=out_shape,
        in_specs=[smem] + [vmem] * (len(flips) + n + 2 + len(state)),
        out_specs=[vmem] * len(out_shape),
        scratch_shapes=[
            pltpu.VMEM((n, rows, rows), jnp.float32),
            pltpu.VMEM((rows, tile), jnp.float32),
            pltpu.VMEM((rows, tile), jnp.float32),
            pltpu.VMEM((rows, head_dim), jnp.float32),
        ],
        compiler_params=pltpu.CompilerParams(vmem_limit_bytes=24 << 20),
        cost_estimate=pl.CostEstimate(
            flops=units * 4 * rows * rows * head_dim,
            bytes_accessed=units * 4 * rows * rows,
            transcendentals=units * rows * rows,
        ),
    )(codes, *queries, *keyvals, table, valid_rows, *state)


def merge_kernel(peak_ref, total_ref, acc_ref, pack_ref, out_ref):
    rows, _ = acc_ref.shape
    tile = peak_ref.shape[1]
    eye = on_diagonal(tile)
    count = rows // tile
    pieces = pack_ref[rows:, :].astype(jnp.float32)
    lines = 2 * count
    exact = pieces[:lines] + pieces[lines : 2 * lines] + pieces[2 * lines : 3 * lines]
    for qt in range(count):
        span = slice(qt * tile, (qt + 1) * tile)

        def column(line):
            row = exact[line : line + 1, :]
            return jnp.sum(jnp.where(eye, row, 0.0), axis=1, keepdims=True)

        peak_a = peak_ref[span, :]
        peak_b = column(qt)
        total_a = jnp.sum(total_ref[span, :], axis=1, keepdims=True)
        total_b = column(count + qt)
        top = jnp.maximum(peak_a, peak_b)
        scale_a = jnp.exp2(peak_a - top)
        scale_b = jnp.exp2(peak_b - top)
        whole = total_a * scale_a + total_b * scale_b
        out_ref[span, :] = (
            (acc_ref[span, :] * scale_a + pack_ref[span, :].astype(jnp.float32) * scale_b) / whole
        ).astype(out_ref.dtype)


def attend_split(queries, keyval, table, tile_codes, bin_valid, seq_size):
    rows = keyval.shape[0]
    reach = HALF // rows
    z = seq_size // 4
    half = z // 2
    valid_rows = bin_valid.reshape(seq_size, 1, rows)

    def trade(x, flip, some=None):
        pairs = [(i, i ^ flip) for i in range(seq_size) if some is None or some(i // z)]
        return lax.ppermute(x, "seq", pairs)

    peer_queries = trade(queries, half)
    far = trade(keyval, 2 * z)
    middle = trade(keyval, 3 * z, lambda level: level in (1, 2))
    near = trade(keyval, z)
    twin = trade(keyval, 1)
    peer_codes = peer_queries[rows : rows + tile_codes.shape[0], : tile_codes.shape[1]]
    codes = jnp.concatenate([tile_codes, peer_codes.astype(jnp.int32)], axis=0)
    common = (table, valid_rows)
    state = absorb(
        reach, codes, [queries, peer_queries], [keyval, twin], *common, (0, half), (0, 1), [], False
    )
    near, middle, state = lax.optimization_barrier((near, middle, state))
    near_twin = trade(near, 1)
    middle_twin = trade(middle, 1)
    state = absorb(
        reach,
        codes,
        [queries, peer_queries],
        [near, near_twin, middle, middle_twin],
        *common,
        (0, half),
        (z, z + 1, 3 * z, 3 * z + 1),
        state,
        False,
    )
    far, state = lax.optimization_barrier((far, state))
    far_twin = trade(far, 1)
    away = [far, far_twin]
    leaps = (2 * z, 2 * z + 1)
    (pack,) = absorb(reach, codes, [peer_queries], away, *common, (half,), leaps, state[3:], True)
    other = trade(pack, half)
    peak, total, acc = absorb(reach, codes, [queries], away, *common, (0,), leaps, state[:3], False)
    vmem = pl.BlockSpec(memory_space=pltpu.VMEM)
    return pl.pallas_call(
        merge_kernel,
        out_shape=jax.ShapeDtypeStruct((rows, queries.shape[1]), jnp.bfloat16),
        in_specs=[vmem] * 4,
        out_specs=vmem,
        compiler_params=pltpu.CompilerParams(vmem_limit_bytes=8 << 20),
        name="merge",
    )(peak, total, acc, other)


def attend(queries, everything, contact_tiles, tile_codes, bin_valid, position, seq_size):
    rows, head_dim = queries.shape
    reach = HALF // rows
    tile = contact_tiles.shape[1]
    slots = min(seq_size, 2 * reach + 1)
    first = jnp.maximum(position - reach, 0)
    last = jnp.minimum(position + reach, seq_size - 1)
    place = jnp.stack([position, first, last - first + 1]).astype(jnp.int32)
    valid_rows = bin_valid.reshape(seq_size, 1, rows)
    vmem = pl.BlockSpec(memory_space=pltpu.VMEM)
    smem = pl.BlockSpec(memory_space=pltpu.SMEM)
    return pl.pallas_call(
        functools.partial(attend_kernel, reach),
        out_shape=jax.ShapeDtypeStruct((rows, head_dim), jnp.bfloat16),
        in_specs=[smem, smem, vmem, pl.BlockSpec(memory_space=pl.ANY), vmem, vmem],
        out_specs=vmem,
        scratch_shapes=[
            pltpu.VMEM((slots, rows, 2 * head_dim), jnp.bfloat16),
            pltpu.VMEM(contact_tiles.shape, jnp.float32),
            pltpu.VMEM((slots, rows, rows), jnp.float32),
            pltpu.VMEM((rows, tile), jnp.float32),
            pltpu.VMEM((rows, tile), jnp.float32),
            pltpu.VMEM((rows, head_dim), jnp.float32),
            pltpu.SemaphoreType.DMA((slots,)),
        ],
        compiler_params=pltpu.CompilerParams(vmem_limit_bytes=60 << 20),
        name="attend",
    )(tile_codes, place, queries, everything, contact_tiles, valid_rows)


def per_device(
    activations,
    dilated_tap_weight,
    conv_mix,
    w_query,
    w_keyval,
    contact_tiles,
    tile_codes,
    bin_valid,
):
    seq_size = lax.axis_size("seq")
    position = lax.axis_index("seq")
    halo = halo_rows(activations)
    *lifted, table = lift(
        activations, dilated_tap_weight, conv_mix, w_query, w_keyval, contact_tiles
    )
    queries, keyval = front(lifted, halo, tile_codes)
    if seq_size == 16 and seq_size * activations.shape[0] == 2 * HALF:
        return attend_split(queries, keyval, table, tile_codes, bin_valid, seq_size)
    queries = queries[: activations.shape[0]]
    everything = lax.all_gather(keyval, "seq", axis=0, tiled=True)
    return attend(queries, everything, contact_tiles, tile_codes, bin_valid, position, seq_size)


def solution(mesh):
    in_specs = (P(("grp", "seq"), None), P(), P(), P(), P(), P(), P(("grp", "seq"), None), P("grp"))
    out_specs = P(("grp", "seq"), None)
    return jax.shard_map(
        per_device, mesh=mesh, in_specs=in_specs, out_specs=out_specs, check_vma=False
    )
```

```python
import functools
import math

import jax
import jax.numpy as jnp
from jax import lax
from jax.experimental import pallas as pl
from jax.experimental.pallas import tpu as pltpu
from jax.sharding import PartitionSpec as P


HDIM = 128
CONV_DILATION = 8
HALF = 4096


masked_score = -1e30
norm_eps = 1e-06
LOG2E = 1.4426950408889634


def halo_rows(activations):
    size = lax.axis_size("seq")
    odd = lax.axis_index("seq") % 2 == 1
    rows = activations.shape[0]
    initial = lax.slice_in_dim(activations, 0, CONV_DILATION, axis=0)
    last = lax.slice_in_dim(activations, rows - CONV_DILATION, rows, axis=0)
    inner = [(i, i ^ 1) for i in range(size)]
    outer = [(i, i + 1) for i in range(1, size - 1, 2)] + [(i + 1, i) for i in range(1, size - 1, 2)]
    from_inner = lax.ppermute(jnp.where(odd, initial, last), "seq", inner)
    from_outer = lax.ppermute(jnp.where(odd, last, initial), "seq", outer)
    return from_inner, from_outer


def gelu(v):
    return 0.5 * v * (1.0 + lax.erf(v * math.sqrt(0.5)))


def lift_kernel(x_hbm, taps_hbm, mix_hbm, wq_hbm, wkv_hbm, tiles_hbm, *refs):
    x_ref, taps, mix, wq, wkv, inner, outer, table, tiles, sems = refs
    copies = [
        pltpu.make_async_copy(source, target, sems.at[i])
        for i, (source, target) in enumerate(
            [
                (x_hbm, x_ref),
                (tiles_hbm, tiles),
                (taps_hbm, taps),
                (mix_hbm, mix),
                (wq_hbm, wq),
                (wkv_hbm, wkv),
            ]
        )
    ]
    for copy in copies:
        copy.start()
    rows, channels = x_ref.shape
    step = 32
    d = CONV_DILATION
    copies[0].wait()

    def lift(i, tail):
        r = pl.multiple_of(i * step, step)
        g = gelu(x_ref[pl.ds(r, step), :].astype(jnp.float32))
        inner[pl.ds(r, step), :] = g.astype(jnp.bfloat16)
        outer[pl.ds(r, step), :] = jnp.concatenate([tail, g[: step - d]], axis=0).astype(
            jnp.bfloat16
        )
        return g[step - d :]

    edge = jnp.zeros((d, channels), jnp.float32)
    tail = lax.fori_loop(0, rows // step, lift, edge)
    outer[rows : rows + 2 * d, :] = jnp.concatenate([tail, edge], axis=0).astype(jnp.bfloat16)
    copies[1].wait()
    table[...] = tiles[...].astype(jnp.float32) * LOG2E
    for copy in copies[2:]:
        copy.wait()


def lift(activations, dilated_tap_weight, conv_mix, w_query, w_keyval, contact_tiles):
    rows, channels = activations.shape
    moved = [
        pltpu.with_memory_space_constraint(a, pltpu.HBM)
        for a in (activations, dilated_tap_weight, conv_mix, w_query, w_keyval)
    ]
    contact_tiles = pltpu.with_memory_space_constraint(contact_tiles, pltpu.HBM)
    vmem = pl.BlockSpec(memory_space=pltpu.VMEM)
    return pl.pallas_call(
        lift_kernel,
        out_shape=[jax.ShapeDtypeStruct(a.shape, a.dtype) for a in moved]
        + [
            jax.ShapeDtypeStruct((rows, channels), jnp.bfloat16),
            jax.ShapeDtypeStruct((rows + 2 * CONV_DILATION, channels), jnp.bfloat16),
            jax.ShapeDtypeStruct(contact_tiles.shape, jnp.float32),
        ],
        in_specs=[pl.BlockSpec(memory_space=pltpu.HBM)] * 6,
        out_specs=[vmem] * 8,
        scratch_shapes=[
            pltpu.VMEM(contact_tiles.shape, contact_tiles.dtype),
            pltpu.SemaphoreType.DMA((6,)),
        ],
        compiler_params=pltpu.CompilerParams(vmem_limit_bytes=24 << 20),
        name="lift",
    )(*moved, contact_tiles)


def front_kernel(
    x_ref,
    taps,
    mix,
    wq,
    wkv,
    inner,
    outer_ref,
    twin_ref,
    outside_ref,
    codes_ref,
    q_ref,
    kv_ref,
    outer,
    squeezed,
    mixed,
):
    rows, channels = x_ref.shape
    hidden = squeezed.shape[1]
    d = CONV_DILATION
    odd = lax.axis_index("seq") % 2 == 1
    beside = gelu(twin_ref[...].astype(jnp.float32))
    beyond = gelu(outside_ref[...].astype(jnp.float32))
    before = jnp.where(odd, beside, beyond)
    after = jnp.where(odd, beyond, beside)
    outer[...] = outer_ref[...]
    initial = outer_ref[0 : 2 * d, :].astype(jnp.float32)[d:]
    last = outer_ref[rows : rows + 2 * d, :].astype(jnp.float32)[:d]
    outer[0 : 2 * d, :] = jnp.concatenate([before, initial], axis=0).astype(jnp.bfloat16)
    outer[rows : rows + 2 * d, :] = jnp.concatenate([last, after], axis=0).astype(jnp.bfloat16)

    wide = 256
    taps_rows, mix_rows, out_rows = rows // 2, rows // 1, rows // 1
    for n in range(hidden // wide):
        cols = slice(n * wide, (n + 1) * wide)
        for r in range(0, rows, taps_rows):
            conv = jnp.dot(
                outer[r : r + taps_rows, :], taps[0, :, cols], preferred_element_type=jnp.float32
            )
            conv += jnp.dot(
                inner[r : r + taps_rows, :], taps[1, :, cols], preferred_element_type=jnp.float32
            )
            conv += jnp.dot(
                outer[r + 2 * d : r + 2 * d + taps_rows, :],
                taps[2, :, cols],
                preferred_element_type=jnp.float32,
            )
            squeezed[r : r + taps_rows, cols] = gelu(conv).astype(jnp.bfloat16)

    squares = [jnp.zeros((mix_rows, 128), jnp.float32) for _ in range(rows // mix_rows)]
    for n in range(channels // wide):
        cols = slice(n * wide, (n + 1) * wide)
        for i in range(rows // mix_rows):
            span = slice(i * mix_rows, (i + 1) * mix_rows)
            part = x_ref[span, cols].astype(jnp.float32) + jnp.dot(
                squeezed[span, :], mix[:, cols], preferred_element_type=jnp.float32
            )
            mixed[span, cols] = part
            for k in range(wide // 128):
                piece = part[:, k * 128 : (k + 1) * 128]
                squares[i] += piece * piece
    gain = lax.rsqrt(
        jnp.sum(jnp.concatenate(squares, axis=0), axis=1, keepdims=True) / channels + norm_eps
    )
    for r in range(0, rows, out_rows):
        span = slice(r, r + out_rows)
        normed = (mixed[span, :] * gain[span]).astype(jnp.bfloat16)
        q_ref[span, :] = jnp.dot(normed, wq[...], preferred_element_type=jnp.float32).astype(
            jnp.bfloat16
        )
        kv_ref[span, :] = jnp.dot(normed, wkv[...], preferred_element_type=jnp.float32).astype(
            jnp.bfloat16
        )
    q_ref[rows:, :] = jnp.zeros((q_ref.shape[0] - rows, q_ref.shape[1]), jnp.bfloat16)
    q_ref[rows : rows + codes_ref.shape[0], 0 : codes_ref.shape[1]] = (
        codes_ref[...].astype(jnp.float32).astype(jnp.bfloat16)
    )


CODE_ROWS = 16


def front(lifted, halo, tile_codes):
    activations, _, conv_mix, w_query, w_keyval, _, outer = lifted
    rows, channels = activations.shape
    vmem = pl.BlockSpec(memory_space=pltpu.VMEM)
    bf16 = jnp.bfloat16
    return pl.pallas_call(
        front_kernel,
        out_shape=[
            jax.ShapeDtypeStruct((rows + CODE_ROWS, w_query.shape[1]), bf16),
            jax.ShapeDtypeStruct((rows, w_keyval.shape[1]), bf16),
        ],
        in_specs=[vmem] * 10,
        out_specs=[vmem, vmem],
        scratch_shapes=[
            pltpu.VMEM(outer.shape, bf16),
            pltpu.VMEM((rows, conv_mix.shape[0]), bf16),
            pltpu.VMEM((rows, channels), jnp.float32),
        ],
        compiler_params=pltpu.CompilerParams(vmem_limit_bytes=24 << 20),
        name="front",
    )(*lifted, *halo, tile_codes)


def attend_kernel(
    reach,
    codes_ref,
    place_ref,
    q_ref,
    kv_ref,
    tiles_ref,
    valid_ref,
    out_ref,
    kv_buf,
    bias_buf,
    scores,
    peak,
    total,
    acc,
    sems,
):
    rows, head_dim = q_ref.shape
    _, tile, _ = tiles_ref.shape
    tiles_per_block = rows // tile
    position = place_ref[0]
    first = place_ref[1]
    count = place_ref[2]
    factor = LOG2E / math.sqrt(head_dim)

    def fetch(i):
        return pltpu.make_async_copy(
            kv_ref.at[pl.ds((first + i) * rows, rows), :], kv_buf.at[i], sems.at[i]
        )

    @pl.loop(0, count)
    def _(i):
        fetch(i).start()

    bias_buf[...] = tiles_ref[...].astype(jnp.float32) * LOG2E
    peak[...] = jnp.full_like(peak, masked_score)

    @pl.loop(0, count)
    def _(i):
        fetch(i).wait()
        block = first + i
        keys = kv_buf[i, :, :head_dim]
        raw = lax.dot_general(
            q_ref[...], keys, (((1,), (1,)), ((), ())), preferred_element_type=jnp.float32
        )
        invalid = jnp.where(valid_ref[block] == 1, 0.0, masked_score)
        shift = block - position

        def tile_scores(qt, kt):
            offset = jnp.clip(shift * tiles_per_block + kt - qt + HALF // tile, 0, 2 * (HALF // tile))
            part = raw[qt * tile : (qt + 1) * tile, kt * tile : (kt + 1) * tile]
            return part * factor + bias_buf[codes_ref[qt, offset]]

        def keep(qt, columns):
            peak_now = peak[qt * tile : (qt + 1) * tile, :]
            for kt, column in enumerate(columns):
                scores[i, qt * tile : (qt + 1) * tile, kt * tile : (kt + 1) * tile] = column
                peak_now = jnp.maximum(peak_now, column)
            peak[qt * tile : (qt + 1) * tile, :] = peak_now

        plain = (shift != 0) & (jnp.abs(shift) < reach)

        @pl.when(plain)
        def _():
            for qt in range(tiles_per_block):
                keep(
                    qt,
                    [
                        tile_scores(qt, kt) + invalid[:, kt * tile : (kt + 1) * tile]
                        for kt in range(tiles_per_block)
                    ],
                )

        @pl.when(jnp.logical_not(plain))
        def _():
            lag = lax.broadcasted_iota(jnp.int32, (tile, tile), 1) - lax.broadcasted_iota(
                jnp.int32, (tile, tile), 0
            )
            for qt in range(tiles_per_block):
                columns = []
                for kt in range(tiles_per_block):
                    apart = lag + (shift * rows + (kt - qt) * tile)
                    dropped = jnp.where(
                        apart == 0, 0.0, invalid[:, kt * tile : (kt + 1) * tile]
                    )
                    dropped = jnp.where(jnp.abs(apart) <= HALF, dropped, masked_score)
                    columns.append(tile_scores(qt, kt) + dropped)
                keep(qt, columns)

    peak[...] = jnp.broadcast_to(jnp.max(peak[...], axis=1, keepdims=True), peak.shape)
    total[...] = jnp.zeros_like(total)
    acc[...] = jnp.zeros_like(acc)

    @pl.loop(0, count)
    def _(i):
        parts = []
        sums = total[...]
        for kt in range(tiles_per_block):
            probs = jnp.exp2(scores[i, :, kt * tile : (kt + 1) * tile] - peak[...])
            sums = sums + probs
            parts.append(probs.astype(jnp.bfloat16))
        total[...] = sums
        acc[...] += jnp.dot(
            jnp.concatenate(parts, axis=1),
            kv_buf[i, :, head_dim:],
            preferred_element_type=jnp.float32,
        )

    out_ref[...] = (acc[...] / jnp.sum(total[...], axis=1, keepdims=True)).astype(out_ref.dtype)


def block_scores(shift, edge, raw, invalid, table, codes_ref, half, qt, tile):
    factor = LOG2E / math.sqrt(HDIM)
    count = raw.shape[1] // tile
    columns = []
    if edge:
        lag = lax.broadcasted_iota(jnp.int32, (tile, tile), 1) - lax.broadcasted_iota(
            jnp.int32, (tile, tile), 0
        )
    for kt in range(count):
        span = slice(kt * tile, (kt + 1) * tile)
        offset = jnp.clip(shift * count + kt - qt + HALF // tile, 0, 2 * (HALF // tile))
        dropped = invalid[:, span]
        if edge:
            apart = lag + (shift * (tile * count) + (kt - qt) * tile)
            dropped = jnp.where(apart == 0, 0.0, dropped)
            dropped = jnp.where(jnp.abs(apart) <= HALF, dropped, masked_score)
        part = raw[qt * tile : (qt + 1) * tile, span]
        columns.append((part * factor + table[codes_ref[half + qt, offset]]) + dropped)
    return columns


def absorb_kernel(reach, flips, blocks, begin, pack, codes_ref, *refs):
    sets, n = len(flips), len(blocks)
    q_refs, refs = refs[:sets], refs[sets:]
    kv_refs, refs = refs[:n], refs[n:]
    table, valid_ref = refs[:2]
    refs = refs[2:]
    if not begin:
        state_refs, refs = refs[: 3 * sets], refs[3 * sets :]
    outs = 1 if pack else 3 * sets
    out_refs, refs = refs[:outs], refs[outs:]
    scores, peak, total, acc = refs
    rows, head_dim = acc.shape
    tile = table.shape[1]
    tiles_per_block = rows // tile
    position = lax.axis_index("seq")

    for s, flip in enumerate(flips):
        owner = position ^ flip
        q_ref = q_refs[s]
        half = 0 if flip == 0 else tiles_per_block
        if begin:
            peak[...] = jnp.full_like(peak, masked_score)
        else:
            peak[...] = state_refs[3 * s][...]

        def each(step):
            for j, block in enumerate(blocks):
                shift = (position ^ block) - owner
                run = functools.partial(step, j, shift, (block ^ flip) in (0, reach))
                if block ^ flip < reach:
                    run()
                else:
                    pl.when(jnp.abs(shift) <= reach)(run)

        def score(j, shift, edge):
            raw = lax.dot_general(
                q_ref[0:rows, :],
                kv_refs[j][:, :head_dim],
                (((1,), (1,)), ((), ())),
                preferred_element_type=jnp.float32,
            )
            invalid = jnp.where(valid_ref[owner + shift] == 1, 0.0, masked_score)
            for qt in range(tiles_per_block):
                span = slice(qt * tile, (qt + 1) * tile)
                peak_now = peak[span, :]
                columns = block_scores(
                    shift, edge, raw, invalid, table, codes_ref, half, qt, tile
                )
                for kt, column in enumerate(columns):
                    scores[j, span, kt * tile : (kt + 1) * tile] = column
                    peak_now = jnp.maximum(peak_now, column)
                peak[span, :] = peak_now

        def weigh(j, shift, edge):
            parts = []
            sums = total[...]
            for kt in range(tiles_per_block):
                probs = jnp.exp2(scores[j, :, kt * tile : (kt + 1) * tile] - peak[...])
                sums = sums + probs
                parts.append(probs.astype(jnp.bfloat16))
            total[...] = sums
            acc[...] += jnp.dot(
                jnp.concatenate(parts, axis=1),
                kv_refs[j][:, head_dim:],
                preferred_element_type=jnp.float32,
            )

        each(score)
        peak[...] = jnp.broadcast_to(jnp.max(peak[...], axis=1, keepdims=True), peak.shape)
        if begin:
            total[...] = jnp.zeros_like(total)
            acc[...] = jnp.zeros_like(acc)
        else:
            rescale = jnp.exp2(state_refs[3 * s][...] - peak[...])
            total[...] = state_refs[3 * s + 1][...] * rescale
            acc[...] = state_refs[3 * s + 2][...] * rescale
        each(weigh)

        if pack:
            out_refs[0][0:rows, :] = acc[...].astype(jnp.bfloat16)
            sums = jnp.broadcast_to(jnp.sum(total[...], axis=1, keepdims=True), total.shape)
            eye = on_diagonal(tile)
            lines = []
            for column in (peak[...], sums):
                for qt in range(tiles_per_block):
                    part = column[qt * tile : (qt + 1) * tile, :]
                    lines.append(jnp.sum(jnp.where(eye, part, 0.0), axis=0, keepdims=True))
            exact = jnp.concatenate(lines, axis=0)
            pieces = []
            for _ in range(3):
                piece = exact.astype(jnp.bfloat16).astype(jnp.float32)
                exact = exact - piece
                pieces.append(piece)
            pieces.append(jnp.zeros_like(exact))
            out_refs[0][rows:, :] = jnp.concatenate(pieces, axis=0).astype(jnp.bfloat16)
        else:
            out_refs[3 * s][...] = peak[...]
            out_refs[3 * s + 1][...] = total[...]
            out_refs[3 * s + 2][...] = acc[...]


def on_diagonal(tile):
    return lax.broadcasted_iota(jnp.int32, (tile, tile), 0) == lax.broadcasted_iota(
        jnp.int32, (tile, tile), 1
    )


def absorb(reach, codes, queries, keyvals, table, valid_rows, flips, blocks, state, pack):
    rows = keyvals[0].shape[0]
    head_dim = queries[0].shape[1]
    tile = table.shape[1]
    n = len(blocks)
    vmem = pl.BlockSpec(memory_space=pltpu.VMEM)
    smem = pl.BlockSpec(memory_space=pltpu.SMEM)
    column = jax.ShapeDtypeStruct((rows, tile), jnp.float32)
    if pack:
        out_shape = [jax.ShapeDtypeStruct((rows + 8 * (rows // tile), head_dim), jnp.bfloat16)]
    else:
        out_shape = [column, column, column] * len(flips)
    units = len(flips) * n
    return pl.pallas_call(
        functools.partial(absorb_kernel, reach, flips, blocks, not state, pack),
        out_shape=out_shape,
        in_specs=[smem] + [vmem] * (len(flips) + n + 2 + len(state)),
        out_specs=[vmem] * len(out_shape),
        scratch_shapes=[
            pltpu.VMEM((n, rows, rows), jnp.float32),
            pltpu.VMEM((rows, tile), jnp.float32),
            pltpu.VMEM((rows, tile), jnp.float32),
            pltpu.VMEM((rows, head_dim), jnp.float32),
        ],
        compiler_params=pltpu.CompilerParams(vmem_limit_bytes=24 << 20),
        cost_estimate=pl.CostEstimate(
            flops=units * 4 * rows * rows * head_dim,
            bytes_accessed=units * 4 * rows * rows,
            transcendentals=units * rows * rows,
        ),
    )(codes, *queries, *keyvals, table, valid_rows, *state)


def merge_kernel(peak_ref, total_ref, acc_ref, pack_ref, out_ref):
    rows, _ = acc_ref.shape
    tile = peak_ref.shape[1]
    eye = on_diagonal(tile)
    count = rows // tile
    pieces = pack_ref[rows:, :].astype(jnp.float32)
    lines = 2 * count
    exact = pieces[:lines] + pieces[lines : 2 * lines] + pieces[2 * lines : 3 * lines]
    for qt in range(count):
        span = slice(qt * tile, (qt + 1) * tile)

        def column(line):
            row = exact[line : line + 1, :]
            return jnp.sum(jnp.where(eye, row, 0.0), axis=1, keepdims=True)

        peak_a = peak_ref[span, :]
        peak_b = column(qt)
        total_a = jnp.sum(total_ref[span, :], axis=1, keepdims=True)
        total_b = column(count + qt)
        top = jnp.maximum(peak_a, peak_b)
        scale_a = jnp.exp2(peak_a - top)
        scale_b = jnp.exp2(peak_b - top)
        whole = total_a * scale_a + total_b * scale_b
        out_ref[span, :] = (
            (acc_ref[span, :] * scale_a + pack_ref[span, :].astype(jnp.float32) * scale_b) / whole
        ).astype(out_ref.dtype)


def attend_split(queries, keyval, table, tile_codes, bin_valid, seq_size):
    rows = keyval.shape[0]
    reach = HALF // rows
    z = seq_size // 4
    half = z // 2
    valid_rows = bin_valid.reshape(seq_size, 1, rows)

    def trade(x, flip, some=None):
        pairs = [(i, i ^ flip) for i in range(seq_size) if some is None or some(i // z)]
        return lax.ppermute(x, "seq", pairs)

    peer_queries = trade(queries, half)
    far = trade(keyval, 2 * z)
    middle = trade(keyval, 3 * z, lambda level: level in (1, 2))
    near = trade(keyval, z)
    twin = trade(keyval, 1)
    peer_codes = peer_queries[rows : rows + tile_codes.shape[0], : tile_codes.shape[1]]
    codes = jnp.concatenate([tile_codes, peer_codes.astype(jnp.int32)], axis=0)
    common = (table, valid_rows)
    state = absorb(
        reach, codes, [queries, peer_queries], [keyval, twin], *common, (0, half), (0, 1), [], False
    )
    near, middle, state = lax.optimization_barrier((near, middle, state))
    near_twin = trade(near, 1)
    middle_twin = trade(middle, 1)
    state = absorb(
        reach,
        codes,
        [queries, peer_queries],
        [near, near_twin, middle, middle_twin],
        *common,
        (0, half),
        (z, z + 1, 3 * z, 3 * z + 1),
        state,
        False,
    )
    far, state = lax.optimization_barrier((far, state))
    far_twin = trade(far, 1)
    away = [far, far_twin]
    leaps = (2 * z, 2 * z + 1)
    theirs = absorb(
        reach, codes, [peer_queries], away[:1], *common, (half,), leaps[:1], state[3:], False
    )
    (pack,) = absorb(
        reach, codes, [peer_queries], away[1:], *common, (half,), leaps[1:], theirs, True
    )
    other = trade(pack, half)
    peak, total, acc = absorb(reach, codes, [queries], away, *common, (0,), leaps, state[:3], False)
    vmem = pl.BlockSpec(memory_space=pltpu.VMEM)
    return pl.pallas_call(
        merge_kernel,
        out_shape=jax.ShapeDtypeStruct((rows, queries.shape[1]), jnp.bfloat16),
        in_specs=[vmem] * 4,
        out_specs=vmem,
        compiler_params=pltpu.CompilerParams(vmem_limit_bytes=8 << 20),
        name="merge",
    )(peak, total, acc, other)


def attend(queries, everything, contact_tiles, tile_codes, bin_valid, position, seq_size):
    rows, head_dim = queries.shape
    reach = HALF // rows
    tile = contact_tiles.shape[1]
    slots = min(seq_size, 2 * reach + 1)
    first = jnp.maximum(position - reach, 0)
    last = jnp.minimum(position + reach, seq_size - 1)
    place = jnp.stack([position, first, last - first + 1]).astype(jnp.int32)
    valid_rows = bin_valid.reshape(seq_size, 1, rows)
    vmem = pl.BlockSpec(memory_space=pltpu.VMEM)
    smem = pl.BlockSpec(memory_space=pltpu.SMEM)
    return pl.pallas_call(
        functools.partial(attend_kernel, reach),
        out_shape=jax.ShapeDtypeStruct((rows, head_dim), jnp.bfloat16),
        in_specs=[smem, smem, vmem, pl.BlockSpec(memory_space=pl.ANY), vmem, vmem],
        out_specs=vmem,
        scratch_shapes=[
            pltpu.VMEM((slots, rows, 2 * head_dim), jnp.bfloat16),
            pltpu.VMEM(contact_tiles.shape, jnp.float32),
            pltpu.VMEM((slots, rows, rows), jnp.float32),
            pltpu.VMEM((rows, tile), jnp.float32),
            pltpu.VMEM((rows, tile), jnp.float32),
            pltpu.VMEM((rows, head_dim), jnp.float32),
            pltpu.SemaphoreType.DMA((slots,)),
        ],
        compiler_params=pltpu.CompilerParams(vmem_limit_bytes=60 << 20),
        name="attend",
    )(tile_codes, place, queries, everything, contact_tiles, valid_rows)


def per_device(
    activations,
    dilated_tap_weight,
    conv_mix,
    w_query,
    w_keyval,
    contact_tiles,
    tile_codes,
    bin_valid,
):
    seq_size = lax.axis_size("seq")
    position = lax.axis_index("seq")
    halo = halo_rows(activations)
    *lifted, table = lift(
        activations, dilated_tap_weight, conv_mix, w_query, w_keyval, contact_tiles
    )
    queries, keyval = front(lifted, halo, tile_codes)
    if seq_size == 16 and seq_size * activations.shape[0] == 2 * HALF:
        return attend_split(queries, keyval, table, tile_codes, bin_valid, seq_size)
    queries = queries[: activations.shape[0]]
    everything = lax.all_gather(keyval, "seq", axis=0, tiled=True)
    return attend(queries, everything, contact_tiles, tile_codes, bin_valid, position, seq_size)


def solution(mesh):
    in_specs = (P(("grp", "seq"), None), P(), P(), P(), P(), P(), P(("grp", "seq"), None), P("grp"))
    out_specs = P(("grp", "seq"), None)
    return jax.shard_map(
        per_device, mesh=mesh, in_specs=in_specs, out_specs=out_specs, check_vma=False
    )
```

```python
import functools
import math

import jax
import jax.numpy as jnp
from jax import lax
from jax.experimental import pallas as pl
from jax.experimental.pallas import tpu as pltpu
from jax.sharding import PartitionSpec as P


HDIM = 128
CONV_DILATION = 8
HALF = 4096


masked_score = -1e30
norm_eps = 1e-06
LOG2E = 1.4426950408889634


def halo_rows(activations):
    size = lax.axis_size("seq")
    odd = lax.axis_index("seq") % 2 == 1
    rows = activations.shape[0]
    initial = lax.slice_in_dim(activations, 0, CONV_DILATION, axis=0)
    last = lax.slice_in_dim(activations, rows - CONV_DILATION, rows, axis=0)
    inner = [(i, i ^ 1) for i in range(size)]
    outer = [(i, i + 1) for i in range(1, size - 1, 2)] + [(i + 1, i) for i in range(1, size - 1, 2)]
    from_inner = lax.ppermute(jnp.where(odd, initial, last), "seq", inner)
    from_outer = lax.ppermute(jnp.where(odd, last, initial), "seq", outer)
    return from_inner, from_outer


def gelu(v):
    return 0.5 * v * (1.0 + lax.erf(v * math.sqrt(0.5)))


def lift_kernel(x_hbm, taps_hbm, mix_hbm, wq_hbm, wkv_hbm, tiles_hbm, *refs):
    x_ref, taps, mix, wq, wkv, inner, outer, table, tiles, sems = refs
    copies = [
        pltpu.make_async_copy(source, target, sems.at[i])
        for i, (source, target) in enumerate(
            [
                (x_hbm, x_ref),
                (tiles_hbm, tiles),
                (taps_hbm, taps),
                (mix_hbm, mix),
                (wq_hbm, wq),
                (wkv_hbm, wkv),
            ]
        )
    ]
    for copy in copies:
        copy.start()
    rows, channels = x_ref.shape
    step = 32
    d = CONV_DILATION
    copies[0].wait()

    def lift(i, tail):
        r = pl.multiple_of(i * step, step)
        g = gelu(x_ref[pl.ds(r, step), :].astype(jnp.float32))
        inner[pl.ds(r, step), :] = g.astype(jnp.bfloat16)
        outer[pl.ds(r, step), :] = jnp.concatenate([tail, g[: step - d]], axis=0).astype(
            jnp.bfloat16
        )
        return g[step - d :]

    edge = jnp.zeros((d, channels), jnp.float32)
    tail = lax.fori_loop(0, rows // step, lift, edge)
    outer[rows : rows + 2 * d, :] = jnp.concatenate([tail, edge], axis=0).astype(jnp.bfloat16)
    copies[1].wait()
    table[...] = tiles[...].astype(jnp.float32) * LOG2E
    for copy in copies[2:]:
        copy.wait()


def lift(activations, dilated_tap_weight, conv_mix, w_query, w_keyval, contact_tiles):
    rows, channels = activations.shape
    moved = [
        pltpu.with_memory_space_constraint(a, pltpu.HBM)
        for a in (activations, dilated_tap_weight, conv_mix, w_query, w_keyval)
    ]
    contact_tiles = pltpu.with_memory_space_constraint(contact_tiles, pltpu.HBM)
    vmem = pl.BlockSpec(memory_space=pltpu.VMEM)
    return pl.pallas_call(
        lift_kernel,
        out_shape=[jax.ShapeDtypeStruct(a.shape, a.dtype) for a in moved]
        + [
            jax.ShapeDtypeStruct((rows, channels), jnp.bfloat16),
            jax.ShapeDtypeStruct((rows + 2 * CONV_DILATION, channels), jnp.bfloat16),
            jax.ShapeDtypeStruct(contact_tiles.shape, jnp.float32),
        ],
        in_specs=[pl.BlockSpec(memory_space=pltpu.HBM)] * 6,
        out_specs=[vmem] * 8,
        scratch_shapes=[
            pltpu.VMEM(contact_tiles.shape, contact_tiles.dtype),
            pltpu.SemaphoreType.DMA((6,)),
        ],
        compiler_params=pltpu.CompilerParams(vmem_limit_bytes=24 << 20),
        name="lift",
    )(*moved, contact_tiles)


def front_kernel(
    x_ref,
    taps,
    mix,
    wq,
    wkv,
    inner,
    outer_ref,
    twin_ref,
    outside_ref,
    codes_ref,
    q_ref,
    kv_ref,
    outer,
    squeezed,
    mixed,
):
    rows, channels = x_ref.shape
    hidden = squeezed.shape[1]
    d = CONV_DILATION
    odd = lax.axis_index("seq") % 2 == 1
    beside = gelu(twin_ref[...].astype(jnp.float32))
    beyond = gelu(outside_ref[...].astype(jnp.float32))
    before = jnp.where(odd, beside, beyond)
    after = jnp.where(odd, beyond, beside)
    outer[...] = outer_ref[...]
    initial = outer_ref[0 : 2 * d, :].astype(jnp.float32)[d:]
    last = outer_ref[rows : rows + 2 * d, :].astype(jnp.float32)[:d]
    outer[0 : 2 * d, :] = jnp.concatenate([before, initial], axis=0).astype(jnp.bfloat16)
    outer[rows : rows + 2 * d, :] = jnp.concatenate([last, after], axis=0).astype(jnp.bfloat16)

    wide = 256
    taps_rows, mix_rows, out_rows = rows // 2, rows // 1, rows // 1
    for n in range(hidden // wide):
        cols = slice(n * wide, (n + 1) * wide)
        for r in range(0, rows, taps_rows):
            conv = jnp.dot(
                outer[r : r + taps_rows, :], taps[0, :, cols], preferred_element_type=jnp.float32
            )
            conv += jnp.dot(
                inner[r : r + taps_rows, :], taps[1, :, cols], preferred_element_type=jnp.float32
            )
            conv += jnp.dot(
                outer[r + 2 * d : r + 2 * d + taps_rows, :],
                taps[2, :, cols],
                preferred_element_type=jnp.float32,
            )
            squeezed[r : r + taps_rows, cols] = gelu(conv).astype(jnp.bfloat16)

    squares = [jnp.zeros((mix_rows, 128), jnp.float32) for _ in range(rows // mix_rows)]
    for n in range(channels // wide):
        cols = slice(n * wide, (n + 1) * wide)
        for i in range(rows // mix_rows):
            span = slice(i * mix_rows, (i + 1) * mix_rows)
            part = x_ref[span, cols].astype(jnp.float32) + jnp.dot(
                squeezed[span, :], mix[:, cols], preferred_element_type=jnp.float32
            )
            mixed[span, cols] = part
            for k in range(wide // 128):
                piece = part[:, k * 128 : (k + 1) * 128]
                squares[i] += piece * piece
    gain = lax.rsqrt(
        jnp.sum(jnp.concatenate(squares, axis=0), axis=1, keepdims=True) / channels + norm_eps
    )
    for r in range(0, rows, out_rows):
        span = slice(r, r + out_rows)
        normed = (mixed[span, :] * gain[span]).astype(jnp.bfloat16)
        q_ref[span, :] = jnp.dot(normed, wq[...], preferred_element_type=jnp.float32).astype(
            jnp.bfloat16
        )
        kv_ref[span, :] = jnp.dot(normed, wkv[...], preferred_element_type=jnp.float32).astype(
            jnp.bfloat16
        )
    q_ref[rows:, :] = jnp.zeros((q_ref.shape[0] - rows, q_ref.shape[1]), jnp.bfloat16)
    q_ref[rows : rows + codes_ref.shape[0], 0 : codes_ref.shape[1]] = (
        codes_ref[...].astype(jnp.float32).astype(jnp.bfloat16)
    )


CODE_ROWS = 16


def front(lifted, halo, tile_codes):
    activations, _, conv_mix, w_query, w_keyval, _, outer = lifted
    rows, channels = activations.shape
    vmem = pl.BlockSpec(memory_space=pltpu.VMEM)
    bf16 = jnp.bfloat16
    return pl.pallas_call(
        front_kernel,
        out_shape=[
            jax.ShapeDtypeStruct((rows + CODE_ROWS, w_query.shape[1]), bf16),
            jax.ShapeDtypeStruct((rows, w_keyval.shape[1]), bf16),
        ],
        in_specs=[vmem] * 10,
        out_specs=[vmem, vmem],
        scratch_shapes=[
            pltpu.VMEM(outer.shape, bf16),
            pltpu.VMEM((rows, conv_mix.shape[0]), bf16),
            pltpu.VMEM((rows, channels), jnp.float32),
        ],
        compiler_params=pltpu.CompilerParams(vmem_limit_bytes=24 << 20),
        name="front",
    )(*lifted, *halo, tile_codes)


def attend_kernel(
    reach,
    codes_ref,
    place_ref,
    q_ref,
    kv_ref,
    tiles_ref,
    valid_ref,
    out_ref,
    kv_buf,
    bias_buf,
    scores,
    peak,
    total,
    acc,
    sems,
):
    rows, head_dim = q_ref.shape
    _, tile, _ = tiles_ref.shape
    tiles_per_block = rows // tile
    position = place_ref[0]
    first = place_ref[1]
    count = place_ref[2]
    factor = LOG2E / math.sqrt(head_dim)

    def fetch(i):
        return pltpu.make_async_copy(
            kv_ref.at[pl.ds((first + i) * rows, rows), :], kv_buf.at[i], sems.at[i]
        )

    @pl.loop(0, count)
    def _(i):
        fetch(i).start()

    bias_buf[...] = tiles_ref[...].astype(jnp.float32) * LOG2E
    peak[...] = jnp.full_like(peak, masked_score)

    @pl.loop(0, count)
    def _(i):
        fetch(i).wait()
        block = first + i
        keys = kv_buf[i, :, :head_dim]
        raw = lax.dot_general(
            q_ref[...], keys, (((1,), (1,)), ((), ())), preferred_element_type=jnp.float32
        )
        invalid = jnp.where(valid_ref[block] == 1, 0.0, masked_score)
        shift = block - position

        def tile_scores(qt, kt):
            offset = jnp.clip(shift * tiles_per_block + kt - qt + HALF // tile, 0, 2 * (HALF // tile))
            part = raw[qt * tile : (qt + 1) * tile, kt * tile : (kt + 1) * tile]
            return part * factor + bias_buf[codes_ref[qt, offset]]

        def keep(qt, columns):
            peak_now = peak[qt * tile : (qt + 1) * tile, :]
            for kt, column in enumerate(columns):
                scores[i, qt * tile : (qt + 1) * tile, kt * tile : (kt + 1) * tile] = column
                peak_now = jnp.maximum(peak_now, column)
            peak[qt * tile : (qt + 1) * tile, :] = peak_now

        plain = (shift != 0) & (jnp.abs(shift) < reach)

        @pl.when(plain)
        def _():
            for qt in range(tiles_per_block):
                keep(
                    qt,
                    [
                        tile_scores(qt, kt) + invalid[:, kt * tile : (kt + 1) * tile]
                        for kt in range(tiles_per_block)
                    ],
                )

        @pl.when(jnp.logical_not(plain))
        def _():
            lag = lax.broadcasted_iota(jnp.int32, (tile, tile), 1) - lax.broadcasted_iota(
                jnp.int32, (tile, tile), 0
            )
            for qt in range(tiles_per_block):
                columns = []
                for kt in range(tiles_per_block):
                    apart = lag + (shift * rows + (kt - qt) * tile)
                    dropped = jnp.where(
                        apart == 0, 0.0, invalid[:, kt * tile : (kt + 1) * tile]
                    )
                    dropped = jnp.where(jnp.abs(apart) <= HALF, dropped, masked_score)
                    columns.append(tile_scores(qt, kt) + dropped)
                keep(qt, columns)

    peak[...] = jnp.broadcast_to(jnp.max(peak[...], axis=1, keepdims=True), peak.shape)
    total[...] = jnp.zeros_like(total)
    acc[...] = jnp.zeros_like(acc)

    @pl.loop(0, count)
    def _(i):
        parts = []
        sums = total[...]
        for kt in range(tiles_per_block):
            probs = jnp.exp2(scores[i, :, kt * tile : (kt + 1) * tile] - peak[...])
            sums = sums + probs
            parts.append(probs.astype(jnp.bfloat16))
        total[...] = sums
        acc[...] += jnp.dot(
            jnp.concatenate(parts, axis=1),
            kv_buf[i, :, head_dim:],
            preferred_element_type=jnp.float32,
        )

    out_ref[...] = (acc[...] / jnp.sum(total[...], axis=1, keepdims=True)).astype(out_ref.dtype)


def block_scores(shift, edge, raw, invalid, table, codes_ref, half, qt, tile):
    factor = LOG2E / math.sqrt(HDIM)
    count = raw.shape[1] // tile
    columns = []
    if edge:
        lag = lax.broadcasted_iota(jnp.int32, (tile, tile), 1) - lax.broadcasted_iota(
            jnp.int32, (tile, tile), 0
        )
    for kt in range(count):
        span = slice(kt * tile, (kt + 1) * tile)
        offset = jnp.clip(shift * count + kt - qt + HALF // tile, 0, 2 * (HALF // tile))
        dropped = invalid[:, span]
        if edge:
            apart = lag + (shift * (tile * count) + (kt - qt) * tile)
            dropped = jnp.where(apart == 0, 0.0, dropped)
            dropped = jnp.where(jnp.abs(apart) <= HALF, dropped, masked_score)
        part = raw[qt * tile : (qt + 1) * tile, span]
        columns.append((part * factor + table[codes_ref[half + qt, offset]]) + dropped)
    return columns


def absorb_kernel(reach, flips, blocks, begin, pack, codes_ref, *refs):
    sets, n = len(flips), len(blocks)
    q_refs, refs = refs[:sets], refs[sets:]
    kv_refs, refs = refs[:n], refs[n:]
    table, valid_ref = refs[:2]
    refs = refs[2:]
    if not begin:
        state_refs, refs = refs[: 3 * sets], refs[3 * sets :]
    outs = 1 if pack else 3 * sets
    out_refs, refs = refs[:outs], refs[outs:]
    scores, *carried = refs
    rows, head_dim = q_refs[0].shape[0] - CODE_ROWS, q_refs[0].shape[1]
    tile = table.shape[1]
    tiles_per_block = rows // tile
    position = lax.axis_index("seq")

    for s, flip in enumerate(flips):
        owner = position ^ flip
        q_ref = q_refs[s]
        half = 0 if flip == 0 else tiles_per_block
        peak, total, acc = carried if pack else out_refs[3 * s : 3 * s + 3]
        if begin:
            peak[...] = jnp.full_like(peak, masked_score)
        else:
            peak[...] = state_refs[3 * s][...]

        def each(step):
            for j, block in enumerate(blocks):
                shift = (position ^ block) - owner
                run = functools.partial(step, j, shift, (block ^ flip) in (0, reach))
                if block ^ flip < reach:
                    run()
                else:
                    pl.when(jnp.abs(shift) <= reach)(run)

        def score(j, shift, edge, peak=peak):
            raw = lax.dot_general(
                q_ref[0:rows, :],
                kv_refs[j][:, :head_dim],
                (((1,), (1,)), ((), ())),
                preferred_element_type=jnp.float32,
            )
            invalid = jnp.where(valid_ref[owner + shift] == 1, 0.0, masked_score)
            for qt in range(tiles_per_block):
                span = slice(qt * tile, (qt + 1) * tile)
                peak_now = peak[span, :]
                columns = block_scores(
                    shift, edge, raw, invalid, table, codes_ref, half, qt, tile
                )
                for kt, column in enumerate(columns):
                    scores[j, span, kt * tile : (kt + 1) * tile] = column
                    peak_now = jnp.maximum(peak_now, column)
                peak[span, :] = peak_now

        def weigh(j, shift, edge, peak=peak, total=total, acc=acc):
            parts = []
            sums = total[...]
            for kt in range(tiles_per_block):
                probs = jnp.exp2(scores[j, :, kt * tile : (kt + 1) * tile] - peak[...])
                sums = sums + probs
                parts.append(probs.astype(jnp.bfloat16))
            total[...] = sums
            acc[...] += jnp.dot(
                jnp.concatenate(parts, axis=1),
                kv_refs[j][:, head_dim:],
                preferred_element_type=jnp.float32,
            )

        each(score)
        peak[...] = jnp.broadcast_to(jnp.max(peak[...], axis=1, keepdims=True), peak.shape)
        if begin:
            total[...] = jnp.zeros_like(total)
            acc[...] = jnp.zeros_like(acc)
        else:
            rescale = jnp.exp2(state_refs[3 * s][...] - peak[...])
            total[...] = state_refs[3 * s + 1][...] * rescale
            acc[...] = state_refs[3 * s + 2][...] * rescale
        each(weigh)

        if pack:
            out_refs[0][0:rows, :] = acc[...].astype(jnp.bfloat16)
            sums = jnp.broadcast_to(jnp.sum(total[...], axis=1, keepdims=True), total.shape)
            eye = on_diagonal(tile)
            lines = []
            for column in (peak[...], sums):
                for qt in range(tiles_per_block):
                    part = column[qt * tile : (qt + 1) * tile, :]
                    lines.append(jnp.sum(jnp.where(eye, part, 0.0), axis=0, keepdims=True))
            exact = jnp.concatenate(lines, axis=0)
            pieces = []
            for _ in range(3):
                piece = exact.astype(jnp.bfloat16).astype(jnp.float32)
                exact = exact - piece
                pieces.append(piece)
            pieces.append(jnp.zeros_like(exact))
            out_refs[0][rows:, :] = jnp.concatenate(pieces, axis=0).astype(jnp.bfloat16)


def on_diagonal(tile):
    return lax.broadcasted_iota(jnp.int32, (tile, tile), 0) == lax.broadcasted_iota(
        jnp.int32, (tile, tile), 1
    )


def absorb(reach, codes, queries, keyvals, table, valid_rows, flips, blocks, state, pack):
    rows = keyvals[0].shape[0]
    head_dim = queries[0].shape[1]
    tile = table.shape[1]
    n = len(blocks)
    vmem = pl.BlockSpec(memory_space=pltpu.VMEM)
    smem = pl.BlockSpec(memory_space=pltpu.SMEM)
    column = jax.ShapeDtypeStruct((rows, tile), jnp.float32)
    if pack:
        out_shape = [jax.ShapeDtypeStruct((rows + 8 * (rows // tile), head_dim), jnp.bfloat16)]
    else:
        out_shape = [column, column, column] * len(flips)
    units = len(flips) * n
    return pl.pallas_call(
        functools.partial(absorb_kernel, reach, flips, blocks, not state, pack),
        out_shape=out_shape,
        in_specs=[smem] + [vmem] * (len(flips) + n + 2 + len(state)),
        out_specs=[vmem] * len(out_shape),
        scratch_shapes=[
            pltpu.VMEM((n, rows, rows), jnp.float32),
        ]
        + pack * [pltpu.VMEM((rows, tile), jnp.float32)] * 3,
        compiler_params=pltpu.CompilerParams(vmem_limit_bytes=24 << 20),
        cost_estimate=pl.CostEstimate(
            flops=units * 4 * rows * rows * head_dim,
            bytes_accessed=units * 4 * rows * rows,
            transcendentals=units * rows * rows,
        ),
    )(codes, *queries, *keyvals, table, valid_rows, *state)


def merge_kernel(peak_ref, total_ref, acc_ref, pack_ref, out_ref):
    rows, _ = acc_ref.shape
    tile = peak_ref.shape[1]
    eye = on_diagonal(tile)
    count = rows // tile
    pieces = pack_ref[rows:, :].astype(jnp.float32)
    lines = 2 * count
    exact = pieces[:lines] + pieces[lines : 2 * lines] + pieces[2 * lines : 3 * lines]
    for qt in range(count):
        span = slice(qt * tile, (qt + 1) * tile)

        def column(line):
            row = exact[line : line + 1, :]
            return jnp.sum(jnp.where(eye, row, 0.0), axis=1, keepdims=True)

        peak_a = peak_ref[span, :]
        peak_b = column(qt)
        total_a = jnp.sum(total_ref[span, :], axis=1, keepdims=True)
        total_b = column(count + qt)
        top = jnp.maximum(peak_a, peak_b)
        scale_a = jnp.exp2(peak_a - top)
        scale_b = jnp.exp2(peak_b - top)
        whole = total_a * scale_a + total_b * scale_b
        out_ref[span, :] = (
            (acc_ref[span, :] * scale_a + pack_ref[span, :].astype(jnp.float32) * scale_b) / whole
        ).astype(out_ref.dtype)


def attend_split(queries, keyval, table, tile_codes, bin_valid, seq_size):
    rows = keyval.shape[0]
    reach = HALF // rows
    z = seq_size // 4
    half = z // 2
    valid_rows = bin_valid.reshape(seq_size, 1, rows)

    def trade(x, flip, some=None):
        pairs = [(i, i ^ flip) for i in range(seq_size) if some is None or some(i // z)]
        return lax.ppermute(x, "seq", pairs)

    peer_queries = trade(queries, half)
    middle = trade(keyval, 3 * z, lambda level: level in (1, 2))
    near = trade(keyval, z)
    twin = trade(keyval, 1)
    peer_codes = peer_queries[rows : rows + tile_codes.shape[0], : tile_codes.shape[1]]
    codes = jnp.concatenate([tile_codes, peer_codes.astype(jnp.int32)], axis=0)
    common = (table, valid_rows)
    state = absorb(
        reach, codes, [queries, peer_queries], [keyval, twin], *common, (0, half), (0, 1), [], False
    )
    near, middle, state = lax.optimization_barrier((near, middle, state))
    level = lax.axis_index("seq") // z
    onward = jnp.where((level == 1) | (level == 2), middle, keyval)
    leap = (2 * z, -z, z, -2 * z)
    far = lax.ppermute(onward, "seq", [(i, i + leap[i // z]) for i in range(seq_size)])
    near_twin = trade(near, 1)
    middle_twin = trade(middle, 1)
    state = absorb(
        reach,
        codes,
        [queries, peer_queries],
        [near, middle],
        *common,
        (0, half),
        (z, 3 * z),
        state,
        False,
    )
    mine = state[:3]
    state = absorb(
        reach,
        codes,
        [peer_queries],
        [near_twin, middle_twin],
        *common,
        (half,),
        (z + 1, 3 * z + 1),
        state[3:],
        False,
    )
    far, state = lax.optimization_barrier((far, state))
    far_twin = trade(far, 1)
    away = [far, far_twin]
    leaps = (2 * z, 2 * z + 1)
    theirs = absorb(
        reach, codes, [peer_queries], away[:1], *common, (half,), leaps[:1], state, False
    )
    (pack,) = absorb(
        reach, codes, [peer_queries], away[1:], *common, (half,), leaps[1:], theirs, True
    )
    other = trade(pack, half)
    peak, total, acc = absorb(
        reach,
        codes,
        [queries],
        [near_twin, middle_twin, *away],
        *common,
        (0,),
        (z + 1, 3 * z + 1, *leaps),
        mine,
        False,
    )
    vmem = pl.BlockSpec(memory_space=pltpu.VMEM)
    return pl.pallas_call(
        merge_kernel,
        out_shape=jax.ShapeDtypeStruct((rows, queries.shape[1]), jnp.bfloat16),
        in_specs=[vmem] * 4,
        out_specs=vmem,
        compiler_params=pltpu.CompilerParams(vmem_limit_bytes=8 << 20),
        name="merge",
    )(peak, total, acc, other)


def attend(queries, everything, contact_tiles, tile_codes, bin_valid, position, seq_size):
    rows, head_dim = queries.shape
    reach = HALF // rows
    tile = contact_tiles.shape[1]
    slots = min(seq_size, 2 * reach + 1)
    first = jnp.maximum(position - reach, 0)
    last = jnp.minimum(position + reach, seq_size - 1)
    place = jnp.stack([position, first, last - first + 1]).astype(jnp.int32)
    valid_rows = bin_valid.reshape(seq_size, 1, rows)
    vmem = pl.BlockSpec(memory_space=pltpu.VMEM)
    smem = pl.BlockSpec(memory_space=pltpu.SMEM)
    return pl.pallas_call(
        functools.partial(attend_kernel, reach),
        out_shape=jax.ShapeDtypeStruct((rows, head_dim), jnp.bfloat16),
        in_specs=[smem, smem, vmem, pl.BlockSpec(memory_space=pl.ANY), vmem, vmem],
        out_specs=vmem,
        scratch_shapes=[
            pltpu.VMEM((slots, rows, 2 * head_dim), jnp.bfloat16),
            pltpu.VMEM(contact_tiles.shape, jnp.float32),
            pltpu.VMEM((slots, rows, rows), jnp.float32),
            pltpu.VMEM((rows, tile), jnp.float32),
            pltpu.VMEM((rows, tile), jnp.float32),
            pltpu.VMEM((rows, head_dim), jnp.float32),
            pltpu.SemaphoreType.DMA((slots,)),
        ],
        compiler_params=pltpu.CompilerParams(vmem_limit_bytes=60 << 20),
        name="attend",
    )(tile_codes, place, queries, everything, contact_tiles, valid_rows)


def per_device(
    activations,
    dilated_tap_weight,
    conv_mix,
    w_query,
    w_keyval,
    contact_tiles,
    tile_codes,
    bin_valid,
):
    seq_size = lax.axis_size("seq")
    position = lax.axis_index("seq")
    halo = halo_rows(activations)
    *lifted, table = lift(
        activations, dilated_tap_weight, conv_mix, w_query, w_keyval, contact_tiles
    )
    queries, keyval = front(lifted, halo, tile_codes)
    if seq_size == 16 and seq_size * activations.shape[0] == 2 * HALF:
        return attend_split(queries, keyval, table, tile_codes, bin_valid, seq_size)
    queries = queries[: activations.shape[0]]
    everything = lax.all_gather(keyval, "seq", axis=0, tiled=True)
    return attend(queries, everything, contact_tiles, tile_codes, bin_valid, position, seq_size)


def solution(mesh):
    in_specs = (P(("grp", "seq"), None), P(), P(), P(), P(), P(), P(("grp", "seq"), None), P("grp"))
    out_specs = P(("grp", "seq"), None)
    return jax.shard_map(
        per_device, mesh=mesh, in_specs=in_specs, out_specs=out_specs, check_vma=False
    )
```

```python
import functools
import math

import jax
import jax.numpy as jnp
from jax import lax
from jax.experimental import pallas as pl
from jax.experimental.pallas import tpu as pltpu
from jax.sharding import PartitionSpec as P


HDIM = 128
CONV_DILATION = 8
HALF = 4096


masked_score = -1e30
norm_eps = 1e-06
LOG2E = 1.4426950408889634


def halo_rows(activations):
    size = lax.axis_size("seq")
    odd = lax.axis_index("seq") % 2 == 1
    rows = activations.shape[0]
    initial = lax.slice_in_dim(activations, 0, CONV_DILATION, axis=0)
    last = lax.slice_in_dim(activations, rows - CONV_DILATION, rows, axis=0)
    inner = [(i, i ^ 1) for i in range(size)]
    outer = [(i, i + 1) for i in range(1, size - 1, 2)] + [(i + 1, i) for i in range(1, size - 1, 2)]
    from_inner = lax.ppermute(jnp.where(odd, initial, last), "seq", inner)
    from_outer = lax.ppermute(jnp.where(odd, last, initial), "seq", outer)
    return from_inner, from_outer


def gelu(v):
    return 0.5 * v * (1.0 + lax.erf(v * math.sqrt(0.5)))


def lift_kernel(x_hbm, taps_hbm, mix_hbm, wq_hbm, wkv_hbm, tiles_hbm, *refs):
    x_ref, taps, mix, wq, wkv, inner, outer, table, tiles, sems = refs
    copies = [
        pltpu.make_async_copy(source, target, sems.at[i])
        for i, (source, target) in enumerate(
            [
                (x_hbm, x_ref),
                (tiles_hbm, tiles),
                (taps_hbm, taps),
                (mix_hbm, mix),
                (wq_hbm, wq),
                (wkv_hbm, wkv),
            ]
        )
    ]
    for copy in copies:
        copy.start()
    rows, channels = x_ref.shape
    step = 32
    d = CONV_DILATION
    copies[0].wait()

    def lift(i, tail):
        r = pl.multiple_of(i * step, step)
        g = gelu(x_ref[pl.ds(r, step), :].astype(jnp.float32))
        inner[pl.ds(r, step), :] = g.astype(jnp.bfloat16)
        outer[pl.ds(r, step), :] = jnp.concatenate([tail, g[: step - d]], axis=0).astype(
            jnp.bfloat16
        )
        return g[step - d :]

    edge = jnp.zeros((d, channels), jnp.float32)
    tail = lax.fori_loop(0, rows // step, lift, edge)
    outer[rows : rows + 2 * d, :] = jnp.concatenate([tail, edge], axis=0).astype(jnp.bfloat16)
    copies[1].wait()
    table[...] = tiles[...].astype(jnp.float32) * LOG2E
    for copy in copies[2:]:
        copy.wait()


def lift(activations, dilated_tap_weight, conv_mix, w_query, w_keyval, contact_tiles):
    rows, channels = activations.shape
    moved = [
        pltpu.with_memory_space_constraint(a, pltpu.HBM)
        for a in (activations, dilated_tap_weight, conv_mix, w_query, w_keyval)
    ]
    contact_tiles = pltpu.with_memory_space_constraint(contact_tiles, pltpu.HBM)
    vmem = pl.BlockSpec(memory_space=pltpu.VMEM)
    return pl.pallas_call(
        lift_kernel,
        out_shape=[jax.ShapeDtypeStruct(a.shape, a.dtype) for a in moved]
        + [
            jax.ShapeDtypeStruct((rows, channels), jnp.bfloat16),
            jax.ShapeDtypeStruct((rows + 2 * CONV_DILATION, channels), jnp.bfloat16),
            jax.ShapeDtypeStruct(contact_tiles.shape, jnp.float32),
        ],
        in_specs=[pl.BlockSpec(memory_space=pltpu.HBM)] * 6,
        out_specs=[vmem] * 8,
        scratch_shapes=[
            pltpu.VMEM(contact_tiles.shape, contact_tiles.dtype),
            pltpu.SemaphoreType.DMA((6,)),
        ],
        compiler_params=pltpu.CompilerParams(vmem_limit_bytes=24 << 20),
        name="lift",
    )(*moved, contact_tiles)


def front_kernel(
    x_ref,
    taps,
    mix,
    wq,
    wkv,
    inner,
    outer_ref,
    twin_ref,
    outside_ref,
    codes_ref,
    q_ref,
    kv_ref,
    outer,
    squeezed,
    mixed,
):
    rows, channels = x_ref.shape
    hidden = squeezed.shape[1]
    d = CONV_DILATION
    odd = lax.axis_index("seq") % 2 == 1
    beside = gelu(twin_ref[...].astype(jnp.float32))
    beyond = gelu(outside_ref[...].astype(jnp.float32))
    before = jnp.where(odd, beside, beyond)
    after = jnp.where(odd, beyond, beside)
    outer[...] = outer_ref[...]
    initial = outer_ref[0 : 2 * d, :].astype(jnp.float32)[d:]
    last = outer_ref[rows : rows + 2 * d, :].astype(jnp.float32)[:d]
    outer[0 : 2 * d, :] = jnp.concatenate([before, initial], axis=0).astype(jnp.bfloat16)
    outer[rows : rows + 2 * d, :] = jnp.concatenate([last, after], axis=0).astype(jnp.bfloat16)

    wide = 256
    taps_rows, mix_rows, out_rows = rows // 2, rows // 1, rows // 1
    for n in range(hidden // wide):
        cols = slice(n * wide, (n + 1) * wide)
        for r in range(0, rows, taps_rows):
            conv = jnp.dot(
                outer[r : r + taps_rows, :], taps[0, :, cols], preferred_element_type=jnp.float32
            )
            conv += jnp.dot(
                inner[r : r + taps_rows, :], taps[1, :, cols], preferred_element_type=jnp.float32
            )
            conv += jnp.dot(
                outer[r + 2 * d : r + 2 * d + taps_rows, :],
                taps[2, :, cols],
                preferred_element_type=jnp.float32,
            )
            squeezed[r : r + taps_rows, cols] = gelu(conv).astype(jnp.bfloat16)

    squares = [jnp.zeros((mix_rows, 128), jnp.float32) for _ in range(rows // mix_rows)]
    for n in range(channels // wide):
        cols = slice(n * wide, (n + 1) * wide)
        for i in range(rows // mix_rows):
            span = slice(i * mix_rows, (i + 1) * mix_rows)
            part = x_ref[span, cols].astype(jnp.float32) + jnp.dot(
                squeezed[span, :], mix[:, cols], preferred_element_type=jnp.float32
            )
            mixed[span, cols] = part
            for k in range(wide // 128):
                piece = part[:, k * 128 : (k + 1) * 128]
                squares[i] += piece * piece
    gain = lax.rsqrt(
        jnp.sum(jnp.concatenate(squares, axis=0), axis=1, keepdims=True) / channels + norm_eps
    )
    for r in range(0, rows, out_rows):
        span = slice(r, r + out_rows)
        normed = (mixed[span, :] * gain[span]).astype(jnp.bfloat16)
        q_ref[span, :] = jnp.dot(normed, wq[...], preferred_element_type=jnp.float32).astype(
            jnp.bfloat16
        )
        kv_ref[span, :] = jnp.dot(normed, wkv[...], preferred_element_type=jnp.float32).astype(
            jnp.bfloat16
        )
    q_ref[rows:, :] = jnp.zeros((q_ref.shape[0] - rows, q_ref.shape[1]), jnp.bfloat16)
    q_ref[rows : rows + codes_ref.shape[0], 0 : codes_ref.shape[1]] = (
        codes_ref[...].astype(jnp.float32).astype(jnp.bfloat16)
    )


CODE_ROWS = 16


def front(lifted, halo, tile_codes):
    activations, _, conv_mix, w_query, w_keyval, _, outer = lifted
    rows, channels = activations.shape
    vmem = pl.BlockSpec(memory_space=pltpu.VMEM)
    bf16 = jnp.bfloat16
    return pl.pallas_call(
        front_kernel,
        out_shape=[
            jax.ShapeDtypeStruct((rows + CODE_ROWS, w_query.shape[1]), bf16),
            jax.ShapeDtypeStruct((rows, w_keyval.shape[1]), bf16),
        ],
        in_specs=[vmem] * 10,
        out_specs=[vmem, vmem],
        scratch_shapes=[
            pltpu.VMEM(outer.shape, bf16),
            pltpu.VMEM((rows, conv_mix.shape[0]), bf16),
            pltpu.VMEM((rows, channels), jnp.float32),
        ],
        compiler_params=pltpu.CompilerParams(vmem_limit_bytes=24 << 20),
        name="front",
    )(*lifted, *halo, tile_codes)


def attend_kernel(
    reach,
    codes_ref,
    place_ref,
    q_ref,
    kv_ref,
    tiles_ref,
    valid_ref,
    out_ref,
    kv_buf,
    bias_buf,
    scores,
    peak,
    total,
    acc,
    sems,
):
    rows, head_dim = q_ref.shape
    _, tile, _ = tiles_ref.shape
    tiles_per_block = rows // tile
    position = place_ref[0]
    first = place_ref[1]
    count = place_ref[2]
    factor = LOG2E / math.sqrt(head_dim)

    def fetch(i):
        return pltpu.make_async_copy(
            kv_ref.at[pl.ds((first + i) * rows, rows), :], kv_buf.at[i], sems.at[i]
        )

    @pl.loop(0, count)
    def _(i):
        fetch(i).start()

    bias_buf[...] = tiles_ref[...].astype(jnp.float32) * LOG2E
    peak[...] = jnp.full_like(peak, masked_score)

    @pl.loop(0, count)
    def _(i):
        fetch(i).wait()
        block = first + i
        keys = kv_buf[i, :, :head_dim]
        raw = lax.dot_general(
            q_ref[...], keys, (((1,), (1,)), ((), ())), preferred_element_type=jnp.float32
        )
        invalid = jnp.where(valid_ref[block] == 1, 0.0, masked_score)
        shift = block - position

        def tile_scores(qt, kt):
            offset = jnp.clip(shift * tiles_per_block + kt - qt + HALF // tile, 0, 2 * (HALF // tile))
            part = raw[qt * tile : (qt + 1) * tile, kt * tile : (kt + 1) * tile]
            return part * factor + bias_buf[codes_ref[qt, offset]]

        def keep(qt, columns):
            peak_now = peak[qt * tile : (qt + 1) * tile, :]
            for kt, column in enumerate(columns):
                scores[i, qt * tile : (qt + 1) * tile, kt * tile : (kt + 1) * tile] = column
                peak_now = jnp.maximum(peak_now, column)
            peak[qt * tile : (qt + 1) * tile, :] = peak_now

        plain = (shift != 0) & (jnp.abs(shift) < reach)

        @pl.when(plain)
        def _():
            for qt in range(tiles_per_block):
                keep(
                    qt,
                    [
                        tile_scores(qt, kt) + invalid[:, kt * tile : (kt + 1) * tile]
                        for kt in range(tiles_per_block)
                    ],
                )

        @pl.when(jnp.logical_not(plain))
        def _():
            lag = lax.broadcasted_iota(jnp.int32, (tile, tile), 1) - lax.broadcasted_iota(
                jnp.int32, (tile, tile), 0
            )
            for qt in range(tiles_per_block):
                columns = []
                for kt in range(tiles_per_block):
                    apart = lag + (shift * rows + (kt - qt) * tile)
                    dropped = jnp.where(
                        apart == 0, 0.0, invalid[:, kt * tile : (kt + 1) * tile]
                    )
                    dropped = jnp.where(jnp.abs(apart) <= HALF, dropped, masked_score)
                    columns.append(tile_scores(qt, kt) + dropped)
                keep(qt, columns)

    peak[...] = jnp.broadcast_to(jnp.max(peak[...], axis=1, keepdims=True), peak.shape)
    total[...] = jnp.zeros_like(total)
    acc[...] = jnp.zeros_like(acc)

    @pl.loop(0, count)
    def _(i):
        parts = []
        sums = total[...]
        for kt in range(tiles_per_block):
            probs = jnp.exp2(scores[i, :, kt * tile : (kt + 1) * tile] - peak[...])
            sums = sums + probs
            parts.append(probs.astype(jnp.bfloat16))
        total[...] = sums
        acc[...] += jnp.dot(
            jnp.concatenate(parts, axis=1),
            kv_buf[i, :, head_dim:],
            preferred_element_type=jnp.float32,
        )

    out_ref[...] = (acc[...] / jnp.sum(total[...], axis=1, keepdims=True)).astype(out_ref.dtype)


def block_scores(shift, edge, raw, invalid, table, codes_ref, half, qt, tile):
    factor = LOG2E / math.sqrt(HDIM)
    count = raw.shape[1] // tile
    columns = []
    if edge:
        lag = lax.broadcasted_iota(jnp.int32, (tile, tile), 1) - lax.broadcasted_iota(
            jnp.int32, (tile, tile), 0
        )
    for kt in range(count):
        span = slice(kt * tile, (kt + 1) * tile)
        offset = jnp.clip(shift * count + kt - qt + HALF // tile, 0, 2 * (HALF // tile))
        dropped = invalid[:, span]
        if edge:
            apart = lag + (shift * (tile * count) + (kt - qt) * tile)
            dropped = jnp.where(apart == 0, 0.0, dropped)
            dropped = jnp.where(jnp.abs(apart) <= HALF, dropped, masked_score)
        part = raw[qt * tile : (qt + 1) * tile, span]
        columns.append((part * factor + table[codes_ref[half + qt, offset]]) + dropped)
    return columns


def absorb_kernel(reach, flips, blocks, begin, pack, codes_ref, *refs):
    sets, n = len(flips), len(blocks)
    q_refs, refs = refs[:sets], refs[sets:]
    kv_refs, refs = refs[:n], refs[n:]
    table, valid_ref = refs[:2]
    refs = refs[2:]
    if not begin:
        state_refs, refs = refs[: 3 * sets], refs[3 * sets :]
    outs = 1 if pack else 3 * sets
    out_refs, refs = refs[:outs], refs[outs:]
    scores, *carried = refs
    rows, head_dim = q_refs[0].shape[0] - CODE_ROWS, q_refs[0].shape[1]
    tile = table.shape[1]
    tiles_per_block = rows // tile
    position = lax.axis_index("seq")

    for s, flip in enumerate(flips):
        owner = position ^ flip
        q_ref = q_refs[s]
        half = 0 if flip == 0 else tiles_per_block
        peak, total, acc = carried if pack else out_refs[3 * s : 3 * s + 3]
        if begin:
            peak[...] = jnp.full_like(peak, masked_score)
        else:
            peak[...] = state_refs[3 * s][...]

        def each(step):
            for j, block in enumerate(blocks):
                shift = (position ^ block) - owner
                run = functools.partial(step, j, shift, (block ^ flip) in (0, reach))
                if block ^ flip < reach:
                    run()
                else:
                    pl.when(jnp.abs(shift) <= reach)(run)

        def score(j, shift, edge, peak=peak):
            raw = lax.dot_general(
                q_ref[0:rows, :],
                kv_refs[j][:, :head_dim],
                (((1,), (1,)), ((), ())),
                preferred_element_type=jnp.float32,
            )
            invalid = jnp.where(valid_ref[owner + shift] == 1, 0.0, masked_score)
            for qt in range(tiles_per_block):
                span = slice(qt * tile, (qt + 1) * tile)
                peak_now = peak[span, :]
                columns = block_scores(
                    shift, edge, raw, invalid, table, codes_ref, half, qt, tile
                )
                for kt, column in enumerate(columns):
                    scores[j, span, kt * tile : (kt + 1) * tile] = column
                    peak_now = jnp.maximum(peak_now, column)
                peak[span, :] = peak_now

        def weigh(j, shift, edge, peak=peak, total=total, acc=acc):
            parts = []
            sums = total[...]
            for kt in range(tiles_per_block):
                probs = jnp.exp2(scores[j, :, kt * tile : (kt + 1) * tile] - peak[...])
                sums = sums + probs
                parts.append(probs.astype(jnp.bfloat16))
            total[...] = sums
            acc[...] += jnp.dot(
                jnp.concatenate(parts, axis=1),
                kv_refs[j][:, head_dim:],
                preferred_element_type=jnp.float32,
            )

        each(score)
        peak[...] = jnp.broadcast_to(jnp.max(peak[...], axis=1, keepdims=True), peak.shape)
        if begin:
            total[...] = jnp.zeros_like(total)
            acc[...] = jnp.zeros_like(acc)
        else:
            rescale = jnp.exp2(state_refs[3 * s][...] - peak[...])
            total[...] = state_refs[3 * s + 1][...] * rescale
            acc[...] = state_refs[3 * s + 2][...] * rescale
        each(weigh)

        if pack:
            out_refs[0][0:rows, :] = acc[...].astype(jnp.bfloat16)
            sums = jnp.broadcast_to(jnp.sum(total[...], axis=1, keepdims=True), total.shape)
            eye = on_diagonal(tile)
            lines = []
            for column in (peak[...], sums):
                for qt in range(tiles_per_block):
                    part = column[qt * tile : (qt + 1) * tile, :]
                    lines.append(jnp.sum(jnp.where(eye, part, 0.0), axis=0, keepdims=True))
            exact = jnp.concatenate(lines, axis=0)
            pieces = []
            for _ in range(3):
                piece = exact.astype(jnp.bfloat16).astype(jnp.float32)
                exact = exact - piece
                pieces.append(piece)
            pieces.append(jnp.zeros_like(exact))
            out_refs[0][rows:, :] = jnp.concatenate(pieces, axis=0).astype(jnp.bfloat16)


def on_diagonal(tile):
    return lax.broadcasted_iota(jnp.int32, (tile, tile), 0) == lax.broadcasted_iota(
        jnp.int32, (tile, tile), 1
    )


def absorb(reach, codes, queries, keyvals, table, valid_rows, flips, blocks, state, pack):
    rows = keyvals[0].shape[0]
    head_dim = queries[0].shape[1]
    tile = table.shape[1]
    n = len(blocks)
    vmem = pl.BlockSpec(memory_space=pltpu.VMEM)
    smem = pl.BlockSpec(memory_space=pltpu.SMEM)
    column = jax.ShapeDtypeStruct((rows, tile), jnp.float32)
    if pack:
        out_shape = [jax.ShapeDtypeStruct((rows + 8 * (rows // tile), head_dim), jnp.bfloat16)]
    else:
        out_shape = [column, column, column] * len(flips)
    units = len(flips) * n
    return pl.pallas_call(
        functools.partial(absorb_kernel, reach, flips, blocks, not state, pack),
        out_shape=out_shape,
        in_specs=[smem] + [vmem] * (len(flips) + n + 2 + len(state)),
        out_specs=[vmem] * len(out_shape),
        scratch_shapes=[
            pltpu.VMEM((n, rows, rows), jnp.float32),
        ]
        + pack * [pltpu.VMEM((rows, tile), jnp.float32)] * 3,
        compiler_params=pltpu.CompilerParams(vmem_limit_bytes=24 << 20),
        cost_estimate=pl.CostEstimate(
            flops=units * 4 * rows * rows * head_dim,
            bytes_accessed=units * 4 * rows * rows,
            transcendentals=units * rows * rows,
        ),
    )(codes, *queries, *keyvals, table, valid_rows, *state)


def merge_kernel(peak_ref, total_ref, acc_ref, pack_ref, out_ref):
    rows, _ = acc_ref.shape
    tile = peak_ref.shape[1]
    eye = on_diagonal(tile)
    count = rows // tile
    pieces = pack_ref[rows:, :].astype(jnp.float32)
    lines = 2 * count
    exact = pieces[:lines] + pieces[lines : 2 * lines] + pieces[2 * lines : 3 * lines]
    for qt in range(count):
        span = slice(qt * tile, (qt + 1) * tile)

        def column(line):
            row = exact[line : line + 1, :]
            return jnp.sum(jnp.where(eye, row, 0.0), axis=1, keepdims=True)

        peak_a = peak_ref[span, :]
        peak_b = column(qt)
        total_a = jnp.sum(total_ref[span, :], axis=1, keepdims=True)
        total_b = column(count + qt)
        top = jnp.maximum(peak_a, peak_b)
        scale_a = jnp.exp2(peak_a - top)
        scale_b = jnp.exp2(peak_b - top)
        whole = total_a * scale_a + total_b * scale_b
        out_ref[span, :] = (
            (acc_ref[span, :] * scale_a + pack_ref[span, :].astype(jnp.float32) * scale_b) / whole
        ).astype(out_ref.dtype)


def attend_split(queries, keyval, table, tile_codes, bin_valid, seq_size):
    rows = keyval.shape[0]
    reach = HALF // rows
    z = seq_size // 4
    half = z // 2
    valid_rows = bin_valid.reshape(seq_size, 1, rows)

    def trade(x, flip, some=None):
        pairs = [(i, i ^ flip) for i in range(seq_size) if some is None or some(i // z)]
        return lax.ppermute(x, "seq", pairs)

    peer_queries = trade(queries, half)
    middle = trade(keyval, 3 * z, lambda level: level in (1, 2))
    near = trade(keyval, z)
    twin = trade(keyval, 1)
    common = (table, valid_rows)
    mine = absorb(reach, tile_codes, [queries], [keyval, twin], *common, (0,), (0, 1), [], False)
    middle, mine = lax.optimization_barrier((middle, mine))
    level = lax.axis_index("seq") // z
    onward = jnp.where((level == 1) | (level == 2), middle, keyval)
    leap = (2 * z, -z, z, -2 * z)
    far = lax.ppermute(onward, "seq", [(i, i + leap[i // z]) for i in range(seq_size)])
    near_twin = trade(near, 1)
    middle_twin = trade(middle, 1)
    peer_codes = peer_queries[rows : rows + tile_codes.shape[0], : tile_codes.shape[1]]
    codes = jnp.concatenate([tile_codes, peer_codes.astype(jnp.int32)], axis=0)
    state = absorb(
        reach,
        codes,
        [peer_queries],
        [keyval, twin, near, middle],
        *common,
        (half,),
        (0, 1, z, 3 * z),
        [],
        False,
    )
    state = absorb(
        reach,
        codes,
        [peer_queries],
        [near_twin, middle_twin],
        *common,
        (half,),
        (z + 1, 3 * z + 1),
        state,
        False,
    )
    far, state = lax.optimization_barrier((far, state))
    far_twin = trade(far, 1)
    away = [far, far_twin]
    leaps = (2 * z, 2 * z + 1)
    theirs = absorb(
        reach, codes, [peer_queries], away[:1], *common, (half,), leaps[:1], state, False
    )
    (pack,) = absorb(
        reach, codes, [peer_queries], away[1:], *common, (half,), leaps[1:], theirs, True
    )
    other = trade(pack, half)
    peak, total, acc = absorb(
        reach,
        codes,
        [queries],
        [near, middle, near_twin, middle_twin, *away],
        *common,
        (0,),
        (z, 3 * z, z + 1, 3 * z + 1, *leaps),
        mine,
        False,
    )
    vmem = pl.BlockSpec(memory_space=pltpu.VMEM)
    return pl.pallas_call(
        merge_kernel,
        out_shape=jax.ShapeDtypeStruct((rows, queries.shape[1]), jnp.bfloat16),
        in_specs=[vmem] * 4,
        out_specs=vmem,
        compiler_params=pltpu.CompilerParams(vmem_limit_bytes=8 << 20),
        name="merge",
    )(peak, total, acc, other)


def attend(queries, everything, contact_tiles, tile_codes, bin_valid, position, seq_size):
    rows, head_dim = queries.shape
    reach = HALF // rows
    tile = contact_tiles.shape[1]
    slots = min(seq_size, 2 * reach + 1)
    first = jnp.maximum(position - reach, 0)
    last = jnp.minimum(position + reach, seq_size - 1)
    place = jnp.stack([position, first, last - first + 1]).astype(jnp.int32)
    valid_rows = bin_valid.reshape(seq_size, 1, rows)
    vmem = pl.BlockSpec(memory_space=pltpu.VMEM)
    smem = pl.BlockSpec(memory_space=pltpu.SMEM)
    return pl.pallas_call(
        functools.partial(attend_kernel, reach),
        out_shape=jax.ShapeDtypeStruct((rows, head_dim), jnp.bfloat16),
        in_specs=[smem, smem, vmem, pl.BlockSpec(memory_space=pl.ANY), vmem, vmem],
        out_specs=vmem,
        scratch_shapes=[
            pltpu.VMEM((slots, rows, 2 * head_dim), jnp.bfloat16),
            pltpu.VMEM(contact_tiles.shape, jnp.float32),
            pltpu.VMEM((slots, rows, rows), jnp.float32),
            pltpu.VMEM((rows, tile), jnp.float32),
            pltpu.VMEM((rows, tile), jnp.float32),
            pltpu.VMEM((rows, head_dim), jnp.float32),
            pltpu.SemaphoreType.DMA((slots,)),
        ],
        compiler_params=pltpu.CompilerParams(vmem_limit_bytes=60 << 20),
        name="attend",
    )(tile_codes, place, queries, everything, contact_tiles, valid_rows)


def per_device(
    activations,
    dilated_tap_weight,
    conv_mix,
    w_query,
    w_keyval,
    contact_tiles,
    tile_codes,
    bin_valid,
):
    seq_size = lax.axis_size("seq")
    position = lax.axis_index("seq")
    halo = halo_rows(activations)
    *lifted, table = lift(
        activations, dilated_tap_weight, conv_mix, w_query, w_keyval, contact_tiles
    )
    queries, keyval = front(lifted, halo, tile_codes)
    if seq_size == 16 and seq_size * activations.shape[0] == 2 * HALF:
        return attend_split(queries, keyval, table, tile_codes, bin_valid, seq_size)
    queries = queries[: activations.shape[0]]
    everything = lax.all_gather(keyval, "seq", axis=0, tiled=True)
    return attend(queries, everything, contact_tiles, tile_codes, bin_valid, position, seq_size)


def solution(mesh):
    in_specs = (P(("grp", "seq"), None), P(), P(), P(), P(), P(), P(("grp", "seq"), None), P("grp"))
    out_specs = P(("grp", "seq"), None)
    return jax.shard_map(
        per_device, mesh=mesh, in_specs=in_specs, out_specs=out_specs, check_vma=False
    )
```
